32 devices in a mesh: rep: 8 (over z, core), shard: 4 (over y, x).
Axes of the slice: x: 2, y: 2, z: 4, core: 2. Of those that a mesh axis runs over, the one named last changes fastest.
Arguments:
- tokens: bfloat16 [4096, 1536], P(('rep', 'shard')), may hold values from -6 to 6
- cotangent: bfloat16 [4096, 1536], P(('rep', 'shard')), may hold values from -6 to 6
- lengths: int32 [8], P('rep'), may hold values from 128 to 512, as said below
- gain_one: bfloat16 [1536], P('shard'), may hold values from 0.5 to 1.5
- w_query: bfloat16 [1536, 1536], P('shard'), may hold values from -0.15625 to 0.15625
- w_key: bfloat16 [1536, 1536], P('shard'), may hold values from -0.15625 to 0.15625
- w_value: bfloat16 [1536, 1536], P('shard'), may hold values from -0.15625 to 0.15625
- w_path: bfloat16 [1536, 1536], P('shard'), may hold values from -0.15625 to 0.15625
- w_beta: bfloat16 [1536, 12], P('shard'), may hold values from -0.15625 to 0.15625
- w_out: bfloat16 [1536, 1536], P('shard'), may hold values from -0.625 to 0.625
- gain_two: bfloat16 [1536], P('shard'), may hold values from 0.5 to 1.5
- w_gate: bfloat16 [1536, 4096], P('shard'), may hold values from -0.15625 to 0.15625
- w_up: bfloat16 [1536, 4096], P('shard'), may hold values from -0.15625 to 0.15625
- w_down: bfloat16 [4096, 1536], P('shard'), may hold values from -0.09375 to 0.09375
Outputs:
- output: bfloat16 [4096, 1536], P(('rep', 'shard'))
- input_grad: bfloat16 [4096, 1536], P(('rep', 'shard'))
- grad_gain_one: float32 [1536], P('shard')
- grad_w_query: float32 [1536, 1536], P('shard')
- grad_w_key: float32 [1536, 1536], P('shard')
- grad_w_value: float32 [1536, 1536], P('shard')
- grad_w_path: float32 [1536, 1536], P('shard')
- grad_w_beta: float32 [1536, 12], P('shard')
- grad_w_out: float32 [1536, 1536], P('shard')
- grad_gain_two: float32 [1536], P('shard')
- grad_w_gate: float32 [1536, 4096], P('shard')
- grad_w_up: float32 [1536, 4096], P('shard')
- grad_w_down: float32 [4096, 1536], P('shard')
- rms_input: float32 [], replicated
- rms_attn: float32 [], replicated
- rms_feed: float32 [], replicated
The draws below stay inside these ranges and needn't reach their ends.
Inputs may be any that keep to these rules, and one draw needn't show every extreme that they name: Sequence r fills the first lengths[r] of its 512 slots; at least one sequence fills all of them.
All inputs are finite; a program needn't handle non-finite values.
Results may differ from the reference program's by a relative error of at most 0.02.
Values may be sent and summed in bfloat16 or wider, within the bound.
No kernel may reach another device: no remote copies, remote signals or barrier semaphores. Data moves between devices by JAX's collectives and lax.ppermute only.
A program may use at most 320 MiB of HBM per device.

```python
import jax
import jax.numpy as jnp
from jax import lax

D = 1536
H = 12
DH = 128
FF = 4096
SEQ = 512
GROUPS = 8
TOKENS = 4096


def draw_lengths(key, part):
    length_key = jax.random.fold_in(key, 11)
    choose_key = jax.random.fold_in(key, 23)
    lengths_drawn = jax.random.randint(length_key, (GROUPS,), SEQ // 4, SEQ + 1)
    chosen = jax.random.randint(choose_key, (), 0, GROUPS)
    return jnp.where(jnp.arange(GROUPS) == chosen, SEQ, lengths_drawn).astype(jnp.int32)


def shard_levels(own_key, extent, shards, smallest, top_value):
    loudness = 1.0
    for dim, parts in shards:
        draws = jax.random.uniform(jax.random.fold_in(jax.random.fold_in(own_key, 6), dim), (parts,), jnp.float32, smallest / len(shards), top_value / len(shards))
        loudness = loudness * jnp.repeat(jnp.exp(draws), extent[dim] // parts).reshape((-1,) + (1,) * (len(extent) - 1 - dim))
    return loudness


def normal_values(own_key, shape, spread, most, shards=(), kind=jnp.bfloat16):
    loudness = shard_levels(own_key, shape, shards, -0.22, 0.18) if shards else 1.0
    drawn = jax.random.normal(own_key, shape, jnp.float32) * spread * loudness
    return jnp.minimum(jnp.maximum(drawn, -most), most).astype(kind)


def setup_inputs(seed: int = 0) -> dict:
    arg_keys = jax.random.split(jax.random.key(seed), 15)
    return {
        "tokens": normal_values(arg_keys[0], (TOKENS, D), 1.0, 6.0, ((0, 32),)),
        "cotangent": normal_values(arg_keys[1], (TOKENS, D), 1.0, 6.0, ((0, 32),)),
        "lengths": draw_lengths(jax.random.fold_in(arg_keys[14], 71), 0),
        "gain_one": jnp.clip(1.0 + 0.1 * jax.random.normal(arg_keys[3], (D,), jnp.float32), 0.5, 1.5).astype(jnp.bfloat16),
        "w_query": normal_values(arg_keys[4], (D, D), D ** -0.5, 0.15625, ((0, 4),)),
        "w_key": normal_values(arg_keys[5], (D, D), D ** -0.5, 0.15625, ((0, 4),)),
        "w_value": normal_values(arg_keys[6], (D, D), D ** -0.5, 0.15625, ((0, 4),)),
        "w_path": normal_values(arg_keys[7], (D, D), D ** -0.5, 0.15625, ((0, 4),)),
        "w_beta": normal_values(arg_keys[8], (D, H), D ** -0.5, 0.15625, ((0, 4),)),
        "w_out": normal_values(arg_keys[9], (D, D), (D // 16) ** -0.5, 0.625, ((0, 4),)),
        "gain_two": jnp.clip(1.0 + 0.1 * jax.random.normal(arg_keys[10], (D,), jnp.float32), 0.5, 1.5).astype(jnp.bfloat16),
        "w_gate": normal_values(arg_keys[11], (D, FF), D ** -0.5, 0.15625, ((0, 4),)),
        "w_up": normal_values(arg_keys[12], (D, FF), D ** -0.5, 0.15625, ((0, 4),)),
        "w_down": normal_values(arg_keys[13], (FF, D), FF ** -0.5, 0.09375, ((0, 4),)),
    }


@jax.custom_vjp
def low(v):
    return lax.optimization_barrier(v.astype(jnp.bfloat16)).astype(jnp.float32)

@jax.custom_vjp
def low_back(v):
    return v

def low_keep(v):
    return (low(v), None)

def low_pass(kept, grad):
    return (grad,)

def back_keep(v):
    return (v, None)

def back_low(kept, grad):
    return (low(grad),)
low.defvjp(low_keep, low_pass)
low_back.defvjp(back_keep, back_low)
eps = 1e-06
highest = lax.Precision.HIGHEST

def matmul_hi(left, right):
    return jnp.dot(left, right, precision=highest)

def rms_norm(value, gain_vec):
    factor = lax.rsqrt(lax.optimization_barrier(jnp.mean(value * value, axis=-1, keepdims=True)) + eps)
    return value * factor * gain_vec

def unit_rows(raw):
    return raw * lax.rsqrt(lax.optimization_barrier(jnp.sum(raw * raw, axis=-1, keepdims=True)) + eps)

def split_heads(matrix):
    return matrix.reshape(matrix.shape[0], H, DH).transpose(1, 0, 2)

def head_attend(queries, keyset, values, direction, beta_rate, length):
    seq_len = queries.shape[0]
    row_ids = jnp.arange(seq_len)[:, None]
    col_ids = jnp.arange(seq_len)[None, :]
    strictly = col_ids < row_ids
    up_to = col_ids <= row_ids
    system = jnp.eye(seq_len, dtype=jnp.float32) + jnp.where(strictly, matmul_hi(direction, direction.T) * beta_rate[None, :], 0.0)
    coupled = jnp.where(strictly, matmul_hi(direction, keyset.T), 0.0)
    solved = jax.scipy.linalg.solve_triangular(system, coupled, lower=True, unit_diagonal=True)
    crossing = jnp.where(up_to, matmul_hi(queries, direction.T), 0.0) * beta_rate[None, :]
    scores = (matmul_hi(queries, keyset.T) - matmul_hi(crossing, solved)) * queries.shape[1] ** (-0.5)
    allowed = up_to & (col_ids < length)
    masked = jnp.where(allowed, scores, -1e+30)
    row_max = lax.optimization_barrier(jnp.max(masked, axis=1, keepdims=True))
    row_total = lax.optimization_barrier(jnp.sum(jnp.where(allowed, jnp.exp(masked - row_max), 0.0), axis=1, keepdims=True))
    log_total = row_max + jnp.log(row_total)
    probs = low(jnp.where(allowed, jnp.exp(masked - log_total), 0.0))
    return matmul_hi(probs, values)

def layer(stream_in, length, gain_one, w_query, w_key, w_value, w_path, w_beta, w_out, gain_two, w_gate, w_up, w_down):
    seq_len = stream_in.shape[0]
    live_mask = (jnp.arange(seq_len) < length).astype(jnp.float32)[:, None]
    normed = low(rms_norm(stream_in, gain_one))
    queries = low(low_back(matmul_hi(normed, w_query)))
    keyset = low(low_back(matmul_hi(normed, w_key)))
    values = low(low_back(matmul_hi(normed, w_value)))
    raw = low_back(matmul_hi(normed, w_path)).reshape(seq_len, H, DH)
    direction = low(unit_rows(raw))
    beta_rate = 2.0 * jax.nn.sigmoid(low_back(matmul_hi(normed, w_beta)))

    def per_head(pieces):
        return head_attend(pieces[0], pieces[1], pieces[2], pieces[3], pieces[4], length)
    stacked = (split_heads(queries), split_heads(keyset), split_heads(values), direction.transpose(1, 0, 2), beta_rate.T)
    heads_out = lax.map(jax.checkpoint(per_head), stacked)
    mixed = low(low_back(heads_out.transpose(1, 0, 2).reshape(seq_len, H * DH)))
    attn_out = low_back(matmul_hi(mixed, w_out))
    stream = stream_in + live_mask * attn_out
    normed_two = low(rms_norm(stream, gain_two))
    gate_pre = low_back(matmul_hi(normed_two, w_gate))
    up_pre = low_back(matmul_hi(normed_two, w_up))
    hidden = low(jax.nn.silu(gate_pre) * up_pre)
    feed_out = low_back(matmul_hi(hidden, w_down))
    return (live_mask * (stream + feed_out), attn_out, feed_out)

def reference(tokens, cotangent, lengths, gain_one, w_query, w_key, w_value, w_path, w_beta, w_out, gain_two, w_gate, w_up, w_down):
    params = tuple((param.astype(jnp.float32) for param in (gain_one, w_query, w_key, w_value, w_path, w_beta, w_out, gain_two, w_gate, w_up, w_down)))
    stream_all = tokens.astype(jnp.float32).reshape(GROUPS, SEQ, D)
    cot_all = cotangent.astype(jnp.float32).reshape(GROUPS, SEQ, D)

    def one_group(carried, item_pair):
        totals, squares = carried
        stream_in, cot_rows, length = item_pair

        def forward(value, *weights):
            result, attn_out, feed_out = layer(value, length, *weights)
            return (result, (attn_out, feed_out))
        result, pull_back, (attn_out, feed_out) = jax.vjp(forward, stream_in, *params, has_aux=True)
        grads = pull_back(cot_rows)
        live_mask = (jnp.arange(SEQ) < length).astype(jnp.float32)[:, None]
        squares = squares + jnp.stack([jnp.sum(live_mask * stream_in * stream_in), jnp.sum(live_mask * attn_out * attn_out), jnp.sum(live_mask * feed_out * feed_out)])
        totals = tuple((running + grad for running, grad in zip(totals, grads[1:])))
        return ((totals, squares), (result.astype(jnp.bfloat16), grads[0].astype(jnp.bfloat16)))
    start = (tuple((jnp.zeros_like(param) for param in params)), jnp.zeros((3,), jnp.float32))
    (totals, squares), (outputs, input_grads) = lax.scan(one_group, start, (stream_all, cot_all, lengths))
    valid_count = jnp.sum(lengths).astype(jnp.float32) * D
    rms_all = jnp.sqrt(squares / valid_count)
    return (outputs.reshape(TOKENS, D), input_grads.reshape(TOKENS, D), totals[0], totals[1], totals[2], totals[3], totals[4], totals[5], totals[6], totals[7], totals[8], totals[9], totals[10], rms_all[0], rms_all[1], rms_all[2])
```

```python
import functools

import jax
import jax.numpy as jnp
from jax import lax
from jax.experimental import pallas as pl
from jax.experimental.pallas import tpu as pltpu
from jax.sharding import PartitionSpec as P

f32 = jnp.float32
bf16 = jnp.bfloat16

eps = 1e-06
highest = lax.Precision.HIGHEST


def rms_norm(value, gain_vec):
    factor = lax.rsqrt(jnp.mean(value * value, axis=-1, keepdims=True) + eps)
    return value * factor * gain_vec


def unit_rows(raw):
    return raw * lax.rsqrt(jnp.sum(raw * raw, axis=-1, keepdims=True) + eps)


def rounded(value):
    return lax.optimization_barrier(value.astype(jnp.bfloat16)).astype(jnp.float32)


def round_pass(value):
    return value + lax.stop_gradient(rounded(value) - value)


def split_heads(matrix, head_count):
    return matrix.reshape(matrix.shape[0], head_count, -1).transpose(1, 0, 2)


def join_heads(matrix):
    return matrix.transpose(1, 0, 2).reshape(matrix.shape[1], -1)


def mul_low(left, right):
    return jnp.dot(left, right, preferred_element_type=jnp.float32)


def back_mul(grad_rows, weight):
    return jnp.einsum("tg,fg->tf", grad_rows, weight, preferred_element_type=jnp.float32)


def weight_grad(left, right):
    return jnp.einsum("tf,tg->fg", left, right, preferred_element_type=jnp.float32)


def masks(block_len):
    row_ids = jnp.arange(block_len)[:, None]
    col_ids = jnp.arange(block_len)[None, :]
    return (col_ids < row_ids, col_ids <= row_ids)


def block_system(direction, beta_rate):
    block_len = direction.shape[1]
    strictly, up_to = masks(block_len)
    gram = jnp.einsum("htd,hsd->hts", direction, direction, precision=highest)
    return jnp.eye(block_len, dtype=jnp.float32)[None] + jnp.where(
        strictly[None], gram * beta_rate[:, None, :], 0.0
    )


def own_context(keyset, values, direction, beta_rate):
    system = block_system(direction, beta_rate)
    strictly, up_to = masks(keyset.shape[1])
    coupled = jnp.where(
        strictly[None], jnp.einsum("htd,hjd->htj", direction, keyset, precision=highest), 0.0
    )
    solved = jax.scipy.linalg.solve_triangular(system, coupled, lower=True, unit_diagonal=True)
    scaled_dir = direction * beta_rate[:, :, None]
    key_end = keyset - jnp.einsum("htj,htd->hjd", solved, scaled_dir, precision=highest)
    through = jax.scipy.linalg.solve_triangular(system, direction, lower=True, unit_diagonal=True)
    block_map = jnp.eye(direction.shape[2], dtype=jnp.float32)[None] - jnp.einsum(
        "htm,htn->hmn", scaled_dir, through, precision=highest
    )
    return (join_heads(key_end), join_heads(values), block_map[None])


def attend(
    queries, keyset, values, direction, beta_rate, key_far, value_far, maps_far, my_block, length
):
    head_count, block_len, head_width = queries.shape
    blocks = maps_far.shape[0]
    score_scale = head_width ** (-0.5)
    strictly, up_to = masks(block_len)
    system = block_system(direction, beta_rate)
    coupled = jnp.where(
        strictly[None], jnp.einsum("htd,hjd->htj", direction, keyset, precision=highest), 0.0
    )
    solved = jax.scipy.linalg.solve_triangular(system, coupled, lower=True, unit_diagonal=True)
    crossing = (
        jnp.where(
            up_to[None], jnp.einsum("hid,htd->hit", queries, direction, precision=highest), 0.0
        )
        * beta_rate[:, None, :]
    )
    near_scores = (
        jnp.einsum("hid,hjd->hij", queries, keyset, precision=highest)
        - jnp.einsum("hit,htj->hij", crossing, solved, precision=highest)
    ) * score_scale
    back_solved = jax.scipy.linalg.solve_triangular(
        system, crossing.transpose(0, 2, 1), lower=True, trans=1, unit_diagonal=True
    )
    moved = queries - jnp.einsum("hti,htd->hid", back_solved, direction, precision=highest)

    def advance(carried, item_pair):
        block_map, index = item_pair
        updated = jnp.einsum("hid,hde->hie", carried, block_map, precision=highest)
        return (jnp.where(index < my_block, updated, carried), carried)

    unused, reached = lax.scan(advance, moved, (maps_far, jnp.arange(blocks)), reverse=True)
    far_keys = key_far.reshape(blocks, block_len, head_count, head_width)
    far_values = value_far.reshape(blocks, block_len, head_count, head_width)
    far_scores = jnp.einsum("ehid,ejhd->ehij", reached, far_keys, precision=highest) * score_scale
    positions = jnp.arange(block_len)
    near_ok = up_to[None] & ((my_block * block_len + positions)[None, None, :] < length)
    block_ids = jnp.arange(blocks)
    far_ok = (block_ids[:, None, None, None] < my_block) & (
        (block_ids[:, None] * block_len + positions[None, :])[:, None, None, :] < length
    )
    near_masked = jnp.where(near_ok, near_scores, -1e30)
    far_masked = jnp.where(far_ok, far_scores, -1e30)
    row_max = jnp.maximum(jnp.max(near_masked, axis=2), jnp.max(far_masked, axis=(0, 3)))[
        :, :, None
    ]
    row_total = jnp.sum(jnp.where(near_ok, jnp.exp(near_masked - row_max), 0.0), axis=2) + jnp.sum(
        jnp.where(far_ok, jnp.exp(far_masked - row_max[None]), 0.0), axis=(0, 3)
    )
    log_total = row_max + jnp.log(row_total)[:, :, None]
    near_probs = round_pass(jnp.where(near_ok, jnp.exp(near_masked - log_total), 0.0))
    far_probs = round_pass(jnp.where(far_ok, jnp.exp(far_masked - log_total[None]), 0.0))
    return jnp.einsum("hij,hjd->hid", near_probs, values, precision=highest) + jnp.einsum(
        "ehij,ejhd->hid", far_probs, far_values, precision=highest
    )


def gathered_layer(
    tokens,
    cotangent,
    lengths,
    gain_one,
    w_query,
    w_key,
    w_value,
    w_path,
    w_beta,
    w_out,
    gain_two,
    w_gate,
    w_up,
    w_down,
):
    gain_a, query_w, key_w, value_w, path_w, beta_w, out_w, gain_b, gate_w, up_w, down_w = (
        lax.all_gather(gain_one, "shard", axis=0, tiled=True),
        lax.all_gather(w_query, "shard", axis=0, tiled=True),
        lax.all_gather(w_key, "shard", axis=0, tiled=True),
        lax.all_gather(w_value, "shard", axis=0, tiled=True),
        lax.all_gather(w_path, "shard", axis=0, tiled=True),
        lax.all_gather(w_beta, "shard", axis=0, tiled=True),
        lax.all_gather(w_out, "shard", axis=0, tiled=True),
        lax.all_gather(gain_two, "shard", axis=0, tiled=True),
        lax.all_gather(w_gate, "shard", axis=0, tiled=True),
        lax.all_gather(w_up, "shard", axis=0, tiled=True),
        lax.all_gather(w_down, "shard", axis=0, tiled=True),
    )
    block_len = tokens.shape[0]
    width = tokens.shape[1]
    head_count = beta_w.shape[1]
    my_block = lax.axis_index("shard")
    length = lengths[0]
    live_mask = (my_block * block_len + jnp.arange(block_len) < length).astype(jnp.float32)[:, None]
    stream_in = tokens.astype(jnp.float32)
    normed_f, norm_pull = jax.vjp(rms_norm, stream_in, gain_a.astype(jnp.float32))
    normed = normed_f.astype(jnp.bfloat16)
    queries = split_heads(rounded(mul_low(normed, query_w)), head_count)
    keyset = split_heads(rounded(mul_low(normed, key_w)), head_count)
    values_h = split_heads(rounded(mul_low(normed, value_w)), head_count)
    raw = mul_low(normed, path_w).reshape(block_len, head_count, -1)
    direction_f, unit_pull = jax.vjp(unit_rows, raw)
    direction = rounded(direction_f).transpose(1, 0, 2)
    beta_rate = 2.0 * jax.nn.sigmoid(mul_low(normed, beta_w))
    (key_end, value_own, map_own), context_pull = jax.vjp(
        own_context, keyset, values_h, direction, beta_rate.T
    )
    key_far, value_far, maps_far = (
        lax.all_gather(key_end.astype(jnp.bfloat16), "shard", axis=0, tiled=True).astype(
            key_end.dtype
        ),
        lax.all_gather(value_own.astype(jnp.bfloat16), "shard", axis=0, tiled=True).astype(
            value_own.dtype
        ),
        lax.all_gather(map_own.astype(jnp.bfloat16), "shard", axis=0, tiled=True).astype(
            map_own.dtype
        ),
    )

    def local_attend(
        queries, keyset, values_h, direction, beta_heads, key_far, value_far, maps_far
    ):
        return attend(
            queries,
            keyset,
            values_h,
            direction,
            beta_heads,
            key_far,
            value_far,
            maps_far,
            my_block,
            length,
        )

    heads_out, attend_pull = jax.vjp(
        local_attend,
        queries,
        keyset,
        values_h,
        direction,
        beta_rate.T,
        key_far,
        value_far,
        maps_far,
    )
    mixed = join_heads(heads_out).astype(jnp.bfloat16)
    attn_out = mul_low(mixed, out_w)
    stream = stream_in + live_mask * attn_out
    normed_two_f, norm_two_pull = jax.vjp(rms_norm, stream, gain_b.astype(jnp.float32))
    normed_two = normed_two_f.astype(jnp.bfloat16)
    gate_pre = mul_low(normed_two, gate_w)
    up_pre = mul_low(normed_two, up_w)
    gate_sig = jax.nn.sigmoid(gate_pre)
    hidden = (gate_pre * gate_sig * up_pre).astype(jnp.bfloat16)
    feed_out = mul_low(hidden, down_w)
    output = (live_mask * (stream + feed_out)).astype(jnp.bfloat16)
    cot_rows = cotangent.astype(jnp.float32) * live_mask
    d_feed = cot_rows.astype(jnp.bfloat16)
    d_hidden = back_mul(d_feed, down_w)
    d_gate = (d_hidden * up_pre * gate_sig * (1.0 + gate_pre * (1.0 - gate_sig))).astype(
        jnp.bfloat16
    )
    d_up = (d_hidden * gate_pre * gate_sig).astype(jnp.bfloat16)
    d_normed_two = back_mul(d_gate, gate_w) + back_mul(d_up, up_w)
    d_stream_norm, grad_gain_b = norm_two_pull(d_normed_two)
    d_stream = cot_rows + d_stream_norm
    d_attn = (live_mask * d_stream).astype(jnp.bfloat16)
    d_mixed = split_heads(rounded(back_mul(d_attn, out_w)), head_count)
    (
        d_queries,
        d_keys_near,
        d_values_near,
        d_dir_near,
        d_beta_near,
        d_key_far,
        d_value_far,
        d_maps_far,
    ) = attend_pull(d_mixed)
    d_key_end, d_value_own, d_map_own = (
        lax.psum_scatter(
            d_key_far.astype(jnp.bfloat16), "shard", scatter_dimension=0, tiled=True
        ).astype(jnp.float32),
        lax.psum_scatter(
            d_value_far.astype(jnp.bfloat16), "shard", scatter_dimension=0, tiled=True
        ).astype(jnp.float32),
        lax.psum_scatter(
            d_maps_far.astype(jnp.bfloat16), "shard", scatter_dimension=0, tiled=True
        ).astype(jnp.float32),
    )
    d_keys_ctx, d_values_ctx, d_dir_ctx, d_beta_ctx = context_pull(
        (d_key_end, d_value_own, d_map_own)
    )
    d_query_b = join_heads(d_queries).astype(jnp.bfloat16)
    d_key_b = join_heads(d_keys_near + d_keys_ctx).astype(jnp.bfloat16)
    d_value_b = join_heads(d_values_near + d_values_ctx).astype(jnp.bfloat16)
    (d_raw,) = unit_pull((d_dir_near + d_dir_ctx).transpose(1, 0, 2))
    d_raw_b = d_raw.reshape(block_len, -1).astype(jnp.bfloat16)
    d_beta_total = (d_beta_near + d_beta_ctx).T
    d_logit_b = (d_beta_total * beta_rate * (1.0 - 0.5 * beta_rate)).astype(jnp.bfloat16)
    d_normed = (
        back_mul(d_query_b, query_w)
        + back_mul(d_key_b, key_w)
        + back_mul(d_value_b, value_w)
        + back_mul(d_raw_b, path_w)
        + back_mul(d_logit_b, beta_w)
    )
    d_stream_in, grad_gain_a = norm_pull(d_normed)
    input_grad = (d_stream_in + d_stream).astype(jnp.bfloat16)
    g_query = weight_grad(normed, d_query_b)
    g_key = weight_grad(normed, d_key_b)
    g_value = weight_grad(normed, d_value_b)
    g_path = weight_grad(normed, d_raw_b)
    g_beta = weight_grad(normed, d_logit_b)
    g_out = weight_grad(mixed, d_attn)
    g_gate = weight_grad(normed_two, d_gate)
    g_up = weight_grad(normed_two, d_up)
    g_down = weight_grad(hidden, d_feed)
    part_sums = (
        lax.psum_scatter(
            grad_gain_a.astype(jnp.bfloat16), "shard", scatter_dimension=0, tiled=True
        ).astype(jnp.float32),
        lax.psum_scatter(
            g_query.astype(jnp.bfloat16), "shard", scatter_dimension=0, tiled=True
        ).astype(jnp.float32),
        lax.psum_scatter(
            g_key.astype(jnp.bfloat16), "shard", scatter_dimension=0, tiled=True
        ).astype(jnp.float32),
        lax.psum_scatter(
            g_value.astype(jnp.bfloat16), "shard", scatter_dimension=0, tiled=True
        ).astype(jnp.float32),
        lax.psum_scatter(
            g_path.astype(jnp.bfloat16), "shard", scatter_dimension=0, tiled=True
        ).astype(jnp.float32),
        lax.psum_scatter(
            g_beta.astype(jnp.bfloat16), "shard", scatter_dimension=0, tiled=True
        ).astype(jnp.float32),
        lax.psum_scatter(
            g_out.astype(jnp.bfloat16), "shard", scatter_dimension=0, tiled=True
        ).astype(jnp.float32),
        lax.psum_scatter(
            grad_gain_b.astype(jnp.bfloat16), "shard", scatter_dimension=0, tiled=True
        ).astype(jnp.float32),
        lax.psum_scatter(
            g_gate.astype(jnp.bfloat16), "shard", scatter_dimension=0, tiled=True
        ).astype(jnp.float32),
        lax.psum_scatter(
            g_up.astype(jnp.bfloat16), "shard", scatter_dimension=0, tiled=True
        ).astype(jnp.float32),
        lax.psum_scatter(
            g_down.astype(jnp.bfloat16), "shard", scatter_dimension=0, tiled=True
        ).astype(jnp.float32),
    )
    owned = (
        lax.psum(part_sums[0].astype(jnp.bfloat16), "rep").astype(jnp.float32),
        lax.psum(part_sums[1].astype(jnp.bfloat16), "rep").astype(jnp.float32),
        lax.psum(part_sums[2].astype(jnp.bfloat16), "rep").astype(jnp.float32),
        lax.psum(part_sums[3].astype(jnp.bfloat16), "rep").astype(jnp.float32),
        lax.psum(part_sums[4].astype(jnp.bfloat16), "rep").astype(jnp.float32),
        lax.psum(part_sums[5].astype(jnp.bfloat16), "rep").astype(jnp.float32),
        lax.psum(part_sums[6].astype(jnp.bfloat16), "rep").astype(jnp.float32),
        lax.psum(part_sums[7].astype(jnp.bfloat16), "rep").astype(jnp.float32),
        lax.psum(part_sums[8].astype(jnp.bfloat16), "rep").astype(jnp.float32),
        lax.psum(part_sums[9].astype(jnp.bfloat16), "rep").astype(jnp.float32),
        lax.psum(part_sums[10].astype(jnp.bfloat16), "rep").astype(jnp.float32),
    )
    sq_input, sq_attn, sq_feed, live_total = lax.psum(
        (
            jnp.sum(live_mask * stream_in * stream_in),
            jnp.sum(live_mask * attn_out * attn_out),
            jnp.sum(live_mask * feed_out * feed_out),
            jnp.sum(live_mask),
        ),
        ("rep", "shard"),
    )
    denom = live_total * width
    return (
        output,
        input_grad,
        owned[0],
        owned[1],
        owned[2],
        owned[3],
        owned[4],
        owned[5],
        owned[6],
        owned[7],
        owned[8],
        owned[9],
        owned[10],
        jnp.sqrt(sq_input / denom),
        jnp.sqrt(sq_attn / denom),
        jnp.sqrt(sq_feed / denom),
    )


def dot_nn(a,b): return lax.dot_general(a,b,(((1,),(0,)),((),())),preferred_element_type=f32)
def dot_nt(a,b): return lax.dot_general(a,b,(((1,),(1,)),((),())),preferred_element_type=f32)
def dot_tn(a,b): return lax.dot_general(a,b,(((0,),(0,)),((),())),preferred_element_type=f32)

def halves(a):
    hi=a.astype(bf16)
    return hi,(a-hi.astype(f32)).astype(bf16)

def mul3(dot,a,b):
    return dot(a[0],b[0])+(dot(a[0],b[1])+dot(a[1],b[0]))

def mul2(dot,a,b):
    return dot(a[0],b)+dot(a[1],b)

def iota2(n,ax): return lax.broadcasted_iota(jnp.int32,(n,n),ax)

def tri_inverse(system, blk):
    n=system.shape[0]
    r=iota2(blk,0); c=iota2(blk,1)
    eye=jnp.where(r==c,1.0,0.0)
    outs=[]
    tiles=[system[i*blk:(i+1)*blk,i*blk:(i+1)*blk] for i in range(n//blk)]
    invs=[eye-jnp.where(((r>>1)==(c>>1))&((r&1)==1)&((c&1)==0),t,0.0) for t in tiles]
    b=2
    while b<blk:
        m=((r//(2*b))==(c//(2*b)))&(((r//b)&1)==1)&(((c//b)&1)==0)
        new=[]
        for t,v in zip(tiles,invs):
            vs=halves(v)
            low=mul3(dot_nn,halves(jnp.where(m,t,0.0)),vs)
            new.append(v-mul3(dot_nn,vs,halves(low)))
        invs=new; b*=2
    size=blk
    while size<n:
        new=[]
        for i in range(0,len(invs),2):
            a,d=invs[i],invs[i+1]
            off=system[(i+1)*size:(i+2)*size,i*size:(i+1)*size]
            low=mul3(dot_nn,halves(off),halves(a))
            low=-mul3(dot_nn,halves(d),halves(low))
            new.append(jnp.concatenate([jnp.concatenate([a,jnp.zeros_like(a)],1),jnp.concatenate([low,d],1)],0))
        invs=new; size*=2
    return invs[0]

def quads(a):
    h=a.shape[0]//2
    return a[:h,:h],a[h:,:h],a[h:,h:]

def join(a11,a21,a22):
    return jnp.concatenate([jnp.concatenate([a11,jnp.zeros_like(a11)],1),jnp.concatenate([a21,a22],1)],0)

def low_nn(a,b):
    a11,a21,a22=zip(*[quads(v) for v in a]); b11,b21,b22=zip(*[quads(v) for v in b])
    return join(mul3(dot_nn,a11,b11), mul3(dot_nn,a21,b11)+mul3(dot_nn,a22,b21), mul3(dot_nn,a22,b22))
def low_nt(a,b):
    a11,a21,a22=zip(*[quads(v) for v in a]); b11,b21,b22=zip(*[quads(v) for v in b])
    return join(mul3(dot_nt,a11,b11), mul3(dot_nt,a21,b11), mul3(dot_nt,a21,b21)+mul3(dot_nt,a22,b22))
def low_tn(a,b):
    a11,a21,a22=zip(*[quads(v) for v in a]); b11,b21,b22=zip(*[quads(v) for v in b])
    return join(mul3(dot_tn,a11,b11)+mul3(dot_tn,a21,b21), mul3(dot_tn,a22,b21), mul3(dot_tn,a22,b22))

def ordered(ref, mine, count):
    return jnp.concatenate([ref[jnp.bitwise_xor(mine,j)] for j in range(count)],0)

def unit(raw):
    u=lax.rsqrt(jnp.sum(raw*raw,axis=-1,keepdims=True)+eps)
    return u

def fwd_kernel(scal, q_ref,k_ref,v_ref,w_ref,b_ref, mixed_ref, inv_ref, ctx_ref, p_ref):
    mine=scal[0]; length=scal[1]
    cnt=q_ref.shape[0]
    q=ordered(q_ref,mine,cnt).astype(bf16); k=ordered(k_ref,mine,cnt).astype(bf16)
    v=ordered(v_ref,mine,cnt).astype(bf16); raw=ordered(w_ref,mine,cnt)
    w=(raw*unit(raw)).astype(bf16)
    logit=jnp.concatenate([b_ref[0,pl.ds(jnp.bitwise_xor(mine,j),1),:] for j in range(cnt)],1)
    beta=2.0*jax.nn.sigmoid(logit)
    n=q.shape[0]
    r=iota2(n,0); c=iota2(n,1)
    strict=c<r; upto=c<=r
    system=jnp.where(strict,dot_nt(w,w)*beta,0.0)
    inv=tri_inverse(system,128)
    coupled=jnp.where(strict,dot_nt(w,k),0.0)
    invs=halves(inv)
    ctx=low_nn(invs,halves(coupled))
    ctxs=halves(ctx)
    cross=jnp.where(upto,dot_nt(q,w)*beta,0.0)
    scores=(dot_nt(q,k)-low_nn(halves(cross),ctxs))*(q.shape[1]**-0.5)
    allowed=upto&(c<length)
    masked=jnp.where(allowed,scores,-1e30)
    top=jnp.max(masked,axis=1,keepdims=True)
    e=jnp.where(allowed,jnp.exp(masked-top),0.0)
    log_total=top+jnp.log(jnp.sum(e,axis=1,keepdims=True))
    p=jnp.where(allowed,jnp.exp(masked-log_total),0.0)
    out=dot_nn(p.astype(bf16),v).astype(bf16)
    blk=n//cnt
    for j in range(cnt):
        mixed_ref[jnp.bitwise_xor(mine,j)]=out[j*blk:(j+1)*blk]
    for i in range(2):
        inv_ref[0,i]=invs[i]; ctx_ref[0,i]=ctxs[i]
    p_ref[0]=p

def bwd_kernel(scal, q_ref,k_ref,v_ref,w_ref,b_ref, inv_ref, ctx_ref, p_ref, dm_ref, dq_ref,dk_ref,dv_ref,dr_ref,dl_ref):
    mine=scal[0]
    cnt=q_ref.shape[0]
    q=ordered(q_ref,mine,cnt).astype(bf16); k=ordered(k_ref,mine,cnt).astype(bf16)
    v=ordered(v_ref,mine,cnt).astype(bf16); raw=ordered(w_ref,mine,cnt)
    dm=ordered(dm_ref,mine,cnt)
    u=unit(raw)
    w=(raw*u).astype(bf16)
    logit=jnp.concatenate([b_ref[0,pl.ds(jnp.bitwise_xor(mine,j),1),:] for j in range(cnt)],1)
    beta=2.0*jax.nn.sigmoid(logit)
    n=q.shape[0]
    r=iota2(n,0); c=iota2(n,1)
    strict=c<r; upto=c<=r
    invs=(inv_ref[0,0],inv_ref[0,1]); ctxs=(ctx_ref[0,0],ctx_ref[0,1])
    p=p_ref[0]
    d_v=dot_tn(p.astype(bf16),dm)
    dp=dot_nt(dm,v)
    g=p*(dp-jnp.sum(p*dp,axis=1,keepdims=True))*(q.shape[1]**-0.5)
    gs=halves(g)
    qw=dot_nt(q,w)
    cross=jnp.where(upto,qw*beta,0.0)
    d_cross=-low_nt(gs,ctxs)
    d_cross=jnp.where(upto,d_cross,0.0)
    y=-low_tn(invs,halves(low_tn(halves(cross),gs)))
    y=jnp.where(strict,y,0.0)
    ys=halves(y)
    d_sys=jnp.where(strict,-low_nt(ys,ctxs),0.0)
    ww=dot_nt(w,w)
    d_beta=jnp.sum(d_cross*qw+d_sys*ww,axis=0,keepdims=True)
    dxb=halves(d_cross*beta)
    bm=halves(d_sys*beta)
    d_q=mul2(dot_nn,gs,k)+mul2(dot_nn,dxb,w)
    d_k=mul2(dot_tn,gs,q)+mul2(dot_tn,ys,w)
    d_w=mul2(dot_tn,dxb,q)+mul2(dot_nn,ys,k)+mul2(dot_nn,bm,w)+mul2(dot_tn,bm,w)
    d_raw=u*d_w-raw*(u*u*u)*jnp.sum(raw*d_w,axis=1,keepdims=True)
    d_logit=d_beta*beta*(1.0-0.5*beta)
    blk=n//cnt
    for j in range(cnt):
        at=jnp.bitwise_xor(mine,j); sl=slice(j*blk,(j+1)*blk)
        dq_ref[at]=d_q[sl].astype(bf16); dk_ref[at]=d_k[sl].astype(bf16)
        dv_ref[at]=d_v[sl].astype(bf16); dr_ref[at]=d_raw[sl].astype(bf16)
        dl_ref[0,pl.ds(at,1),:]=d_logit[:,sl]

def specs(cnt,blk,width,heads,n):
    def col(off): return pl.BlockSpec((cnt,blk,width),lambda h,s,off=off:(0,0,off+h))
    bs=pl.BlockSpec((1,cnt,blk),lambda h,s:(s[2]+h,0,0))
    pair=pl.BlockSpec((1,2,n,n),lambda h,s:(h,0,0,0))
    full=pl.BlockSpec((1,n,n),lambda h,s:(h,0,0))
    return col,bs,pair,full

def attend_forward(scal, proj, logit, heads):
    cnt,blk,cols=proj.shape; width=cols//(4*heads); n=cnt*blk
    col,bs,pair,full=specs(cnt,blk,width,heads,n)
    return pl.pallas_call(fwd_kernel,
      grid_spec=pltpu.PrefetchScalarGridSpec(num_scalar_prefetch=1,grid=(heads,),
        in_specs=[col(0),col(heads),col(2*heads),col(3*heads),bs],
        out_specs=[col(0),pair,pair,full]),
      out_shape=[jax.ShapeDtypeStruct((cnt,blk,heads*width),bf16),jax.ShapeDtypeStruct((heads,2,n,n),bf16),
        jax.ShapeDtypeStruct((heads,2,n,n),bf16),jax.ShapeDtypeStruct((heads,n,n),f32)],
      compiler_params=pltpu.CompilerParams(vmem_limit_bytes=56<<20),
      name="path_forward")(scal,proj,proj,proj,proj,logit)

def attend_backward(scal, proj, logit, inv, ctx, p, d_mixed, heads):
    cnt,blk,cols=proj.shape; width=cols//(4*heads); n=cnt*blk
    col,bs,pair,full=specs(cnt,blk,width,heads,n)
    ob=pl.BlockSpec((1,cnt,blk),lambda h,s:(h,0,0))
    act=jax.ShapeDtypeStruct((cnt,blk,heads*width),bf16)
    return pl.pallas_call(bwd_kernel,
      grid_spec=pltpu.PrefetchScalarGridSpec(num_scalar_prefetch=1,grid=(heads,),
        in_specs=[col(0),col(heads),col(2*heads),col(3*heads),bs,pair,pair,full,col(0)],
        out_specs=[col(0)]*4+[ob]),
      out_shape=[act]*4+[jax.ShapeDtypeStruct((heads,cnt,blk),f32)],
      compiler_params=pltpu.CompilerParams(vmem_limit_bytes=56<<20),
      name="path_backward")(scal,proj,proj,proj,proj,logit,inv,ctx,p,d_mixed)

SHARDS = 4
CHIPS = 4


def shard_swap(value, k):
    return lax.ppermute(value, "shard", [(i, i ^ k) for i in range(SHARDS)])


def core_swap(value):
    return lax.ppermute(value, "rep", [(i, i ^ 1) for i in range(2 * CHIPS)])


def chip_swap(value, k):
    return lax.ppermute(value, "rep", [(i, i ^ (2 * k)) for i in range(2 * CHIPS)])


def chip_send(value, pairs):
    return lax.ppermute(value, "rep", [(2 * a + c, 2 * b + c) for a, b in pairs for c in (0, 1)])


def gather_xor(value):
    return [value] + [shard_swap(value, k) for k in range(1, SHARDS)]


def mat(left, right):
    return dot_nn(left, right)


def put(target, value, row, col):
    return lax.dynamic_update_slice(target, value, (row, col))


def take_cols(value, at, size):
    return lax.dynamic_slice_in_dim(value, at, size, axis=1)


def take_rows(value, at, size):
    return lax.dynamic_slice_in_dim(value, at, size, axis=0)


def chip_sum(chunks, hub):
    count = len(chunks)
    arrived = {}
    totals = {}
    outs = {}
    for t in range(count):
        own = chunks[t]
        if t >= 2:
            own, _ = lax.optimization_barrier((own, arrived[t - 2]))
        arrived[t] = chip_send(own, [(0, 1), (3, 2)])
        pair = (chunks[t].astype(f32) + arrived[t].astype(f32)).astype(bf16)
        other = chip_send(pair, [(1, 2), (2, 1)])
        totals[t] = (pair.astype(f32) + other.astype(f32)).astype(bf16)
        back = chip_send(totals[t], [(1, 0), (2, 3)])
        outs[t] = jnp.where(hub, totals[t], back)
    return [outs[t] for t in range(count)]


def sharded_layer(
    tokens,
    cotangent,
    lengths,
    gain_one,
    w_query,
    w_key,
    w_value,
    w_path,
    w_beta,
    w_out,
    gain_two,
    w_gate,
    w_up,
    w_down,
):
    rows, width = tokens.shape
    part = w_query.shape[0]
    head_count = w_beta.shape[1]
    heads = head_count // SHARDS
    ff_part = w_down.shape[0]
    ff_core = ff_part // 2
    seq = rows * SHARDS
    mine = lax.axis_index("shard")
    rep = lax.axis_index("rep")
    core = rep % 2
    chip = rep // 2
    hub = (chip == 1) | (chip == 2)
    first_core = core == 0
    length = lengths[0]
    peers = [jnp.bitwise_xor(mine, k) for k in range(SHARDS)]
    live = (mine * rows + jnp.arange(rows) < length).astype(f32)[:, None]
    scal = jnp.stack([mine, length, mine * heads]).astype(jnp.int32)

    tok = jnp.stack(gather_xor(tokens))
    small = jnp.concatenate(
        [w_beta.T, gain_one[None], gain_two[None], jnp.zeros((2, part), bf16)], 0
    )
    small_all = jnp.zeros((small.shape[0], width), bf16)
    for k, piece in enumerate(gather_xor(small)):
        small_all = put(small_all, piece, 0, peers[k] * part)
    beta_w = small_all[:head_count]
    gain_a = small_all[head_count].astype(f32)
    gain_b = small_all[head_count + 1].astype(f32)

    def head_cols(k, flip):
        at = peers[k] * part
        left = jnp.where(
            first_core != flip, take_cols(w_query, at, part), take_cols(w_value, at, part)
        )
        right = jnp.where(
            first_core != flip, take_cols(w_key, at, part), take_cols(w_path, at, part)
        )
        return jnp.concatenate([left, right], 1)

    proj_w = jnp.zeros((width, 4 * part), bf16)
    own_at, other_at = core * 2 * part, (1 - core) * 2 * part
    for k in range(SHARDS):
        at = peers[k] * part
        if k == 0:
            ours, theirs = head_cols(0, False), head_cols(0, True)
        else:
            ours = shard_swap(head_cols(k, False), k)
            theirs = core_swap(ours)
        proj_w = put(put(proj_w, ours, at, own_at), theirs, at, other_at)

    tok_f = tok.astype(f32)
    factor_one = lax.rsqrt(jnp.mean(tok_f * tok_f, axis=-1, keepdims=True) + eps)
    normed = (tok_f * factor_one * gain_a).astype(bf16).reshape(seq, width)
    proj = mat(normed, proj_w).reshape(SHARDS, rows, 4 * part)
    logit = dot_nt(beta_w, normed).reshape(head_count, SHARDS, rows)
    mixed, inv, ctx, probs = attend_forward(scal, proj, logit, heads)

    half = width // 2
    out_w = jnp.zeros((width, width), bf16)
    for k in range(SHARDS):
        if k == 0:
            ours, theirs = take_cols(w_out, core * half, half), take_cols(w_out, (1 - core) * half, half)
        else:
            ours = shard_swap(take_cols(w_out, core * half, half), k)
            theirs = core_swap(ours)
        out_w = put(put(out_w, ours, k * part, core * half), theirs, k * part, (1 - core) * half)
    ff_w = jnp.zeros((width, 2 * ff_core), bf16)
    for k in range(SHARDS):
        at = peers[k] * ff_part + core * ff_core
        piece = jnp.concatenate([take_cols(w_gate, at, ff_core), take_cols(w_up, at, ff_core)], 1)
        if k:
            piece = shard_swap(piece, k)
        ff_w = put(ff_w, piece, peers[k] * part, 0)
    down_w = take_rows(w_down, core * ff_core, ff_core)
    cot_rows = cotangent.astype(f32) * live
    d_feed_own = gather_xor(cot_rows.astype(bf16))
    d_feed = jnp.concatenate(d_feed_own + [core_swap(v) for v in d_feed_own], 0)

    mixed_rows = jnp.concatenate(
        [mixed[0]] + [shard_swap(mixed[k], k) for k in range(1, SHARDS)], 1
    )
    attn_out = mat(mixed_rows, out_w)
    own_tok = tokens.astype(f32)
    stream = own_tok + live * attn_out
    factor_two = lax.rsqrt(jnp.mean(stream * stream, axis=-1, keepdims=True) + eps)
    normed_two = (stream * factor_two * gain_b).astype(bf16)
    n_two_own = gather_xor(normed_two)
    n_two = jnp.concatenate(n_two_own + [core_swap(v) for v in n_two_own], 0)

    gate_up = mat(n_two, ff_w)
    gate, up = gate_up[:, :ff_core], gate_up[:, ff_core:]
    sig = jax.nn.sigmoid(gate)
    hidden = (gate * sig * up).astype(bf16)
    d_hidden = dot_nt(d_feed, down_w)
    d_gate = (d_hidden * up * sig * (1.0 + gate * (1.0 - sig))).astype(bf16)
    d_up = (d_hidden * gate * sig).astype(bf16)
    d_gate_up = jnp.concatenate([d_gate, d_up], 1)

    def rows_home(partial):
        sent = core_swap(partial[seq:].astype(bf16))
        chip_part = partial[:seq] + sent.astype(f32)
        total = chip_part[:rows]
        for k in range(1, SHARDS):
            piece = chip_part[k * rows : (k + 1) * rows].astype(bf16)
            total = total + shard_swap(piece, k).astype(f32)
        return total

    d_n_two = rows_home(dot_nt(d_gate_up, ff_w))
    g_down = dot_tn(hidden, d_feed).astype(bf16)
    g_ff = dot_tn(n_two, d_gate_up).astype(bf16)
    feed_out = rows_home(mat(hidden, down_w))
    output = (live * (stream + feed_out)).astype(bf16)

    def home_rows(grad):
        pieces = [take_rows(grad, peers[k] * part, part) for k in range(SHARDS)]
        return [pieces[0]] + [shard_swap(pieces[k], k) for k in range(1, SHARDS)]

    chunks = [g_down[: ff_core // 2], g_down[ff_core // 2 :]] + home_rows(g_ff)

    scaled = d_n_two * gain_b
    mean_two = jnp.mean(stream * scaled, axis=-1, keepdims=True)
    d_stream = cot_rows + factor_two * scaled - stream * (factor_two**3 * mean_two)
    part_gain_b = jnp.sum(d_n_two * stream * factor_two, axis=0)
    d_attn = jnp.concatenate(gather_xor((live * d_stream).astype(bf16)), 0)
    d_mixed = dot_nt(d_attn, w_out).astype(bf16).reshape(SHARDS, rows, part)
    g_out = dot_tn(mixed.reshape(seq, part), d_attn)
    g_out_sent = core_swap(take_rows(g_out, (1 - core) * (part // 2), part // 2).astype(bf16))
    g_out_own = take_rows(g_out, core * (part // 2), part // 2) + g_out_sent.astype(f32)
    chunks.append(g_out_own.astype(bf16))

    d_query, d_key, d_value, d_raw, d_logit = attend_backward(
        scal, proj, logit, inv, ctx, probs, d_mixed, heads
    )
    d_proj = jnp.concatenate([d_query, d_key, d_value, d_raw], 2).reshape(seq, 4 * part)
    d_logit_b = d_logit.astype(bf16).reshape(heads, seq)
    g_theirs = dot_tn(normed, take_cols(d_proj, other_at, 2 * part)).astype(bf16)
    g_ours = dot_tn(normed, take_cols(d_proj, own_at, 2 * part))
    g_proj = (g_ours + core_swap(g_theirs).astype(f32)).astype(bf16)
    chunks += home_rows(g_proj)
    sums = chip_sum(chunks, hub)

    beta_rows = take_rows(beta_w, mine * heads, heads)
    d_n_one = dot_nt(d_proj, proj_w) + dot_tn(d_logit_b, beta_rows)
    part_gain_a = jnp.sum(
        d_n_one.reshape(SHARDS, rows, width) * tok_f * factor_one, axis=(0, 1)
    )
    d_one = d_n_one[:rows]
    for k in range(1, SHARDS):
        d_one = d_one + shard_swap(d_n_one[k * rows : (k + 1) * rows].astype(bf16), k).astype(f32)
    scaled = d_one * gain_a
    factor_own = factor_one[0]
    mean_one = jnp.mean(own_tok * scaled, axis=-1, keepdims=True)
    input_grad = (
        d_stream + factor_own * scaled - own_tok * (factor_own**3 * mean_one)
    ).astype(bf16)

    part_beta = mat(d_logit_b, normed)
    squares = jnp.stack(
        [
            jnp.sum(live * own_tok * own_tok),
            jnp.sum(live * attn_out * attn_out),
            jnp.sum(live * feed_out * feed_out),
            jnp.sum(live),
        ]
    )
    squares = jnp.concatenate([squares, jnp.zeros((part - 4,), f32)])
    gains = jnp.stack([part_gain_a, part_gain_b])
    beta_grad = jnp.zeros((head_count, part), f32)
    shared = jnp.zeros((3, part), f32)
    for k in range(SHARDS):
        at = peers[k] * part
        piece = jnp.concatenate(
            [take_cols(part_beta, at, part), take_cols(gains, at, part), squares[None]], 0
        )
        if k:
            piece = shard_swap(piece, k)
        beta_grad = put(beta_grad, piece[:heads], peers[k] * heads, 0)
        shared = shared + piece[heads:]
    shared = jnp.concatenate([beta_grad, shared], 0)
    shared = shared + core_swap(shared)
    shared = shared + chip_swap(shared, 1)
    shared = shared + chip_swap(shared, 2)
    grad_beta = shared[:head_count].T
    grad_gain_a, grad_gain_b = shared[head_count], shared[head_count + 1]
    sq_input, sq_attn, sq_feed, live_total = (shared[head_count + 2, i] for i in range(4))
    denom = live_total * width

    down_sum = jnp.concatenate(sums[:2], 0)
    grad_down = jnp.zeros((ff_part, width), f32)
    grad_down = put(grad_down, down_sum.astype(f32), core * ff_core, 0)
    grad_down = put(grad_down, core_swap(down_sum).astype(f32), (1 - core) * ff_core, 0)
    grad_gate = jnp.zeros((part, SHARDS * ff_part), f32)
    grad_up = jnp.zeros((part, SHARDS * ff_part), f32)
    for k in range(SHARDS):
        both = sums[2 + k]
        for piece, which in ((both, core), (core_swap(both), 1 - core)):
            piece = piece.astype(f32)
            at = peers[k] * ff_part + which * ff_core
            grad_gate = put(grad_gate, piece[:, :ff_core], 0, at)
            grad_up = put(grad_up, piece[:, ff_core:], 0, at)
    grad_out = jnp.zeros((part, width), f32)
    grad_out = put(grad_out, sums[6].astype(f32), core * (part // 2), 0)
    grad_out = put(grad_out, core_swap(sums[6]).astype(f32), (1 - core) * (part // 2), 0)
    grads = [jnp.zeros((part, width), f32) for i in range(4)]
    for k in range(SHARDS):
        ours = sums[7 + k]
        theirs = core_swap(ours)
        low = jnp.where(first_core, ours, theirs).astype(f32)
        high = jnp.where(first_core, theirs, ours).astype(f32)
        for i, both in enumerate((low, low, high, high)):
            off = (i % 2) * part
            grads[i] = put(grads[i], both[:, off : off + part], 0, peers[k] * part)

    return (
        output,
        input_grad,
        grad_gain_a,
        grads[0],
        grads[1],
        grads[2],
        grads[3],
        grad_beta,
        grad_out,
        grad_gain_b,
        grad_gate,
        grad_up,
        grad_down,
        jnp.sqrt(sq_input / denom),
        jnp.sqrt(sq_attn / denom),
        jnp.sqrt(sq_feed / denom),
    )


def pick(mesh):
    def layer(*args):
        head_count, ff_part = args[8].shape[1], args[13].shape[0]
        fits = mesh.shape["shard"] == SHARDS and mesh.shape["rep"] == 2 * CHIPS
        fits = fits and head_count % SHARDS == 0 and ff_part % 256 == 0
        fits = fits and args[4].shape[1] == 128 * head_count and args[0].shape[0] == 128
        return (sharded_layer if fits else gathered_layer)(*args)

    return layer


def solution(mesh):
    return jax.shard_map(
        pick(mesh),
        mesh=mesh,
        in_specs=(
            P(("rep", "shard"), None),
            P(("rep", "shard"), None),
            P("rep"),
            P("shard"),
            P("shard", None),
            P("shard", None),
            P("shard", None),
            P("shard", None),
            P("shard", None),
            P("shard", None),
            P("shard"),
            P("shard", None),
            P("shard", None),
            P("shard", None),
        ),
        out_specs=(
            P(("rep", "shard"), None),
            P(("rep", "shard"), None),
            P("shard"),
            P("shard", None),
            P("shard", None),
            P("shard", None),
            P("shard", None),
            P("shard", None),
            P("shard", None),
            P("shard"),
            P("shard", None),
            P("shard", None),
            P("shard", None),
            P(),
            P(),
            P(),
        ),
        check_vma=False,
    )
```

```python
import functools

import jax
import jax.numpy as jnp
from jax import lax
from jax.experimental import pallas as pl
from jax.experimental.pallas import tpu as pltpu
from jax.sharding import PartitionSpec as P

f32 = jnp.float32
bf16 = jnp.bfloat16

eps = 1e-06
highest = lax.Precision.HIGHEST


def rms_norm(value, gain_vec):
    factor = lax.rsqrt(jnp.mean(value * value, axis=-1, keepdims=True) + eps)
    return value * factor * gain_vec


def unit_rows(raw):
    return raw * lax.rsqrt(jnp.sum(raw * raw, axis=-1, keepdims=True) + eps)


def rounded(value):
    return lax.optimization_barrier(value.astype(jnp.bfloat16)).astype(jnp.float32)


def round_pass(value):
    return value + lax.stop_gradient(rounded(value) - value)


def split_heads(matrix, head_count):
    return matrix.reshape(matrix.shape[0], head_count, -1).transpose(1, 0, 2)


def join_heads(matrix):
    return matrix.transpose(1, 0, 2).reshape(matrix.shape[1], -1)


def mul_low(left, right):
    return jnp.dot(left, right, preferred_element_type=jnp.float32)


def back_mul(grad_rows, weight):
    return jnp.einsum("tg,fg->tf", grad_rows, weight, preferred_element_type=jnp.float32)


def weight_grad(left, right):
    return jnp.einsum("tf,tg->fg", left, right, preferred_element_type=jnp.float32)


def masks(block_len):
    row_ids = jnp.arange(block_len)[:, None]
    col_ids = jnp.arange(block_len)[None, :]
    return (col_ids < row_ids, col_ids <= row_ids)


def block_system(direction, beta_rate):
    block_len = direction.shape[1]
    strictly, up_to = masks(block_len)
    gram = jnp.einsum("htd,hsd->hts", direction, direction, precision=highest)
    return jnp.eye(block_len, dtype=jnp.float32)[None] + jnp.where(
        strictly[None], gram * beta_rate[:, None, :], 0.0
    )


def own_context(keyset, values, direction, beta_rate):
    system = block_system(direction, beta_rate)
    strictly, up_to = masks(keyset.shape[1])
    coupled = jnp.where(
        strictly[None], jnp.einsum("htd,hjd->htj", direction, keyset, precision=highest), 0.0
    )
    solved = jax.scipy.linalg.solve_triangular(system, coupled, lower=True, unit_diagonal=True)
    scaled_dir = direction * beta_rate[:, :, None]
    key_end = keyset - jnp.einsum("htj,htd->hjd", solved, scaled_dir, precision=highest)
    through = jax.scipy.linalg.solve_triangular(system, direction, lower=True, unit_diagonal=True)
    block_map = jnp.eye(direction.shape[2], dtype=jnp.float32)[None] - jnp.einsum(
        "htm,htn->hmn", scaled_dir, through, precision=highest
    )
    return (join_heads(key_end), join_heads(values), block_map[None])


def attend(
    queries, keyset, values, direction, beta_rate, key_far, value_far, maps_far, my_block, length
):
    head_count, block_len, head_width = queries.shape
    blocks = maps_far.shape[0]
    score_scale = head_width ** (-0.5)
    strictly, up_to = masks(block_len)
    system = block_system(direction, beta_rate)
    coupled = jnp.where(
        strictly[None], jnp.einsum("htd,hjd->htj", direction, keyset, precision=highest), 0.0
    )
    solved = jax.scipy.linalg.solve_triangular(system, coupled, lower=True, unit_diagonal=True)
    crossing = (
        jnp.where(
            up_to[None], jnp.einsum("hid,htd->hit", queries, direction, precision=highest), 0.0
        )
        * beta_rate[:, None, :]
    )
    near_scores = (
        jnp.einsum("hid,hjd->hij", queries, keyset, precision=highest)
        - jnp.einsum("hit,htj->hij", crossing, solved, precision=highest)
    ) * score_scale
    back_solved = jax.scipy.linalg.solve_triangular(
        system, crossing.transpose(0, 2, 1), lower=True, trans=1, unit_diagonal=True
    )
    moved = queries - jnp.einsum("hti,htd->hid", back_solved, direction, precision=highest)

    def advance(carried, item_pair):
        block_map, index = item_pair
        updated = jnp.einsum("hid,hde->hie", carried, block_map, precision=highest)
        return (jnp.where(index < my_block, updated, carried), carried)

    unused, reached = lax.scan(advance, moved, (maps_far, jnp.arange(blocks)), reverse=True)
    far_keys = key_far.reshape(blocks, block_len, head_count, head_width)
    far_values = value_far.reshape(blocks, block_len, head_count, head_width)
    far_scores = jnp.einsum("ehid,ejhd->ehij", reached, far_keys, precision=highest) * score_scale
    positions = jnp.arange(block_len)
    near_ok = up_to[None] & ((my_block * block_len + positions)[None, None, :] < length)
    block_ids = jnp.arange(blocks)
    far_ok = (block_ids[:, None, None, None] < my_block) & (
        (block_ids[:, None] * block_len + positions[None, :])[:, None, None, :] < length
    )
    near_masked = jnp.where(near_ok, near_scores, -1e30)
    far_masked = jnp.where(far_ok, far_scores, -1e30)
    row_max = jnp.maximum(jnp.max(near_masked, axis=2), jnp.max(far_masked, axis=(0, 3)))[
        :, :, None
    ]
    row_total = jnp.sum(jnp.where(near_ok, jnp.exp(near_masked - row_max), 0.0), axis=2) + jnp.sum(
        jnp.where(far_ok, jnp.exp(far_masked - row_max[None]), 0.0), axis=(0, 3)
    )
    log_total = row_max + jnp.log(row_total)[:, :, None]
    near_probs = round_pass(jnp.where(near_ok, jnp.exp(near_masked - log_total), 0.0))
    far_probs = round_pass(jnp.where(far_ok, jnp.exp(far_masked - log_total[None]), 0.0))
    return jnp.einsum("hij,hjd->hid", near_probs, values, precision=highest) + jnp.einsum(
        "ehij,ejhd->hid", far_probs, far_values, precision=highest
    )


def gathered_layer(
    tokens,
    cotangent,
    lengths,
    gain_one,
    w_query,
    w_key,
    w_value,
    w_path,
    w_beta,
    w_out,
    gain_two,
    w_gate,
    w_up,
    w_down,
):
    gain_a, query_w, key_w, value_w, path_w, beta_w, out_w, gain_b, gate_w, up_w, down_w = (
        lax.all_gather(gain_one, "shard", axis=0, tiled=True),
        lax.all_gather(w_query, "shard", axis=0, tiled=True),
        lax.all_gather(w_key, "shard", axis=0, tiled=True),
        lax.all_gather(w_value, "shard", axis=0, tiled=True),
        lax.all_gather(w_path, "shard", axis=0, tiled=True),
        lax.all_gather(w_beta, "shard", axis=0, tiled=True),
        lax.all_gather(w_out, "shard", axis=0, tiled=True),
        lax.all_gather(gain_two, "shard", axis=0, tiled=True),
        lax.all_gather(w_gate, "shard", axis=0, tiled=True),
        lax.all_gather(w_up, "shard", axis=0, tiled=True),
        lax.all_gather(w_down, "shard", axis=0, tiled=True),
    )
    block_len = tokens.shape[0]
    width = tokens.shape[1]
    head_count = beta_w.shape[1]
    my_block = lax.axis_index("shard")
    length = lengths[0]
    live_mask = (my_block * block_len + jnp.arange(block_len) < length).astype(jnp.float32)[:, None]
    stream_in = tokens.astype(jnp.float32)
    normed_f, norm_pull = jax.vjp(rms_norm, stream_in, gain_a.astype(jnp.float32))
    normed = normed_f.astype(jnp.bfloat16)
    queries = split_heads(rounded(mul_low(normed, query_w)), head_count)
    keyset = split_heads(rounded(mul_low(normed, key_w)), head_count)
    values_h = split_heads(rounded(mul_low(normed, value_w)), head_count)
    raw = mul_low(normed, path_w).reshape(block_len, head_count, -1)
    direction_f, unit_pull = jax.vjp(unit_rows, raw)
    direction = rounded(direction_f).transpose(1, 0, 2)
    beta_rate = 2.0 * jax.nn.sigmoid(mul_low(normed, beta_w))
    (key_end, value_own, map_own), context_pull = jax.vjp(
        own_context, keyset, values_h, direction, beta_rate.T
    )
    key_far, value_far, maps_far = (
        lax.all_gather(key_end.astype(jnp.bfloat16), "shard", axis=0, tiled=True).astype(
            key_end.dtype
        ),
        lax.all_gather(value_own.astype(jnp.bfloat16), "shard", axis=0, tiled=True).astype(
            value_own.dtype
        ),
        lax.all_gather(map_own.astype(jnp.bfloat16), "shard", axis=0, tiled=True).astype(
            map_own.dtype
        ),
    )

    def local_attend(
        queries, keyset, values_h, direction, beta_heads, key_far, value_far, maps_far
    ):
        return attend(
            queries,
            keyset,
            values_h,
            direction,
            beta_heads,
            key_far,
            value_far,
            maps_far,
            my_block,
            length,
        )

    heads_out, attend_pull = jax.vjp(
        local_attend,
        queries,
        keyset,
        values_h,
        direction,
        beta_rate.T,
        key_far,
        value_far,
        maps_far,
    )
    mixed = join_heads(heads_out).astype(jnp.bfloat16)
    attn_out = mul_low(mixed, out_w)
    stream = stream_in + live_mask * attn_out
    normed_two_f, norm_two_pull = jax.vjp(rms_norm, stream, gain_b.astype(jnp.float32))
    normed_two = normed_two_f.astype(jnp.bfloat16)
    gate_pre = mul_low(normed_two, gate_w)
    up_pre = mul_low(normed_two, up_w)
    gate_sig = jax.nn.sigmoid(gate_pre)
    hidden = (gate_pre * gate_sig * up_pre).astype(jnp.bfloat16)
    feed_out = mul_low(hidden, down_w)
    output = (live_mask * (stream + feed_out)).astype(jnp.bfloat16)
    cot_rows = cotangent.astype(jnp.float32) * live_mask
    d_feed = cot_rows.astype(jnp.bfloat16)
    d_hidden = back_mul(d_feed, down_w)
    d_gate = (d_hidden * up_pre * gate_sig * (1.0 + gate_pre * (1.0 - gate_sig))).astype(
        jnp.bfloat16
    )
    d_up = (d_hidden * gate_pre * gate_sig).astype(jnp.bfloat16)
    d_normed_two = back_mul(d_gate, gate_w) + back_mul(d_up, up_w)
    d_stream_norm, grad_gain_b = norm_two_pull(d_normed_two)
    d_stream = cot_rows + d_stream_norm
    d_attn = (live_mask * d_stream).astype(jnp.bfloat16)
    d_mixed = split_heads(rounded(back_mul(d_attn, out_w)), head_count)
    (
        d_queries,
        d_keys_near,
        d_values_near,
        d_dir_near,
        d_beta_near,
        d_key_far,
        d_value_far,
        d_maps_far,
    ) = attend_pull(d_mixed)
    d_key_end, d_value_own, d_map_own = (
        lax.psum_scatter(
            d_key_far.astype(jnp.bfloat16), "shard", scatter_dimension=0, tiled=True
        ).astype(jnp.float32),
        lax.psum_scatter(
            d_value_far.astype(jnp.bfloat16), "shard", scatter_dimension=0, tiled=True
        ).astype(jnp.float32),
        lax.psum_scatter(
            d_maps_far.astype(jnp.bfloat16), "shard", scatter_dimension=0, tiled=True
        ).astype(jnp.float32),
    )
    d_keys_ctx, d_values_ctx, d_dir_ctx, d_beta_ctx = context_pull(
        (d_key_end, d_value_own, d_map_own)
    )
    d_query_b = join_heads(d_queries).astype(jnp.bfloat16)
    d_key_b = join_heads(d_keys_near + d_keys_ctx).astype(jnp.bfloat16)
    d_value_b = join_heads(d_values_near + d_values_ctx).astype(jnp.bfloat16)
    (d_raw,) = unit_pull((d_dir_near + d_dir_ctx).transpose(1, 0, 2))
    d_raw_b = d_raw.reshape(block_len, -1).astype(jnp.bfloat16)
    d_beta_total = (d_beta_near + d_beta_ctx).T
    d_logit_b = (d_beta_total * beta_rate * (1.0 - 0.5 * beta_rate)).astype(jnp.bfloat16)
    d_normed = (
        back_mul(d_query_b, query_w)
        + back_mul(d_key_b, key_w)
        + back_mul(d_value_b, value_w)
        + back_mul(d_raw_b, path_w)
        + back_mul(d_logit_b, beta_w)
    )
    d_stream_in, grad_gain_a = norm_pull(d_normed)
    input_grad = (d_stream_in + d_stream).astype(jnp.bfloat16)
    g_query = weight_grad(normed, d_query_b)
    g_key = weight_grad(normed, d_key_b)
    g_value = weight_grad(normed, d_value_b)
    g_path = weight_grad(normed, d_raw_b)
    g_beta = weight_grad(normed, d_logit_b)
    g_out = weight_grad(mixed, d_attn)
    g_gate = weight_grad(normed_two, d_gate)
    g_up = weight_grad(normed_two, d_up)
    g_down = weight_grad(hidden, d_feed)
    part_sums = (
        lax.psum_scatter(
            grad_gain_a.astype(jnp.bfloat16), "shard", scatter_dimension=0, tiled=True
        ).astype(jnp.float32),
        lax.psum_scatter(
            g_query.astype(jnp.bfloat16), "shard", scatter_dimension=0, tiled=True
        ).astype(jnp.float32),
        lax.psum_scatter(
            g_key.astype(jnp.bfloat16), "shard", scatter_dimension=0, tiled=True
        ).astype(jnp.float32),
        lax.psum_scatter(
            g_value.astype(jnp.bfloat16), "shard", scatter_dimension=0, tiled=True
        ).astype(jnp.float32),
        lax.psum_scatter(
            g_path.astype(jnp.bfloat16), "shard", scatter_dimension=0, tiled=True
        ).astype(jnp.float32),
        lax.psum_scatter(
            g_beta.astype(jnp.bfloat16), "shard", scatter_dimension=0, tiled=True
        ).astype(jnp.float32),
        lax.psum_scatter(
            g_out.astype(jnp.bfloat16), "shard", scatter_dimension=0, tiled=True
        ).astype(jnp.float32),
        lax.psum_scatter(
            grad_gain_b.astype(jnp.bfloat16), "shard", scatter_dimension=0, tiled=True
        ).astype(jnp.float32),
        lax.psum_scatter(
            g_gate.astype(jnp.bfloat16), "shard", scatter_dimension=0, tiled=True
        ).astype(jnp.float32),
        lax.psum_scatter(
            g_up.astype(jnp.bfloat16), "shard", scatter_dimension=0, tiled=True
        ).astype(jnp.float32),
        lax.psum_scatter(
            g_down.astype(jnp.bfloat16), "shard", scatter_dimension=0, tiled=True
        ).astype(jnp.float32),
    )
    owned = (
        lax.psum(part_sums[0].astype(jnp.bfloat16), "rep").astype(jnp.float32),
        lax.psum(part_sums[1].astype(jnp.bfloat16), "rep").astype(jnp.float32),
        lax.psum(part_sums[2].astype(jnp.bfloat16), "rep").astype(jnp.float32),
        lax.psum(part_sums[3].astype(jnp.bfloat16), "rep").astype(jnp.float32),
        lax.psum(part_sums[4].astype(jnp.bfloat16), "rep").astype(jnp.float32),
        lax.psum(part_sums[5].astype(jnp.bfloat16), "rep").astype(jnp.float32),
        lax.psum(part_sums[6].astype(jnp.bfloat16), "rep").astype(jnp.float32),
        lax.psum(part_sums[7].astype(jnp.bfloat16), "rep").astype(jnp.float32),
        lax.psum(part_sums[8].astype(jnp.bfloat16), "rep").astype(jnp.float32),
        lax.psum(part_sums[9].astype(jnp.bfloat16), "rep").astype(jnp.float32),
        lax.psum(part_sums[10].astype(jnp.bfloat16), "rep").astype(jnp.float32),
    )
    sq_input, sq_attn, sq_feed, live_total = lax.psum(
        (
            jnp.sum(live_mask * stream_in * stream_in),
            jnp.sum(live_mask * attn_out * attn_out),
            jnp.sum(live_mask * feed_out * feed_out),
            jnp.sum(live_mask),
        ),
        ("rep", "shard"),
    )
    denom = live_total * width
    return (
        output,
        input_grad,
        owned[0],
        owned[1],
        owned[2],
        owned[3],
        owned[4],
        owned[5],
        owned[6],
        owned[7],
        owned[8],
        owned[9],
        owned[10],
        jnp.sqrt(sq_input / denom),
        jnp.sqrt(sq_attn / denom),
        jnp.sqrt(sq_feed / denom),
    )


def dot_nn(a, b):
    return lax.dot_general(a, b, (((1,), (0,)), ((), ())), preferred_element_type=f32)


def dot_nt(a, b):
    return lax.dot_general(a, b, (((1,), (1,)), ((), ())), preferred_element_type=f32)


def dot_tn(a, b):
    return lax.dot_general(a, b, (((0,), (0,)), ((), ())), preferred_element_type=f32)


def halves(a):
    hi = a.astype(bf16)
    return hi, (a - hi.astype(f32)).astype(bf16)


def mul3(dot, a, b):
    return dot(a[0], b[0]) + (dot(a[0], b[1]) + dot(a[1], b[0]))


def mul2(dot, a, b):
    return dot(a[0], b) + dot(a[1], b)


def iota2(n, ax):
    return lax.broadcasted_iota(jnp.int32, (n, n), ax)


def tri_inverse(system, blk):
    n = system.shape[0]
    r, c = iota2(blk, 0), iota2(blk, 1)
    eye = jnp.where(r == c, 1.0, 0.0)
    tiles = [system[i * blk : (i + 1) * blk, i * blk : (i + 1) * blk] for i in range(n // blk)]
    pairs = ((r >> 1) == (c >> 1)) & ((r & 1) == 1) & ((c & 1) == 0)
    invs = [eye - jnp.where(pairs, t, 0.0) for t in tiles]
    b = 2
    while b < blk:
        m = ((r // (2 * b)) == (c // (2 * b))) & (((r // b) & 1) == 1) & (((c // b) & 1) == 0)
        new = []
        for t, v in zip(tiles, invs):
            vs = halves(v)
            low = mul3(dot_nn, halves(jnp.where(m, t, 0.0)), vs)
            new.append(v - mul3(dot_nn, vs, halves(low)))
        invs = new
        b *= 2
    size = blk
    while size < n:
        new = []
        for i in range(0, len(invs), 2):
            a, d = invs[i], invs[i + 1]
            off = system[(i + 1) * size : (i + 2) * size, i * size : (i + 1) * size]
            low = mul3(dot_nn, halves(off), halves(a))
            new.append(join(a, -mul3(dot_nn, halves(d), halves(low)), d))
        invs = new
        size *= 2
    return invs[0]


def quads(a):
    h = a.shape[0] // 2
    return a[:h, :h], a[h:, :h], a[h:, h:]


def join(a11, a21, a22):
    upper = jnp.concatenate([a11, jnp.zeros_like(a11)], 1)
    return jnp.concatenate([upper, jnp.concatenate([a21, a22], 1)], 0)


def low_nn(a, b):
    a11, a21, a22 = zip(*[quads(v) for v in a])
    b11, b21, b22 = zip(*[quads(v) for v in b])
    return join(
        mul3(dot_nn, a11, b11),
        mul3(dot_nn, a21, b11) + mul3(dot_nn, a22, b21),
        mul3(dot_nn, a22, b22),
    )


def low_nt(a, b):
    a11, a21, a22 = zip(*[quads(v) for v in a])
    b11, b21, b22 = zip(*[quads(v) for v in b])
    return join(
        mul3(dot_nt, a11, b11),
        mul3(dot_nt, a21, b11),
        mul3(dot_nt, a21, b21) + mul3(dot_nt, a22, b22),
    )


def low_tn(a, b):
    a11, a21, a22 = zip(*[quads(v) for v in a])
    b11, b21, b22 = zip(*[quads(v) for v in b])
    return join(
        mul3(dot_tn, a11, b11) + mul3(dot_tn, a21, b21),
        mul3(dot_tn, a22, b21),
        mul3(dot_tn, a22, b22),
    )


def aligned(at, size):
    return pl.ds(pl.multiple_of(at, 128), size)


def unit_factor(raw):
    return lax.rsqrt(jnp.sum(raw * raw, axis=-1, keepdims=True) + eps)


def forward_kernel(scal, q_ref, k_ref, v_ref, w_ref, b_ref, mixed_ref, inv_ref, ctx_ref, p_ref):
    length = scal[2]
    q, k, v, raw = q_ref[...], k_ref[...], v_ref[...], w_ref[...]
    w = (raw * unit_factor(raw)).astype(bf16)
    beta = 2.0 * jax.nn.sigmoid(b_ref[0])
    n = q.shape[0]
    r, c = iota2(n, 0), iota2(n, 1)
    strict, upto = c < r, c <= r
    inv = halves(tri_inverse(jnp.where(strict, dot_nt(w, w) * beta, 0.0), 128))
    ctx = halves(low_nn(inv, halves(jnp.where(strict, dot_nt(w, k), 0.0))))
    cross = jnp.where(upto, dot_nt(q, w) * beta, 0.0)
    scores = (dot_nt(q, k) - low_nn(halves(cross), ctx)) * (q.shape[1] ** -0.5)
    allowed = upto & (c < length)
    masked = jnp.where(allowed, scores, -1e30)
    top = jnp.max(masked, axis=1, keepdims=True)
    e = jnp.where(allowed, jnp.exp(masked - top), 0.0)
    log_total = top + jnp.log(jnp.sum(e, axis=1, keepdims=True))
    p = jnp.where(allowed, jnp.exp(masked - log_total), 0.0)
    mixed_ref[...] = dot_nn(p.astype(bf16), v).astype(bf16)
    for i in range(2):
        inv_ref[0, i] = inv[i]
        ctx_ref[0, i] = ctx[i]
    p_ref[0] = p


def backward_kernel(scal, *refs):
    q_ref, k_ref, v_ref, w_ref, b_ref, inv_ref, ctx_ref, p_ref, dm_ref = refs[:9]
    dq_ref, dk_ref, dv_ref, dr_ref, dl_ref = refs[9:]
    q, k, v, raw, dm = q_ref[...], k_ref[...], v_ref[...], w_ref[...], dm_ref[...]
    u = unit_factor(raw)
    w = (raw * u).astype(bf16)
    beta = 2.0 * jax.nn.sigmoid(b_ref[0])
    n = q.shape[0]
    r, c = iota2(n, 0), iota2(n, 1)
    strict, upto = c < r, c <= r
    inv = inv_ref[0, 0], inv_ref[0, 1]
    ctx = ctx_ref[0, 0], ctx_ref[0, 1]
    p = p_ref[0]
    d_v = dot_tn(p.astype(bf16), dm)
    dp = dot_nt(dm, v)
    g = p * (dp - jnp.sum(p * dp, axis=1, keepdims=True)) * (q.shape[1] ** -0.5)
    gs = halves(g)
    qw = dot_nt(q, w)
    cross = jnp.where(upto, qw * beta, 0.0)
    d_cross = jnp.where(upto, -low_nt(gs, ctx), 0.0)
    y = jnp.where(strict, -low_tn(inv, halves(low_tn(halves(cross), gs))), 0.0)
    ys = halves(y)
    d_sys = jnp.where(strict, -low_nt(ys, ctx), 0.0)
    d_beta = jnp.sum(d_cross * qw + d_sys * dot_nt(w, w), axis=0, keepdims=True)
    dx = halves(d_cross * beta)
    bm = halves(d_sys * beta)
    d_q = mul2(dot_nn, gs, k) + mul2(dot_nn, dx, w)
    d_k = mul2(dot_tn, gs, q) + mul2(dot_tn, ys, w)
    d_w = mul2(dot_tn, dx, q) + mul2(dot_nn, ys, k) + mul2(dot_nn, bm, w) + mul2(dot_tn, bm, w)
    d_raw = u * d_w - raw * (u * u * u) * jnp.sum(raw * d_w, axis=1, keepdims=True)
    for ref, val in ((dq_ref, d_q), (dk_ref, d_k), (dv_ref, d_v), (dr_ref, d_raw)):
        ref[...] = val.astype(bf16)
    dl_ref[0] = d_beta * beta * (1.0 - 0.5 * beta)


def grant():
    return pltpu.CompilerParams(vmem_limit_bytes=60 << 20)


def cost(micros):
    return pl.CostEstimate(flops=int(micros * 1e6), bytes_accessed=0, transcendentals=0)


def struct(shape, kind):
    return jax.ShapeDtypeStruct(shape, kind)


def head_specs(n, width):
    col = pl.BlockSpec((n, width), lambda h, s: (0, h))
    row = pl.BlockSpec((1, 1, n), lambda h, s: (h, 0, 0))
    pair = pl.BlockSpec((1, 2, n, n), lambda h, s: (h, 0, 0, 0))
    full = pl.BlockSpec((1, n, n), lambda h, s: (h, 0, 0))
    return col, row, pair, full


def attend_forward(scal, q, k, v, raw, logit, heads):
    n, width = q.shape[0], q.shape[1] // heads
    col, row, pair, full = head_specs(n, width)
    two = struct((heads, 2, n, n), bf16)
    return pl.pallas_call(
        forward_kernel,
        grid_spec=pltpu.PrefetchScalarGridSpec(
            num_scalar_prefetch=1,
            grid=(heads,),
            in_specs=[col] * 4 + [row],
            out_specs=[col, pair, pair, full],
        ),
        out_shape=[struct(q.shape, bf16), two, two, struct((heads, n, n), f32)],
        compiler_params=grant(),
        cost_estimate=cost(8),
        name="attend_forward",
    )(scal, q, k, v, raw, logit)


def attend_backward(scal, q, k, v, raw, logit, inv, ctx, p, dm, heads):
    n, width = q.shape[0], q.shape[1] // heads
    col, row, pair, full = head_specs(n, width)
    return pl.pallas_call(
        backward_kernel,
        grid_spec=pltpu.PrefetchScalarGridSpec(
            num_scalar_prefetch=1,
            grid=(heads,),
            in_specs=[col] * 4 + [row, pair, pair, full, col],
            out_specs=[col] * 4 + [row],
        ),
        out_shape=[struct(q.shape, bf16)] * 4 + [struct((heads, 1, n), f32)],
        compiler_params=grant(),
        cost_estimate=cost(4),
        name="attend_backward",
    )(scal, q, k, v, raw, logit, inv, ctx, p, dm)


def whole(kernel, name, micros, outs, scal, *args, scratch=()):
    vmem = pl.BlockSpec(memory_space=pltpu.VMEM)
    return pl.pallas_call(
        kernel,
        in_specs=[pl.BlockSpec(memory_space=pltpu.SMEM)] + [vmem] * len(args),
        out_specs=[vmem] * len(outs),
        out_shape=list(outs),
        scratch_shapes=list(scratch),
        compiler_params=grant(),
        cost_estimate=cost(micros),
        name=name,
    )(scal, *args)


def head_pick_kernel(scal, wq, wk, wv, wp, *outs):
    mine, first = scal[0], scal[1] == 0
    part = wq.shape[0]
    for k, out in enumerate(outs, 1):
        at = aligned((mine ^ k) * part, part)
        out[:, :part] = jnp.where(first, wq[:, at], wv[:, at])
        out[:, part:] = jnp.where(first, wk[:, at], wp[:, at])


def ff_pick_kernel(scal, wg, wu, out):
    half = out.shape[2] // 2
    for k in range(4):
        at = aligned((2 * k + scal[1]) * half, half)
        out[k, :, :half] = wg[:, at]
        out[k, :, half:] = wu[:, at]


def project_kernel(scal, *refs):
    toks, own_w, ours, theirs = refs[:4], refs[4:8], refs[8:11], refs[11:14]
    tok_ref, normed, q_ref, k_ref, v_ref, raw_ref = refs[14:20]
    logit_ref, beta_ref, gain_a, gain_b, small = refs[20:]
    mine, first = scal[0], scal[1] == 0
    part = own_w[0].shape[0]
    rows = tok_ref.shape[1]
    heads = beta_ref.shape[0]
    count = 4 * heads
    ats = [aligned((mine ^ k) * part, part) for k in range(4)]
    for k in range(4):
        lines = toks[k][rows : rows + 4, :].astype(f32)
        for r in range(count + 2):
            piece = lines[r // 4 : r // 4 + 1, (r % 4) * part : (r % 4 + 1) * part]
            small[r : r + 1, ats[k]] = piece
    gain_a[...] = small[count : count + 1, :]
    gain_b[...] = small[count + 1 : count + 2, :]
    for h in range(heads):
        beta_ref[h : h + 1, :] = small[pl.ds(mine * heads + h, 1), :]
    for b in range(4):
        tok_ref[mine ^ b] = toks[b][:rows, :]
        x = toks[b][:rows, :].astype(f32)
        factor = lax.rsqrt(jnp.mean(x * x, axis=-1, keepdims=True) + eps)
        normed[aligned((mine ^ b) * rows, rows), :] = (x * factor * gain_a[...]).astype(bf16)
    logit = dot_nt(beta_ref[...].astype(bf16), normed[...])
    for h in range(heads):
        logit_ref[h] = logit[h : h + 1]
    n_own = normed[:, ats[0]]
    sums = [dot_nn(n_own, w[:, ats[0]]) for w in own_w]
    left, right = jnp.concatenate(sums[:2], 1), jnp.concatenate(sums[2:], 1)
    a, b = jnp.where(first, left, right), jnp.where(first, right, left)
    for k in range(1, 4):
        n_k = normed[:, ats[k]]
        a = a + dot_nn(n_k, ours[k - 1][...])
        b = b + dot_nn(n_k, theirs[k - 1][...])
    qk, vp = jnp.where(first, a, b), jnp.where(first, b, a)
    q_ref[...] = qk[:, :part].astype(bf16)
    k_ref[...] = qk[:, part:].astype(bf16)
    v_ref[...] = vp[:, :part].astype(bf16)
    raw_ref[...] = vp[:, part:]


def live_rows(scal, rows):
    at = scal[0] * rows + lax.broadcasted_iota(jnp.int32, (rows, 1), 0)
    return jnp.where(at < scal[2], 1.0, 0.0)


def block_sum(ref):
    return (ref[0].astype(f32) + ref[1].astype(f32)) + (ref[2].astype(f32) + ref[3].astype(f32))


def middle_kernel(scal, tok, gain, come, stream_ref, normed_ref, square_ref):
    rows = stream_ref.shape[0]
    attn = live_rows(scal, rows) * block_sum(come)
    square_ref[...] = jnp.sum(attn * attn, axis=0, keepdims=True)
    stream = tok[...].astype(f32) + attn
    stream_ref[...] = stream
    factor = lax.rsqrt(jnp.mean(stream * stream, axis=-1, keepdims=True) + eps)
    normed = (stream * factor * gain[...]).astype(bf16)
    for k in range(4):
        normed_ref[k] = normed


def feed_kernel(scal, n_two, c0, c1, c2, c3, w_down, ours, theirs, *refs):
    hid_a, hid_b, dgu_a, dgu_b, d_feed = refs
    core = scal[1]
    rows = c0.shape[0]
    for k, piece in enumerate((c0, c1, c2, c3)):
        d_feed[aligned((scal[0] ^ k) * rows, rows), :] = piece[...]
    part = ours.shape[1]
    half = hid_a.shape[1]
    for which, ws, hid, dgu in ((core, ours, hid_a, dgu_a), (1 - core, theirs, hid_b, dgu_b)):
        gu = 0.0
        for k in range(4):
            gu = gu + dot_nn(n_two[:, k * part : (k + 1) * part], ws[k])
        gate, up = gu[:, :half], gu[:, half:]
        d_hid = dot_nt(d_feed[...], w_down[aligned(which * half, half), :])
        sig = jax.nn.sigmoid(gate)
        act = gate * sig
        hid[...] = (act * up).astype(bf16)
        dgu[:, :half] = (d_hid * up * sig * (1.0 + gate * (1.0 - sig))).astype(bf16)
        dgu[:, half:] = (d_hid * act).astype(bf16)


def feed_back_kernel(scal, dgu_a, dgu_b, ours, theirs, out):
    part = ours.shape[1]
    for k in range(4):
        d_n = dot_nt(dgu_a[...], ours[k]) + dot_nt(dgu_b[...], theirs[k])
        out[:, k * part : (k + 1) * part] = d_n.astype(bf16)


def norm_two_kernel(scal, stream_ref, cot, gain, come, d_stream_ref, d_attn_ref, gain_ref):
    rows = stream_ref.shape[0]
    live = live_rows(scal, rows)
    d_n = block_sum(come)
    stream = stream_ref[...]
    factor = lax.rsqrt(jnp.mean(stream * stream, axis=-1, keepdims=True) + eps)
    scaled = d_n * gain[...]
    mean = jnp.mean(stream * scaled, axis=-1, keepdims=True)
    d_stream = cot[...].astype(f32) * live + factor * scaled - stream * (factor**3 * mean)
    d_stream_ref[...] = d_stream
    d_attn = (live * d_stream).astype(bf16)
    for k in range(4):
        d_attn_ref[k] = d_attn
    gain_ref[...] = jnp.sum(d_n * stream * factor, axis=0, keepdims=True)


def input_kernel(scal, tok, dq, dk, dv, dr, dl, beta, hid_a, hid_b, w_down, *refs):
    own_w, ours, theirs, (out, gain_ref) = refs[:4], refs[4:7], refs[7:10], refs[10:]
    mine, core = scal[0], scal[1]
    first = core == 0
    part = own_w[0].shape[0]
    rows = tok.shape[1]
    half = hid_a.shape[1]
    qk = jnp.concatenate([dq[...], dk[...]], 1)
    vp = jnp.concatenate([dv[...], dr[...]], 1)
    x, y = jnp.where(first, qk, vp), jnp.where(first, vp, qk)
    d_logit = jnp.concatenate([dl[h] for h in range(dl.shape[0])], 0).astype(bf16)
    factors = []
    for b in range(4):
        t = tok[b].astype(f32)
        factors.append(lax.rsqrt(jnp.mean(t * t, axis=-1, keepdims=True) + eps))
    for k in range(4):
        at = aligned((mine ^ k) * part, part)
        d_n = dot_tn(d_logit, beta[:, at].astype(bf16))
        if k == 0:
            for d, w in zip((dq, dk, dv, dr), own_w):
                d_n = d_n + dot_nt(d[...], w[:, at])
        else:
            d_n = d_n + dot_nt(x, ours[k - 1][...]) + dot_nt(y, theirs[k - 1][...])
        total = jnp.zeros((1, part), f32)
        for b in range(4):
            piece = d_n[b * rows : (b + 1) * rows]
            out[b, :rows, at] = piece.astype(bf16)
            piece = piece * tok[b, :, at].astype(f32) * factors[b]
            total = total + jnp.sum(piece, axis=0, keepdims=True)
        gain_ref[:, at] = total
        cols = slice(k * part, (k + 1) * part)
        feed = dot_nn(hid_a[...], w_down[aligned(core * half, half), cols])
        feed = feed + dot_nn(hid_b[...], w_down[aligned((1 - core) * half, half), cols])
        for b in range(4):
            out[b, rows:, cols] = feed[b * rows : (b + 1) * rows].astype(bf16)


def last_kernel(scal, tok, gain, come, d_stream, stream, grad_out, out, square_ref):
    rows = tok.shape[0]
    live = live_rows(scal, rows)
    x = tok[...].astype(f32)
    both = block_sum(come)
    d_n, feed = both[:rows], live * both[rows:]
    factor = lax.rsqrt(jnp.mean(x * x, axis=-1, keepdims=True) + eps)
    scaled = d_n * gain[...]
    mean = jnp.mean(x * scaled, axis=-1, keepdims=True)
    grad_out[...] = (d_stream[...] + factor * scaled - x * (factor**3 * mean)).astype(bf16)
    square_ref[...] = jnp.sum(feed * feed, axis=0, keepdims=True)
    out[...] = (live * stream[...] + feed).astype(bf16)


def head_grads_kernel(scal, *refs):
    ours, theirs, outs = refs[:3], refs[3:6], refs[6:]
    first = scal[1] == 0
    part, width = outs[0].shape
    for k in range(5):
        at = slice((k % 2) * part, (k % 2 + 1) * part)
        a, b = ours[k // 2][at, :], theirs[k // 2][at, :]
        low, high = jnp.where(first, a, b).astype(f32), jnp.where(first, b, a).astype(f32)
        if k == 0:
            outs[4][:, : width // 2] = low
            outs[4][:, width // 2 :] = high
        else:
            at = slice((k - 1) * part, k * part)
            outs[0][:, at] = low[:, :part]
            outs[1][:, at] = low[:, part:]
            outs[2][:, at] = high[:, :part]
            outs[3][:, at] = high[:, part:]


def ff_grads_kernel(scal, ours, theirs_low, theirs_high, gate, up):
    first = scal[1] == 0
    half = ours.shape[2] // 2
    for k in range(4):
        a, b = ours[k], (theirs_low, theirs_high)[k // 2][k % 2]
        for i, v in enumerate((jnp.where(first, a, b), jnp.where(first, b, a))):
            at = slice((2 * k + i) * half, (2 * k + i + 1) * half)
            gate[:, at] = v[:, :half].astype(f32)
            up[:, at] = v[:, half:].astype(f32)


def blocked(kernel, name, flag, *args):
    rows, width = args[0].shape
    step = max(s for s in (384, 256, 208, 200, 192, 128, 80) if rows % s == 0)
    spec = pl.BlockSpec((step, width), lambda i: (i, 0))
    return pl.pallas_call(
        kernel,
        grid=(rows // step,),
        in_specs=[pl.BlockSpec(memory_space=pltpu.SMEM)] + [spec] * len(args),
        out_specs=spec,
        out_shape=struct((rows, width), bf16),
        compiler_params=grant(),
        cost_estimate=cost(1),
        name=name,
    )(flag, *args)


def add_kernel(flag, a, b, out):
    out[...] = (a[...].astype(f32) + b[...].astype(f32)).astype(bf16)


def choose_kernel(flag, a, b, out):
    out[...] = jnp.where(flag[0] == 1, a[...], b[...])


def down_grads_kernel(scal, a0, a1, b0, b1, out):
    first = scal[1] == 0
    rows = a0.shape[0]
    for i, (a, b) in enumerate(((a0, b0), (a1, b1))):
        a, b = a[...], b[...]
        out[i * rows : (i + 1) * rows, :] = jnp.where(first, a, b).astype(f32)
        out[(i + 2) * rows : (i + 3) * rows, :] = jnp.where(first, b, a).astype(f32)


def out_kernel(scal, mixed, w_out, out):
    out[...] = dot_nn(mixed[...], w_out[...]).astype(bf16)

SHARDS = 4
CHIPS = 4


def shard_exchange(blocks):
    return lax.all_to_all(blocks, "shard", 0, 0)


def shard_gather(value):
    return shard_exchange(jnp.broadcast_to(value[None], (SHARDS,) + value.shape))


def shard_swap(value, k):
    return lax.ppermute(value, "shard", [(i, i ^ k) for i in range(SHARDS)])


def core_swap(value):
    return lax.ppermute(value, "rep", [(i, i ^ 1) for i in range(2 * CHIPS)])


def chip_send(value, pairs):
    return lax.ppermute(value, "rep", [(2 * a + c, 2 * b + c) for a, b in pairs for c in (0, 1)])


def take_rows(value, at, size):
    return lax.dynamic_slice_in_dim(value, at, size, axis=0)


def after(value, *others):
    return lax.optimization_barrier((value,) + others)[0]


def product_low(left, right, add=None):
    total = dot_tn(left, right)
    return (total if add is None else total + add.astype(f32)).astype(bf16)


class ChipSum:
    def __init__(self, hub):
        self.hub = hub.astype(jnp.int32).reshape(1)
        self.own, self.come, self.pair, self.other, self.total, self.back, self.out = (
            {} for _ in range(7)
        )

    def send(self, name, value, *deps):
        self.own[name] = value
        self.come[name] = chip_send(after(value, *deps) if deps else value, [(0, 1), (3, 2)])

    def cross(self, name, *deps):
        come = after(self.come[name], *deps) if deps else self.come[name]
        self.pair[name] = blocked(add_kernel, "pair", self.hub, self.own[name], come)
        self.other[name] = chip_send(self.pair[name], [(1, 2), (2, 1)])
        return self.pair[name]

    def give(self, name, *deps):
        other = after(self.other[name], *deps) if deps else self.other[name]
        self.total[name] = blocked(add_kernel, "total", self.hub, self.pair[name], other)
        self.back[name] = chip_send(self.total[name], [(1, 0), (2, 3)])
        return self.total[name]

    def result(self, name, *deps):
        back = after(self.back[name], *deps) if deps else self.back[name]
        self.out[name] = blocked(choose_kernel, "result", self.hub, self.total[name], back)
        return self.out[name]

    def play(self, events, tick):
        for what, name in events:
            tick = getattr(self, what)(name, tick)
        return tick


def sharded_layer(
    tokens,
    cotangent,
    lengths,
    gain_one,
    w_query,
    w_key,
    w_value,
    w_path,
    w_beta,
    w_out,
    gain_two,
    w_gate,
    w_up,
    w_down,
):
    rows, width = tokens.shape
    part = w_query.shape[0]
    head_count = w_beta.shape[1]
    heads = head_count // SHARDS
    ff_part = w_down.shape[0]
    ff_core = ff_part // 2
    seq = rows * SHARDS
    mine = lax.axis_index("shard")
    rep = lax.axis_index("rep")
    core = rep % 2
    chip = rep // 2
    first_core = core == 0
    length = lengths[0]
    scal = jnp.stack([mine, core, length]).astype(jnp.int32)
    live = (mine * rows + jnp.arange(rows) < length).astype(f32)[:, None]
    row_f = struct((rows, width), f32)
    blocks = struct((SHARDS, rows, width), bf16)
    half = width // 2
    line = struct((1, width), f32)
    wide = struct((seq, width), bf16)

    small = jnp.concatenate(
        [w_beta.T, gain_one[None], gain_two[None], jnp.zeros((2, part), bf16)], 0
    )
    extra = small.size // width
    pad = jnp.zeros((16 - extra, width), bf16)
    tok = jnp.concatenate([tokens, small.reshape(extra, width), pad], 0)
    toks = [tok] + [shard_swap(tok, k) for k in range(1, SHARDS)]
    own_w = (w_query, w_key, w_value, w_path)
    picked = whole(
        head_pick_kernel,
        "pick_heads",
        1,
        [struct((part, 2 * part), bf16)] * 3,
        scal,
        w_query,
        w_key,
        w_value,
        w_path,
    )
    heads_ours = [shard_swap(v, k) for k, v in enumerate(picked, 1)]
    heads_theirs = [core_swap(v) for v in heads_ours]

    low = struct((seq, part), bf16)
    tok, normed, queries, keyset, values, raw, logit, beta_rows, gain_a, gain_b = whole(
        project_kernel,
        "project",
        4,
        [
            blocks,
            wide,
            low,
            low,
            low,
            struct((seq, part), f32),
            struct((heads, 1, seq), f32),
            struct((heads, width), f32),
            line,
            line,
        ],
        scal,
        *toks,
        *own_w,
        *heads_ours,
        *heads_theirs,
        scratch=[pltpu.VMEM((16, width), f32)],
    )

    d_feed_own = (cotangent.astype(f32) * live).astype(bf16)
    d_feeds = [d_feed_own] + [
        shard_swap(after(d_feed_own, *toks[1:], *heads_ours), k) for k in range(1, SHARDS)
    ]
    (picked,) = whole(
        ff_pick_kernel,
        "pick_hidden",
        1,
        [struct((SHARDS, part, 2 * ff_core), bf16)],
        scal,
        w_gate,
        w_up,
    )
    ff_ours = shard_exchange(after(picked, *toks[1:], *heads_ours))
    mixed, inv, ctx, probs = attend_forward(
        scal, queries, keyset, values, raw, logit, heads
    )
    (attn_part,) = whole(
        out_kernel, "out_project", 1, [wide], scal, after(mixed, ff_ours), w_out
    )

    attn_come = shard_exchange(attn_part.reshape(SHARDS, rows, width))
    ff_theirs = core_swap(after(ff_ours, attn_part))
    stream, normed_two, attn_square = whole(
        middle_kernel,
        "residual_norm",
        1,
        [row_f, blocks, line],
        scal,
        tokens,
        gain_b,
        after(attn_come, *d_feeds[1:]),
    )
    n_two = shard_exchange(normed_two).reshape(seq, width)

    hid = struct((seq, ff_core), bf16)
    dgu = struct((seq, 2 * ff_core), bf16)
    ff_half = ff_core // 2
    hid_a, hid_b, dgu_a, dgu_b, d_feed = whole(
        feed_kernel,
        "feed",
        6,
        [hid, hid, dgu, dgu, wide],
        scal,
        n_two,
        *d_feeds,
        w_down,
        ff_ours,
        ff_theirs,
    )

    zsum = ChipSum((chip == 1) | (chip == 2))
    down_theirs = product_low(hid_b, d_feed)
    down_come = core_swap(down_theirs)
    ff_theirs_grad = product_low(n_two, after(dgu_b, down_theirs))
    ff_come = core_swap(ff_theirs_grad)
    (d_n_part,) = whole(
        feed_back_kernel,
        "feed_back",
        3,
        [wide],
        scal,
        after(dgu_a, ff_theirs_grad),
        dgu_b,
        ff_ours,
        ff_theirs,
    )
    tick = d_n_part
    for i in range(2):
        at = slice(i * (ff_core // 2), (i + 1) * (ff_core // 2))
        tick = product_low(after(hid_a, tick)[:, at], d_feed, down_come[at])
        zsum.send(f"down{i}", tick)
    for i in range(2):
        at = slice(i * 2 * part, (i + 1) * 2 * part)
        tick = product_low(n_two[:, at], after(dgu_a, tick), ff_come[at])
        zsum.send(f"ff{i}", tick)
    d_n_come = shard_exchange(after(d_n_part, tick).reshape(SHARDS, rows, width))

    d_stream, d_attn_own, part_gain_b = whole(
        norm_two_kernel,
        "norm_two_back",
        1,
        [row_f, blocks, line],
        scal,
        stream,
        cotangent,
        gain_b,
        d_n_come,
    )
    tick = zsum.play([("cross", "down0")], d_attn_own)
    d_attn = shard_exchange(after(d_attn_own, tick)).reshape(seq, width)
    tick = zsum.play([("cross", "down1")], d_attn)
    d_attn = after(d_attn, tick)

    d_mixed = dot_nt(d_attn, w_out).astype(bf16)
    d_query, d_key, d_value, d_raw, d_logit = attend_backward(
        scal, queries, keyset, values, raw, logit, inv, ctx, probs, d_mixed, heads
    )
    tick = zsum.play([("give", "down0"), ("give", "down1"), ("cross", "ff0")], d_logit)

    qk = jnp.concatenate([d_query, d_key], 1)
    vp = jnp.concatenate([d_value, d_raw], 1)
    keep = after(jnp.where(first_core, vp, qk), tick)
    p_theirs = [product_low(normed[:, i * 2 * part : (i + 1) * 2 * part], keep) for i in range(2)]
    come = [core_swap(v) for v in p_theirs]
    g_out_theirs = product_low(
        mixed, lax.dynamic_slice_in_dim(after(d_attn, *p_theirs), (1 - core) * half, half, axis=1)
    )
    g_out_come = core_swap(g_out_theirs)
    tick = zsum.play([("cross", "ff1")], g_out_theirs)
    keep = after(jnp.where(first_core, qk, vp), tick)
    grad = [
        product_low(normed[:, i * 2 * part : (i + 1) * 2 * part], keep, come[i]) for i in range(2)
    ]
    grad = jnp.concatenate(grad, 0)
    grad_home = shard_exchange(grad.reshape(SHARDS, part, 2 * part))
    last_part, part_gain_a = whole(
        input_kernel,
        "input_back",
        4,
        [struct((SHARDS, 2 * rows, width), bf16), line],
        scal,
        tok,
        d_query,
        d_key,
        d_value,
        d_raw,
        after(d_logit, grad),
        beta_rows,
        hid_a,
        hid_b,
        w_down,
        *own_w,
        *heads_ours,
        *heads_theirs,
    )
    g_out = product_low(
        mixed,
        lax.dynamic_slice_in_dim(after(d_attn, grad), core * half, half, axis=1),
        g_out_come,
    )
    tick = zsum.play([("result", "down0")], part_gain_a)
    grad_home = after(grad_home, tick)
    zsum.send("first", jnp.concatenate([g_out, grad_home[0]], 0))
    zsum.send("second", grad_home[1:3].reshape(2 * part, 2 * part))
    tick = zsum.play([("give", "ff0"), ("result", "down1")], grad_home)
    last_come = shard_exchange(after(last_part, zsum.own["first"]))
    tick = zsum.play([("give", "ff1"), ("cross", "first"), ("result", "ff0")], tick)
    input_grad, output, feed_square = whole(
        last_kernel,
        "last",
        1,
        [struct((rows, width), bf16), struct((rows, width), bf16), line],
        scal,
        tokens,
        gain_a,
        after(last_come, tick),
        d_stream,
        stream,
    )
    tick = zsum.play([("cross", "second"), ("give", "first"), ("result", "ff1")], feed_square)

    part_beta = dot_nn(d_logit[:, 0].astype(bf16), normed)
    pack = jnp.concatenate([part_beta, part_gain_a, part_gain_b], 0)
    pack = pack.reshape(heads + 2, SHARDS, part).transpose(1, 0, 2)
    own_tok = tokens.astype(f32)
    squares = jnp.stack(
        [
            jnp.sum(live * own_tok * own_tok),
            jnp.sum(attn_square),
            jnp.sum(feed_square),
            jnp.sum(live),
        ]
    )
    squares = jnp.concatenate([squares, jnp.zeros((part - 4,), f32)])
    pack = jnp.concatenate([pack, jnp.broadcast_to(squares, (SHARDS, 1, part))], 1)
    pack = shard_exchange(pack)
    pack = jnp.concatenate(
        [
            pack[:, :heads].reshape(head_count, part),
            jnp.sum(pack[:, heads:], axis=0),
            jnp.zeros((1, part), f32),
        ],
        0,
    )
    pack = pack + core_swap(pack)
    pack_hi = pack.astype(bf16)
    pack_lo = (pack - pack_hi.astype(f32)).astype(bf16)
    pack = jnp.concatenate([pack_hi, pack_lo], 1)
    zsum.send("third", jnp.concatenate([grad_home[SHARDS - 1], pack], 0))
    tick = zsum.play([("cross", "third"), ("give", "second"), ("result", "first"), ("give", "third")], tick)
    ff_sum = jnp.concatenate([zsum.out["ff0"], zsum.out["ff1"]], 0)
    ff_sum = shard_exchange(ff_sum.reshape(SHARDS, part, 2 * ff_core))
    ff_sum = after(ff_sum, tick)
    ff_other = [core_swap(ff_sum[:2]), core_swap(ff_sum[2:])]
    tick = zsum.play([("result", "second")], ff_sum)
    ff_grad = struct((part, SHARDS * ff_part), f32)
    grad_gate, grad_up = whole(
        ff_grads_kernel, "ff_grads", 4, [ff_grad] * 2, scal, ff_sum, after(ff_other[0], tick), ff_other[1]
    )
    tick = zsum.play([("result", "third")], grad_gate)
    last = zsum.out["third"]
    pack = last[part:, :part].astype(f32) + last[part:, part:].astype(f32)
    grad_beta = pack[:head_count].T
    grad_gain_a, grad_gain_b = pack[head_count], pack[head_count + 1]
    sq_input, sq_attn, sq_feed, live_total = (pack[head_count + 2, i] for i in range(4))
    denom = live_total * width

    downs = [zsum.out["down0"], zsum.out["down1"]]
    (grad_down,) = whole(
        down_grads_kernel, "down_grads", 2, [struct((ff_part, width), f32)], scal, *downs, *map(core_swap, downs)
    )
    ours = (zsum.out["first"], zsum.out["second"], last)
    theirs = [core_swap(v) for v in (zsum.out["first"], zsum.out["second"], last[:part])]
    head_grad = struct((part, width), f32)
    grad_query, grad_key, grad_value, grad_path, grad_out = whole(
        head_grads_kernel, "head_grads", 3, [head_grad] * 5, scal, *ours, *theirs
    )
    return (
        output,
        input_grad,
        grad_gain_a,
        grad_query,
        grad_key,
        grad_value,
        grad_path,
        grad_beta,
        grad_out,
        grad_gain_b,
        grad_gate,
        grad_up,
        grad_down,
        jnp.sqrt(sq_input / denom),
        jnp.sqrt(sq_attn / denom),
        jnp.sqrt(sq_feed / denom),
    )


def pick(mesh):
    def layer(*args):
        head_count, ff_part = args[8].shape[1], args[13].shape[0]
        fits = mesh.shape["shard"] == SHARDS and mesh.shape["rep"] == 2 * CHIPS
        fits = fits and head_count % SHARDS == 0 and ff_part % 256 == 0
        fits = fits and args[4].shape[1] == 128 * head_count and args[0].shape[0] == 128
        return (sharded_layer if fits else gathered_layer)(*args)

    return layer


def solution(mesh):
    return jax.shard_map(
        pick(mesh),
        mesh=mesh,
        in_specs=(
            P(("rep", "shard"), None),
            P(("rep", "shard"), None),
            P("rep"),
            P("shard"),
            P("shard", None),
            P("shard", None),
            P("shard", None),
            P("shard", None),
            P("shard", None),
            P("shard", None),
            P("shard"),
            P("shard", None),
            P("shard", None),
            P("shard", None),
        ),
        out_specs=(
            P(("rep", "shard"), None),
            P(("rep", "shard"), None),
            P("shard"),
            P("shard", None),
            P("shard", None),
            P("shard", None),
            P("shard", None),
            P("shard", None),
            P("shard", None),
            P("shard"),
            P("shard", None),
            P("shard", None),
            P("shard", None),
            P(),
            P(),
            P(),
        ),
        check_vma=False,
    )
```

```python
import functools

import jax
import jax.numpy as jnp
from jax import lax
from jax.experimental import pallas as pl
from jax.experimental.pallas import tpu as pltpu
from jax.sharding import PartitionSpec as P

f32 = jnp.float32
bf16 = jnp.bfloat16

eps = 1e-06
highest = lax.Precision.HIGHEST


def rms_norm(value, gain_vec):
    factor = lax.rsqrt(jnp.mean(value * value, axis=-1, keepdims=True) + eps)
    return value * factor * gain_vec


def unit_rows(raw):
    return raw * lax.rsqrt(jnp.sum(raw * raw, axis=-1, keepdims=True) + eps)


def rounded(value):
    return lax.optimization_barrier(value.astype(jnp.bfloat16)).astype(jnp.float32)


def round_pass(value):
    return value + lax.stop_gradient(rounded(value) - value)


def split_heads(matrix, head_count):
    return matrix.reshape(matrix.shape[0], head_count, -1).transpose(1, 0, 2)


def join_heads(matrix):
    return matrix.transpose(1, 0, 2).reshape(matrix.shape[1], -1)


def mul_low(left, right):
    return jnp.dot(left, right, preferred_element_type=jnp.float32)


def back_mul(grad_rows, weight):
    return jnp.einsum("tg,fg->tf", grad_rows, weight, preferred_element_type=jnp.float32)


def weight_grad(left, right):
    return jnp.einsum("tf,tg->fg", left, right, preferred_element_type=jnp.float32)


def masks(block_len):
    row_ids = jnp.arange(block_len)[:, None]
    col_ids = jnp.arange(block_len)[None, :]
    return (col_ids < row_ids, col_ids <= row_ids)


def block_system(direction, beta_rate):
    block_len = direction.shape[1]
    strictly, up_to = masks(block_len)
    gram = jnp.einsum("htd,hsd->hts", direction, direction, precision=highest)
    return jnp.eye(block_len, dtype=jnp.float32)[None] + jnp.where(
        strictly[None], gram * beta_rate[:, None, :], 0.0
    )


def own_context(keyset, values, direction, beta_rate):
    system = block_system(direction, beta_rate)
    strictly, up_to = masks(keyset.shape[1])
    coupled = jnp.where(
        strictly[None], jnp.einsum("htd,hjd->htj", direction, keyset, precision=highest), 0.0
    )
    solved = jax.scipy.linalg.solve_triangular(system, coupled, lower=True, unit_diagonal=True)
    scaled_dir = direction * beta_rate[:, :, None]
    key_end = keyset - jnp.einsum("htj,htd->hjd", solved, scaled_dir, precision=highest)
    through = jax.scipy.linalg.solve_triangular(system, direction, lower=True, unit_diagonal=True)
    block_map = jnp.eye(direction.shape[2], dtype=jnp.float32)[None] - jnp.einsum(
        "htm,htn->hmn", scaled_dir, through, precision=highest
    )
    return (join_heads(key_end), join_heads(values), block_map[None])


def attend(
    queries, keyset, values, direction, beta_rate, key_far, value_far, maps_far, my_block, length
):
    head_count, block_len, head_width = queries.shape
    blocks = maps_far.shape[0]
    score_scale = head_width ** (-0.5)
    strictly, up_to = masks(block_len)
    system = block_system(direction, beta_rate)
    coupled = jnp.where(
        strictly[None], jnp.einsum("htd,hjd->htj", direction, keyset, precision=highest), 0.0
    )
    solved = jax.scipy.linalg.solve_triangular(system, coupled, lower=True, unit_diagonal=True)
    crossing = (
        jnp.where(
            up_to[None], jnp.einsum("hid,htd->hit", queries, direction, precision=highest), 0.0
        )
        * beta_rate[:, None, :]
    )
    near_scores = (
        jnp.einsum("hid,hjd->hij", queries, keyset, precision=highest)
        - jnp.einsum("hit,htj->hij", crossing, solved, precision=highest)
    ) * score_scale
    back_solved = jax.scipy.linalg.solve_triangular(
        system, crossing.transpose(0, 2, 1), lower=True, trans=1, unit_diagonal=True
    )
    moved = queries - jnp.einsum("hti,htd->hid", back_solved, direction, precision=highest)

    def advance(carried, item_pair):
        block_map, index = item_pair
        updated = jnp.einsum("hid,hde->hie", carried, block_map, precision=highest)
        return (jnp.where(index < my_block, updated, carried), carried)

    unused, reached = lax.scan(advance, moved, (maps_far, jnp.arange(blocks)), reverse=True)
    far_keys = key_far.reshape(blocks, block_len, head_count, head_width)
    far_values = value_far.reshape(blocks, block_len, head_count, head_width)
    far_scores = jnp.einsum("ehid,ejhd->ehij", reached, far_keys, precision=highest) * score_scale
    positions = jnp.arange(block_len)
    near_ok = up_to[None] & ((my_block * block_len + positions)[None, None, :] < length)
    block_ids = jnp.arange(blocks)
    far_ok = (block_ids[:, None, None, None] < my_block) & (
        (block_ids[:, None] * block_len + positions[None, :])[:, None, None, :] < length
    )
    near_masked = jnp.where(near_ok, near_scores, -1e30)
    far_masked = jnp.where(far_ok, far_scores, -1e30)
    row_max = jnp.maximum(jnp.max(near_masked, axis=2), jnp.max(far_masked, axis=(0, 3)))[
        :, :, None
    ]
    row_total = jnp.sum(jnp.where(near_ok, jnp.exp(near_masked - row_max), 0.0), axis=2) + jnp.sum(
        jnp.where(far_ok, jnp.exp(far_masked - row_max[None]), 0.0), axis=(0, 3)
    )
    log_total = row_max + jnp.log(row_total)[:, :, None]
    near_probs = round_pass(jnp.where(near_ok, jnp.exp(near_masked - log_total), 0.0))
    far_probs = round_pass(jnp.where(far_ok, jnp.exp(far_masked - log_total[None]), 0.0))
    return jnp.einsum("hij,hjd->hid", near_probs, values, precision=highest) + jnp.einsum(
        "ehij,ejhd->hid", far_probs, far_values, precision=highest
    )


def gathered_layer(
    tokens,
    cotangent,
    lengths,
    gain_one,
    w_query,
    w_key,
    w_value,
    w_path,
    w_beta,
    w_out,
    gain_two,
    w_gate,
    w_up,
    w_down,
):
    gain_a, query_w, key_w, value_w, path_w, beta_w, out_w, gain_b, gate_w, up_w, down_w = (
        lax.all_gather(gain_one, "shard", axis=0, tiled=True),
        lax.all_gather(w_query, "shard", axis=0, tiled=True),
        lax.all_gather(w_key, "shard", axis=0, tiled=True),
        lax.all_gather(w_value, "shard", axis=0, tiled=True),
        lax.all_gather(w_path, "shard", axis=0, tiled=True),
        lax.all_gather(w_beta, "shard", axis=0, tiled=True),
        lax.all_gather(w_out, "shard", axis=0, tiled=True),
        lax.all_gather(gain_two, "shard", axis=0, tiled=True),
        lax.all_gather(w_gate, "shard", axis=0, tiled=True),
        lax.all_gather(w_up, "shard", axis=0, tiled=True),
        lax.all_gather(w_down, "shard", axis=0, tiled=True),
    )
    block_len = tokens.shape[0]
    width = tokens.shape[1]
    head_count = beta_w.shape[1]
    my_block = lax.axis_index("shard")
    length = lengths[0]
    live_mask = (my_block * block_len + jnp.arange(block_len) < length).astype(jnp.float32)[:, None]
    stream_in = tokens.astype(jnp.float32)
    normed_f, norm_pull = jax.vjp(rms_norm, stream_in, gain_a.astype(jnp.float32))
    normed = normed_f.astype(jnp.bfloat16)
    queries = split_heads(rounded(mul_low(normed, query_w)), head_count)
    keyset = split_heads(rounded(mul_low(normed, key_w)), head_count)
    values_h = split_heads(rounded(mul_low(normed, value_w)), head_count)
    raw = mul_low(normed, path_w).reshape(block_len, head_count, -1)
    direction_f, unit_pull = jax.vjp(unit_rows, raw)
    direction = rounded(direction_f).transpose(1, 0, 2)
    beta_rate = 2.0 * jax.nn.sigmoid(mul_low(normed, beta_w))
    (key_end, value_own, map_own), context_pull = jax.vjp(
        own_context, keyset, values_h, direction, beta_rate.T
    )
    key_far, value_far, maps_far = (
        lax.all_gather(key_end.astype(jnp.bfloat16), "shard", axis=0, tiled=True).astype(
            key_end.dtype
        ),
        lax.all_gather(value_own.astype(jnp.bfloat16), "shard", axis=0, tiled=True).astype(
            value_own.dtype
        ),
        lax.all_gather(map_own.astype(jnp.bfloat16), "shard", axis=0, tiled=True).astype(
            map_own.dtype
        ),
    )

    def local_attend(
        queries, keyset, values_h, direction, beta_heads, key_far, value_far, maps_far
    ):
        return attend(
            queries,
            keyset,
            values_h,
            direction,
            beta_heads,
            key_far,
            value_far,
            maps_far,
            my_block,
            length,
        )

    heads_out, attend_pull = jax.vjp(
        local_attend,
        queries,
        keyset,
        values_h,
        direction,
        beta_rate.T,
        key_far,
        value_far,
        maps_far,
    )
    mixed = join_heads(heads_out).astype(jnp.bfloat16)
    attn_out = mul_low(mixed, out_w)
    stream = stream_in + live_mask * attn_out
    normed_two_f, norm_two_pull = jax.vjp(rms_norm, stream, gain_b.astype(jnp.float32))
    normed_two = normed_two_f.astype(jnp.bfloat16)
    gate_pre = mul_low(normed_two, gate_w)
    up_pre = mul_low(normed_two, up_w)
    gate_sig = jax.nn.sigmoid(gate_pre)
    hidden = (gate_pre * gate_sig * up_pre).astype(jnp.bfloat16)
    feed_out = mul_low(hidden, down_w)
    output = (live_mask * (stream + feed_out)).astype(jnp.bfloat16)
    cot_rows = cotangent.astype(jnp.float32) * live_mask
    d_feed = cot_rows.astype(jnp.bfloat16)
    d_hidden = back_mul(d_feed, down_w)
    d_gate = (d_hidden * up_pre * gate_sig * (1.0 + gate_pre * (1.0 - gate_sig))).astype(
        jnp.bfloat16
    )
    d_up = (d_hidden * gate_pre * gate_sig).astype(jnp.bfloat16)
    d_normed_two = back_mul(d_gate, gate_w) + back_mul(d_up, up_w)
    d_stream_norm, grad_gain_b = norm_two_pull(d_normed_two)
    d_stream = cot_rows + d_stream_norm
    d_attn = (live_mask * d_stream).astype(jnp.bfloat16)
    d_mixed = split_heads(rounded(back_mul(d_attn, out_w)), head_count)
    (
        d_queries,
        d_keys_near,
        d_values_near,
        d_dir_near,
        d_beta_near,
        d_key_far,
        d_value_far,
        d_maps_far,
    ) = attend_pull(d_mixed)
    d_key_end, d_value_own, d_map_own = (
        lax.psum_scatter(
            d_key_far.astype(jnp.bfloat16), "shard", scatter_dimension=0, tiled=True
        ).astype(jnp.float32),
        lax.psum_scatter(
            d_value_far.astype(jnp.bfloat16), "shard", scatter_dimension=0, tiled=True
        ).astype(jnp.float32),
        lax.psum_scatter(
            d_maps_far.astype(jnp.bfloat16), "shard", scatter_dimension=0, tiled=True
        ).astype(jnp.float32),
    )
    d_keys_ctx, d_values_ctx, d_dir_ctx, d_beta_ctx = context_pull(
        (d_key_end, d_value_own, d_map_own)
    )
    d_query_b = join_heads(d_queries).astype(jnp.bfloat16)
    d_key_b = join_heads(d_keys_near + d_keys_ctx).astype(jnp.bfloat16)
    d_value_b = join_heads(d_values_near + d_values_ctx).astype(jnp.bfloat16)
    (d_raw,) = unit_pull((d_dir_near + d_dir_ctx).transpose(1, 0, 2))
    d_raw_b = d_raw.reshape(block_len, -1).astype(jnp.bfloat16)
    d_beta_total = (d_beta_near + d_beta_ctx).T
    d_logit_b = (d_beta_total * beta_rate * (1.0 - 0.5 * beta_rate)).astype(jnp.bfloat16)
    d_normed = (
        back_mul(d_query_b, query_w)
        + back_mul(d_key_b, key_w)
        + back_mul(d_value_b, value_w)
        + back_mul(d_raw_b, path_w)
        + back_mul(d_logit_b, beta_w)
    )
    d_stream_in, grad_gain_a = norm_pull(d_normed)
    input_grad = (d_stream_in + d_stream).astype(jnp.bfloat16)
    g_query = weight_grad(normed, d_query_b)
    g_key = weight_grad(normed, d_key_b)
    g_value = weight_grad(normed, d_value_b)
    g_path = weight_grad(normed, d_raw_b)
    g_beta = weight_grad(normed, d_logit_b)
    g_out = weight_grad(mixed, d_attn)
    g_gate = weight_grad(normed_two, d_gate)
    g_up = weight_grad(normed_two, d_up)
    g_down = weight_grad(hidden, d_feed)
    part_sums = (
        lax.psum_scatter(
            grad_gain_a.astype(jnp.bfloat16), "shard", scatter_dimension=0, tiled=True
        ).astype(jnp.float32),
        lax.psum_scatter(
            g_query.astype(jnp.bfloat16), "shard", scatter_dimension=0, tiled=True
        ).astype(jnp.float32),
        lax.psum_scatter(
            g_key.astype(jnp.bfloat16), "shard", scatter_dimension=0, tiled=True
        ).astype(jnp.float32),
        lax.psum_scatter(
            g_value.astype(jnp.bfloat16), "shard", scatter_dimension=0, tiled=True
        ).astype(jnp.float32),
        lax.psum_scatter(
            g_path.astype(jnp.bfloat16), "shard", scatter_dimension=0, tiled=True
        ).astype(jnp.float32),
        lax.psum_scatter(
            g_beta.astype(jnp.bfloat16), "shard", scatter_dimension=0, tiled=True
        ).astype(jnp.float32),
        lax.psum_scatter(
            g_out.astype(jnp.bfloat16), "shard", scatter_dimension=0, tiled=True
        ).astype(jnp.float32),
        lax.psum_scatter(
            grad_gain_b.astype(jnp.bfloat16), "shard", scatter_dimension=0, tiled=True
        ).astype(jnp.float32),
        lax.psum_scatter(
            g_gate.astype(jnp.bfloat16), "shard", scatter_dimension=0, tiled=True
        ).astype(jnp.float32),
        lax.psum_scatter(
            g_up.astype(jnp.bfloat16), "shard", scatter_dimension=0, tiled=True
        ).astype(jnp.float32),
        lax.psum_scatter(
            g_down.astype(jnp.bfloat16), "shard", scatter_dimension=0, tiled=True
        ).astype(jnp.float32),
    )
    owned = (
        lax.psum(part_sums[0].astype(jnp.bfloat16), "rep").astype(jnp.float32),
        lax.psum(part_sums[1].astype(jnp.bfloat16), "rep").astype(jnp.float32),
        lax.psum(part_sums[2].astype(jnp.bfloat16), "rep").astype(jnp.float32),
        lax.psum(part_sums[3].astype(jnp.bfloat16), "rep").astype(jnp.float32),
        lax.psum(part_sums[4].astype(jnp.bfloat16), "rep").astype(jnp.float32),
        lax.psum(part_sums[5].astype(jnp.bfloat16), "rep").astype(jnp.float32),
        lax.psum(part_sums[6].astype(jnp.bfloat16), "rep").astype(jnp.float32),
        lax.psum(part_sums[7].astype(jnp.bfloat16), "rep").astype(jnp.float32),
        lax.psum(part_sums[8].astype(jnp.bfloat16), "rep").astype(jnp.float32),
        lax.psum(part_sums[9].astype(jnp.bfloat16), "rep").astype(jnp.float32),
        lax.psum(part_sums[10].astype(jnp.bfloat16), "rep").astype(jnp.float32),
    )
    sq_input, sq_attn, sq_feed, live_total = lax.psum(
        (
            jnp.sum(live_mask * stream_in * stream_in),
            jnp.sum(live_mask * attn_out * attn_out),
            jnp.sum(live_mask * feed_out * feed_out),
            jnp.sum(live_mask),
        ),
        ("rep", "shard"),
    )
    denom = live_total * width
    return (
        output,
        input_grad,
        owned[0],
        owned[1],
        owned[2],
        owned[3],
        owned[4],
        owned[5],
        owned[6],
        owned[7],
        owned[8],
        owned[9],
        owned[10],
        jnp.sqrt(sq_input / denom),
        jnp.sqrt(sq_attn / denom),
        jnp.sqrt(sq_feed / denom),
    )


def dot_nn(a, b):
    return lax.dot_general(a, b, (((1,), (0,)), ((), ())), preferred_element_type=f32)


def dot_nt(a, b):
    return lax.dot_general(a, b, (((1,), (1,)), ((), ())), preferred_element_type=f32)


def dot_tn(a, b):
    return lax.dot_general(a, b, (((0,), (0,)), ((), ())), preferred_element_type=f32)


def halves(a):
    hi = a.astype(bf16)
    return hi, (a - hi.astype(f32)).astype(bf16)


def mul3(dot, a, b):
    return dot(a[0], b[0]) + (dot(a[0], b[1]) + dot(a[1], b[0]))


def mul2(dot, a, b):
    return dot(a[0], b) + dot(a[1], b)


def iota2(n, ax):
    return lax.broadcasted_iota(jnp.int32, (n, n), ax)


def tri_inverse(system, blk):
    n = system.shape[0]
    r, c = iota2(blk, 0), iota2(blk, 1)
    eye = jnp.where(r == c, 1.0, 0.0)
    tiles = [system[i * blk : (i + 1) * blk, i * blk : (i + 1) * blk] for i in range(n // blk)]
    pairs = ((r >> 1) == (c >> 1)) & ((r & 1) == 1) & ((c & 1) == 0)
    invs = [eye - jnp.where(pairs, t, 0.0) for t in tiles]
    b = 2
    while b < blk:
        m = ((r // (2 * b)) == (c // (2 * b))) & (((r // b) & 1) == 1) & (((c // b) & 1) == 0)
        new = []
        for t, v in zip(tiles, invs):
            vs = halves(v)
            low = mul3(dot_nn, halves(jnp.where(m, t, 0.0)), vs)
            new.append(v - mul3(dot_nn, vs, halves(low)))
        invs = new
        b *= 2
    size = blk
    while size < n:
        new = []
        for i in range(0, len(invs), 2):
            a, d = invs[i], invs[i + 1]
            off = system[(i + 1) * size : (i + 2) * size, i * size : (i + 1) * size]
            low = mul3(dot_nn, halves(off), halves(a))
            new.append(join(a, -mul3(dot_nn, halves(d), halves(low)), d))
        invs = new
        size *= 2
    return invs[0]


def quads(a):
    h = a.shape[0] // 2
    return a[:h, :h], a[h:, :h], a[h:, h:]


def join(a11, a21, a22):
    upper = jnp.concatenate([a11, jnp.zeros_like(a11)], 1)
    return jnp.concatenate([upper, jnp.concatenate([a21, a22], 1)], 0)


def low_nn(a, b):
    a11, a21, a22 = zip(*[quads(v) for v in a])
    b11, b21, b22 = zip(*[quads(v) for v in b])
    return join(
        mul3(dot_nn, a11, b11),
        mul3(dot_nn, a21, b11) + mul3(dot_nn, a22, b21),
        mul3(dot_nn, a22, b22),
    )


def low_nt(a, b):
    a11, a21, a22 = zip(*[quads(v) for v in a])
    b11, b21, b22 = zip(*[quads(v) for v in b])
    return join(
        mul3(dot_nt, a11, b11),
        mul3(dot_nt, a21, b11),
        mul3(dot_nt, a21, b21) + mul3(dot_nt, a22, b22),
    )


def low_tn(a, b):
    a11, a21, a22 = zip(*[quads(v) for v in a])
    b11, b21, b22 = zip(*[quads(v) for v in b])
    return join(
        mul3(dot_tn, a11, b11) + mul3(dot_tn, a21, b21),
        mul3(dot_tn, a22, b21),
        mul3(dot_tn, a22, b22),
    )


def aligned(at, size):
    return pl.ds(pl.multiple_of(at, 128), size)


def unit_factor(raw):
    return lax.rsqrt(jnp.sum(raw * raw, axis=-1, keepdims=True) + eps)


def forward_kernel(scal, q_ref, k_ref, v_ref, w_ref, b_ref, mixed_ref, inv_ref, ctx_ref, p_ref):
    length = scal[2]
    q, k, v, raw = q_ref[...], k_ref[...], v_ref[...], w_ref[...]
    w = (raw * unit_factor(raw)).astype(bf16)
    beta = 2.0 * jax.nn.sigmoid(b_ref[0])
    n = q.shape[0]
    r, c = iota2(n, 0), iota2(n, 1)
    strict, upto = c < r, c <= r
    inv = halves(tri_inverse(jnp.where(strict, dot_nt(w, w) * beta, 0.0), 128))
    ctx = halves(low_nn(inv, halves(jnp.where(strict, dot_nt(w, k), 0.0))))
    cross = jnp.where(upto, dot_nt(q, w) * beta, 0.0)
    scores = (dot_nt(q, k) - low_nn(halves(cross), ctx)) * (q.shape[1] ** -0.5)
    allowed = upto & (c < length)
    masked = jnp.where(allowed, scores, -1e30)
    top = jnp.max(masked, axis=1, keepdims=True)
    e = jnp.where(allowed, jnp.exp(masked - top), 0.0)
    log_total = top + jnp.log(jnp.sum(e, axis=1, keepdims=True))
    p = jnp.where(allowed, jnp.exp(masked - log_total), 0.0)
    mixed_ref[...] = dot_nn(p.astype(bf16), v).astype(bf16)
    for i in range(2):
        inv_ref[0, i] = inv[i]
        ctx_ref[0, i] = ctx[i]
    p_ref[0] = p


def backward_kernel(scal, *refs):
    q_ref, k_ref, v_ref, w_ref, b_ref, inv_ref, ctx_ref, p_ref, dm_ref = refs[:9]
    dq_ref, dk_ref, dv_ref, dr_ref, dl_ref = refs[9:]
    q, k, v, raw, dm = q_ref[...], k_ref[...], v_ref[...], w_ref[...], dm_ref[...]
    u = unit_factor(raw)
    w = (raw * u).astype(bf16)
    beta = 2.0 * jax.nn.sigmoid(b_ref[0])
    n = q.shape[0]
    r, c = iota2(n, 0), iota2(n, 1)
    strict, upto = c < r, c <= r
    inv = inv_ref[0, 0], inv_ref[0, 1]
    ctx = ctx_ref[0, 0], ctx_ref[0, 1]
    p = p_ref[0]
    d_v = dot_tn(p.astype(bf16), dm)
    dp = dot_nt(dm, v)
    g = p * (dp - jnp.sum(p * dp, axis=1, keepdims=True)) * (q.shape[1] ** -0.5)
    gs = halves(g)
    qw = dot_nt(q, w)
    cross = jnp.where(upto, qw * beta, 0.0)
    d_cross = jnp.where(upto, -low_nt(gs, ctx), 0.0)
    y = jnp.where(strict, -low_tn(inv, halves(low_tn(halves(cross), gs))), 0.0)
    ys = halves(y)
    d_sys = jnp.where(strict, -low_nt(ys, ctx), 0.0)
    d_beta = jnp.sum(d_cross * qw + d_sys * dot_nt(w, w), axis=0, keepdims=True)
    dx = halves(d_cross * beta)
    bm = halves(d_sys * beta)
    d_q = mul2(dot_nn, gs, k) + mul2(dot_nn, dx, w)
    d_k = mul2(dot_tn, gs, q) + mul2(dot_tn, ys, w)
    d_w = mul2(dot_tn, dx, q) + mul2(dot_nn, ys, k) + mul2(dot_nn, bm, w) + mul2(dot_tn, bm, w)
    d_raw = u * d_w - raw * (u * u * u) * jnp.sum(raw * d_w, axis=1, keepdims=True)
    for ref, val in ((dq_ref, d_q), (dk_ref, d_k), (dv_ref, d_v), (dr_ref, d_raw)):
        ref[...] = val.astype(bf16)
    dl_ref[0] = d_beta * beta * (1.0 - 0.5 * beta)


def grant():
    return pltpu.CompilerParams(vmem_limit_bytes=60 << 20)


def cost(micros):
    return pl.CostEstimate(flops=int(micros * 1e6), bytes_accessed=0, transcendentals=0)


def struct(shape, kind):
    return jax.ShapeDtypeStruct(shape, kind)


def head_specs(n, width):
    col = pl.BlockSpec((n, width), lambda h, s: (0, h))
    row = pl.BlockSpec((1, 1, n), lambda h, s: (h, 0, 0))
    pair = pl.BlockSpec((1, 2, n, n), lambda h, s: (h, 0, 0, 0))
    full = pl.BlockSpec((1, n, n), lambda h, s: (h, 0, 0))
    return col, row, pair, full


def attend_forward(scal, q, k, v, raw, logit, heads):
    n, width = q.shape[0], q.shape[1] // heads
    col, row, pair, full = head_specs(n, width)
    two = struct((heads, 2, n, n), bf16)
    return pl.pallas_call(
        forward_kernel,
        grid_spec=pltpu.PrefetchScalarGridSpec(
            num_scalar_prefetch=1,
            grid=(heads,),
            in_specs=[col] * 4 + [row],
            out_specs=[col, pair, pair, full],
        ),
        out_shape=[struct(q.shape, bf16), two, two, struct((heads, n, n), f32)],
        compiler_params=grant(),
        cost_estimate=cost(8),
        name="attend_forward",
    )(scal, q, k, v, raw, logit)


def attend_backward(scal, q, k, v, raw, logit, inv, ctx, p, dm, heads):
    n, width = q.shape[0], q.shape[1] // heads
    col, row, pair, full = head_specs(n, width)
    return pl.pallas_call(
        backward_kernel,
        grid_spec=pltpu.PrefetchScalarGridSpec(
            num_scalar_prefetch=1,
            grid=(heads,),
            in_specs=[col] * 4 + [row, pair, pair, full, col],
            out_specs=[col] * 4 + [row],
        ),
        out_shape=[struct(q.shape, bf16)] * 4 + [struct((heads, 1, n), f32)],
        compiler_params=grant(),
        cost_estimate=cost(4),
        name="attend_backward",
    )(scal, q, k, v, raw, logit, inv, ctx, p, dm)


def whole(kernel, name, micros, outs, scal, *args, scratch=()):
    vmem = pl.BlockSpec(memory_space=pltpu.VMEM)
    return pl.pallas_call(
        kernel,
        in_specs=[pl.BlockSpec(memory_space=pltpu.SMEM)] + [vmem] * len(args),
        out_specs=[vmem] * len(outs),
        out_shape=list(outs),
        scratch_shapes=list(scratch),
        compiler_params=grant(),
        cost_estimate=cost(micros),
        name=name,
    )(scal, *args)


def head_pick_kernel(scal, wq, wk, wv, wp, *outs):
    mine, first = scal[0], scal[1] == 0
    part = wq.shape[0]
    for k, out in enumerate(outs, 1):
        at = aligned((mine ^ k) * part, part)
        out[:, :part] = jnp.where(first, wq[:, at], wv[:, at])
        out[:, part:] = jnp.where(first, wk[:, at], wp[:, at])


def ff_pick_kernel(scal, wg, wu, out):
    half = out.shape[2] // 2
    for k in range(4):
        at = aligned((2 * k + scal[1]) * half, half)
        out[k, :, :half] = wg[:, at]
        out[k, :, half:] = wu[:, at]


def project_kernel(scal, *refs):
    toks, own_w, ours, theirs = refs[:4], refs[4:8], refs[8:11], refs[11:14]
    tok_ref, normed, q_ref, k_ref, v_ref, raw_ref = refs[14:20]
    logit_ref, beta_ref, gain_a, gain_b, small = refs[20:]
    mine, first = scal[0], scal[1] == 0
    part = own_w[0].shape[0]
    rows = tok_ref.shape[1]
    heads = beta_ref.shape[0]
    count = 4 * heads
    ats = [aligned((mine ^ k) * part, part) for k in range(4)]
    for k in range(4):
        lines = toks[k][rows : rows + 4, :].astype(f32)
        for r in range(count + 2):
            piece = lines[r // 4 : r // 4 + 1, (r % 4) * part : (r % 4 + 1) * part]
            small[r : r + 1, ats[k]] = piece
    gain_a[...] = small[count : count + 1, :]
    gain_b[...] = small[count + 1 : count + 2, :]
    for h in range(heads):
        beta_ref[h : h + 1, :] = small[pl.ds(mine * heads + h, 1), :]
    for b in range(4):
        tok_ref[mine ^ b] = toks[b][:rows, :]
        x = toks[b][:rows, :].astype(f32)
        factor = lax.rsqrt(jnp.mean(x * x, axis=-1, keepdims=True) + eps)
        normed[aligned((mine ^ b) * rows, rows), :] = (x * factor * gain_a[...]).astype(bf16)
    logit = dot_nt(beta_ref[...].astype(bf16), normed[...])
    for h in range(heads):
        logit_ref[h] = logit[h : h + 1]
    n_own = normed[:, ats[0]]
    sums = [dot_nn(n_own, w[:, ats[0]]) for w in own_w]
    left, right = jnp.concatenate(sums[:2], 1), jnp.concatenate(sums[2:], 1)
    a, b = jnp.where(first, left, right), jnp.where(first, right, left)
    for k in range(1, 4):
        n_k = normed[:, ats[k]]
        a = a + dot_nn(n_k, ours[k - 1][...])
        b = b + dot_nn(n_k, theirs[k - 1][...])
    qk, vp = jnp.where(first, a, b), jnp.where(first, b, a)
    q_ref[...] = qk[:, :part].astype(bf16)
    k_ref[...] = qk[:, part:].astype(bf16)
    v_ref[...] = vp[:, :part].astype(bf16)
    raw_ref[...] = vp[:, part:]


def live_rows(scal, rows):
    at = scal[0] * rows + lax.broadcasted_iota(jnp.int32, (rows, 1), 0)
    return jnp.where(at < scal[2], 1.0, 0.0)


def block_sum(ref):
    return (ref[0].astype(f32) + ref[1].astype(f32)) + (ref[2].astype(f32) + ref[3].astype(f32))


def middle_kernel(scal, tok, gain, come, stream_ref, normed_ref, square_ref):
    rows = stream_ref.shape[0]
    attn = live_rows(scal, rows) * block_sum(come)
    square_ref[...] = jnp.sum(attn * attn, axis=0, keepdims=True)
    stream = tok[...].astype(f32) + attn
    stream_ref[...] = stream
    factor = lax.rsqrt(jnp.mean(stream * stream, axis=-1, keepdims=True) + eps)
    normed = (stream * factor * gain[...]).astype(bf16)
    for k in range(4):
        normed_ref[k] = normed


def feed_kernel(scal, n_two, c0, c1, c2, c3, w_down, ours, theirs, *refs):
    hid_a, hid_b, dgu_a, dgu_b, d_feed = refs
    core = scal[1]
    rows = c0.shape[0]
    for k, piece in enumerate((c0, c1, c2, c3)):
        d_feed[aligned((scal[0] ^ k) * rows, rows), :] = piece[...]
    part = ours.shape[1]
    half = hid_a.shape[1]
    for which, ws, hid, dgu in ((core, ours, hid_a, dgu_a), (1 - core, theirs, hid_b, dgu_b)):
        gu = 0.0
        for k in range(4):
            gu = gu + dot_nn(n_two[:, k * part : (k + 1) * part], ws[k])
        gate, up = gu[:, :half], gu[:, half:]
        d_hid = dot_nt(d_feed[...], w_down[aligned(which * half, half), :])
        sig = jax.nn.sigmoid(gate)
        act = gate * sig
        hid[...] = (act * up).astype(bf16)
        dgu[:, :half] = (d_hid * up * sig * (1.0 + gate * (1.0 - sig))).astype(bf16)
        dgu[:, half:] = (d_hid * act).astype(bf16)


def feed_back_kernel(scal, dgu_a, dgu_b, ours, theirs, out):
    part = ours.shape[1]
    for k in range(4):
        d_n = dot_nt(dgu_a[...], ours[k]) + dot_nt(dgu_b[...], theirs[k])
        out[:, k * part : (k + 1) * part] = d_n.astype(bf16)


def norm_two_kernel(scal, stream_ref, cot, gain, come, d_stream_ref, d_attn_ref, gain_ref):
    rows = stream_ref.shape[0]
    live = live_rows(scal, rows)
    d_n = block_sum(come)
    stream = stream_ref[...]
    factor = lax.rsqrt(jnp.mean(stream * stream, axis=-1, keepdims=True) + eps)
    scaled = d_n * gain[...]
    mean = jnp.mean(stream * scaled, axis=-1, keepdims=True)
    d_stream = cot[...].astype(f32) * live + factor * scaled - stream * (factor**3 * mean)
    d_stream_ref[...] = d_stream
    d_attn = (live * d_stream).astype(bf16)
    for k in range(4):
        d_attn_ref[k] = d_attn
    gain_ref[...] = jnp.sum(d_n * stream * factor, axis=0, keepdims=True)


def input_kernel(scal, tok, dq, dk, dv, dr, dl, beta, hid_a, hid_b, w_down, *refs):
    own_w, ours, theirs, (out, gain_ref) = refs[:4], refs[4:7], refs[7:10], refs[10:]
    mine, core = scal[0], scal[1]
    first = core == 0
    part = own_w[0].shape[0]
    rows = tok.shape[1]
    half = hid_a.shape[1]
    qk = jnp.concatenate([dq[...], dk[...]], 1)
    vp = jnp.concatenate([dv[...], dr[...]], 1)
    x, y = jnp.where(first, qk, vp), jnp.where(first, vp, qk)
    d_logit = jnp.concatenate([dl[h] for h in range(dl.shape[0])], 0).astype(bf16)
    factors = []
    for b in range(4):
        t = tok[b].astype(f32)
        factors.append(lax.rsqrt(jnp.mean(t * t, axis=-1, keepdims=True) + eps))
    for k in range(4):
        at = aligned((mine ^ k) * part, part)
        d_n = dot_tn(d_logit, beta[:, at].astype(bf16))
        if k == 0:
            for d, w in zip((dq, dk, dv, dr), own_w):
                d_n = d_n + dot_nt(d[...], w[:, at])
        else:
            d_n = d_n + dot_nt(x, ours[k - 1][...]) + dot_nt(y, theirs[k - 1][...])
        total = jnp.zeros((1, part), f32)
        for b in range(4):
            piece = d_n[b * rows : (b + 1) * rows]
            out[b, :rows, at] = piece.astype(bf16)
            piece = piece * tok[b, :, at].astype(f32) * factors[b]
            total = total + jnp.sum(piece, axis=0, keepdims=True)
        gain_ref[:, at] = total
        cols = slice(k * part, (k + 1) * part)
        feed = dot_nn(hid_a[...], w_down[aligned(core * half, half), cols])
        feed = feed + dot_nn(hid_b[...], w_down[aligned((1 - core) * half, half), cols])
        for b in range(4):
            out[b, rows:, cols] = feed[b * rows : (b + 1) * rows].astype(bf16)


def last_kernel(scal, tok, gain, come, d_stream, stream, grad_out, out, square_ref):
    rows = tok.shape[0]
    live = live_rows(scal, rows)
    x = tok[...].astype(f32)
    both = block_sum(come)
    d_n, feed = both[:rows], live * both[rows:]
    factor = lax.rsqrt(jnp.mean(x * x, axis=-1, keepdims=True) + eps)
    scaled = d_n * gain[...]
    mean = jnp.mean(x * scaled, axis=-1, keepdims=True)
    grad_out[...] = (d_stream[...] + factor * scaled - x * (factor**3 * mean)).astype(bf16)
    square_ref[...] = jnp.sum(feed * feed, axis=0, keepdims=True)
    out[...] = (live * stream[...] + feed).astype(bf16)


def head_grads_kernel(scal, *refs):
    ours, theirs, outs = refs[:3], refs[3:6], refs[6:]
    first = scal[1] == 0
    part, width = outs[0].shape
    for k in range(5):
        at = slice((k % 2) * part, (k % 2 + 1) * part)
        a, b = ours[k // 2][at, :], theirs[k // 2][at, :]
        low, high = jnp.where(first, a, b).astype(f32), jnp.where(first, b, a).astype(f32)
        if k == 0:
            outs[4][:, : width // 2] = low
            outs[4][:, width // 2 :] = high
        else:
            at = slice((k - 1) * part, k * part)
            outs[0][:, at] = low[:, :part]
            outs[1][:, at] = low[:, part:]
            outs[2][:, at] = high[:, :part]
            outs[3][:, at] = high[:, part:]


def ff_grads_kernel(scal, ours, theirs_low, theirs_high, gate, up):
    first = scal[1] == 0
    half = ours.shape[2] // 2
    for k in range(4):
        a, b = ours[k], (theirs_low, theirs_high)[k // 2][k % 2]
        for i, v in enumerate((jnp.where(first, a, b), jnp.where(first, b, a))):
            at = slice((2 * k + i) * half, (2 * k + i + 1) * half)
            gate[:, at] = v[:, :half].astype(f32)
            up[:, at] = v[:, half:].astype(f32)


def product_kernel(a, b, c, out):
    out[...] = (dot_tn(a[...], b[...]) + c[...].astype(f32)).astype(bf16)


def product(name, left, right, add, start, size):
    step = 384
    rows, width = right.shape
    line = pl.BlockSpec((step, width), lambda i: (start // step + i, 0))
    return pl.pallas_call(
        product_kernel,
        grid=(size // step,),
        in_specs=[
            pl.BlockSpec((rows, step), lambda i: (0, start // step + i)),
            pl.BlockSpec((rows, width), lambda i: (0, 0)),
            line,
        ],
        out_specs=pl.BlockSpec((step, width), lambda i: (i, 0)),
        out_shape=struct((size, width), bf16),
        compiler_params=grant(),
        cost_estimate=cost(1),
        name=name,
    )(left, right, add)


def blocked(kernel, name, flag, *args):
    rows, width = args[0].shape
    step = max(s for s in (384, 256, 208, 200, 192, 128, 80) if rows % s == 0)
    spec = pl.BlockSpec((step, width), lambda i: (i, 0))
    return pl.pallas_call(
        kernel,
        grid=(rows // step,),
        in_specs=[pl.BlockSpec(memory_space=pltpu.SMEM)] + [spec] * len(args),
        out_specs=spec,
        out_shape=struct((rows, width), bf16),
        compiler_params=grant(),
        cost_estimate=cost(1),
        name=name,
    )(flag, *args)


def add_kernel(flag, a, b, out):
    out[...] = (a[...].astype(f32) + b[...].astype(f32)).astype(bf16)


def choose_kernel(flag, a, b, out):
    out[...] = jnp.where(flag[0] == 1, a[...], b[...])


def down_grads_kernel(scal, a0, a1, b0, b1, out):
    first = scal[1] == 0
    rows = a0.shape[0]
    for i, (a, b) in enumerate(((a0, b0), (a1, b1))):
        a, b = a[...], b[...]
        out[i * rows : (i + 1) * rows, :] = jnp.where(first, a, b).astype(f32)
        out[(i + 2) * rows : (i + 3) * rows, :] = jnp.where(first, b, a).astype(f32)


def out_kernel(scal, mixed, w_out, out):
    out[...] = dot_nn(mixed[...], w_out[...]).astype(bf16)

SHARDS = 4
CHIPS = 4


def shard_exchange(blocks):
    return lax.all_to_all(blocks, "shard", 0, 0)


def shard_gather(value):
    return shard_exchange(jnp.broadcast_to(value[None], (SHARDS,) + value.shape))


def shard_swap(value, k):
    return lax.ppermute(value, "shard", [(i, i ^ k) for i in range(SHARDS)])


def core_swap(value):
    return lax.ppermute(value, "rep", [(i, i ^ 1) for i in range(2 * CHIPS)])


def chip_send(value, pairs):
    return lax.ppermute(value, "rep", [(2 * a + c, 2 * b + c) for a, b in pairs for c in (0, 1)])


def take_rows(value, at, size):
    return lax.dynamic_slice_in_dim(value, at, size, axis=0)


def after(value, *others):
    return lax.optimization_barrier((value,) + others)[0]


def product_low(left, right, add=None):
    total = dot_tn(left, right)
    return (total if add is None else total + add.astype(f32)).astype(bf16)


class ChipSum:
    def __init__(self, hub):
        self.hub = hub.astype(jnp.int32).reshape(1)
        self.own, self.come, self.pair, self.other, self.total, self.back, self.out = (
            {} for _ in range(7)
        )

    def send(self, name, value, *deps):
        self.own[name] = value
        self.come[name] = chip_send(after(value, *deps) if deps else value, [(0, 1), (3, 2)])

    def cross(self, name, *deps):
        come = after(self.come[name], *deps) if deps else self.come[name]
        self.pair[name] = blocked(add_kernel, "pair", self.hub, self.own[name], come)
        self.other[name] = chip_send(self.pair[name], [(1, 2), (2, 1)])
        return self.pair[name]

    def give(self, name, *deps):
        other = after(self.other[name], *deps) if deps else self.other[name]
        self.total[name] = blocked(add_kernel, "total", self.hub, self.pair[name], other)
        self.back[name] = chip_send(self.total[name], [(1, 0), (2, 3)])
        return self.total[name]

    def result(self, name, *deps):
        back = after(self.back[name], *deps) if deps else self.back[name]
        self.out[name] = blocked(choose_kernel, "result", self.hub, self.total[name], back)
        return self.out[name]

    def play(self, events, tick):
        for what, name in events:
            tick = getattr(self, what)(name, tick)
        return tick


def sharded_layer(
    tokens,
    cotangent,
    lengths,
    gain_one,
    w_query,
    w_key,
    w_value,
    w_path,
    w_beta,
    w_out,
    gain_two,
    w_gate,
    w_up,
    w_down,
):
    rows, width = tokens.shape
    part = w_query.shape[0]
    head_count = w_beta.shape[1]
    heads = head_count // SHARDS
    ff_part = w_down.shape[0]
    ff_core = ff_part // 2
    seq = rows * SHARDS
    mine = lax.axis_index("shard")
    rep = lax.axis_index("rep")
    core = rep % 2
    chip = rep // 2
    first_core = core == 0
    length = lengths[0]
    scal = jnp.stack([mine, core, length]).astype(jnp.int32)
    live = (mine * rows + jnp.arange(rows) < length).astype(f32)[:, None]
    row_f = struct((rows, width), f32)
    blocks = struct((SHARDS, rows, width), bf16)
    half = width // 2
    line = struct((1, width), f32)
    wide = struct((seq, width), bf16)

    small = jnp.concatenate(
        [w_beta.T, gain_one[None], gain_two[None], jnp.zeros((2, part), bf16)], 0
    )
    extra = small.size // width
    pad = jnp.zeros((16 - extra, width), bf16)
    tok = jnp.concatenate([tokens, small.reshape(extra, width), pad], 0)
    toks = [tok] + [shard_swap(tok, k) for k in range(1, SHARDS)]
    own_w = (w_query, w_key, w_value, w_path)
    picked = whole(
        head_pick_kernel,
        "pick_heads",
        1,
        [struct((part, 2 * part), bf16)] * 3,
        scal,
        w_query,
        w_key,
        w_value,
        w_path,
    )
    heads_ours = [shard_swap(v, k) for k, v in enumerate(picked, 1)]
    heads_theirs = [core_swap(v) for v in heads_ours]

    low = struct((seq, part), bf16)
    tok, normed, queries, keyset, values, raw, logit, beta_rows, gain_a, gain_b = whole(
        project_kernel,
        "project",
        4,
        [
            blocks,
            wide,
            low,
            low,
            low,
            struct((seq, part), f32),
            struct((heads, 1, seq), f32),
            struct((heads, width), f32),
            line,
            line,
        ],
        scal,
        *toks,
        *own_w,
        *heads_ours,
        *heads_theirs,
        scratch=[pltpu.VMEM((16, width), f32)],
    )

    d_feed_own = (cotangent.astype(f32) * live).astype(bf16)
    d_feeds = [d_feed_own] + [
        shard_swap(after(d_feed_own, *toks[1:], *heads_ours), k) for k in range(1, SHARDS)
    ]
    (picked,) = whole(
        ff_pick_kernel,
        "pick_hidden",
        1,
        [struct((SHARDS, part, 2 * ff_core), bf16)],
        scal,
        w_gate,
        w_up,
    )
    ff_ours = shard_exchange(after(picked, *toks[1:], *heads_ours))
    mixed, inv, ctx, probs = attend_forward(
        scal, queries, keyset, values, raw, logit, heads
    )
    (attn_part,) = whole(
        out_kernel, "out_project", 1, [wide], scal, after(mixed, ff_ours), w_out
    )

    attn_come = shard_exchange(attn_part.reshape(SHARDS, rows, width))
    ff_theirs = core_swap(after(ff_ours, attn_part))
    stream, normed_two, attn_square = whole(
        middle_kernel,
        "residual_norm",
        1,
        [row_f, blocks, line],
        scal,
        tokens,
        gain_b,
        after(attn_come, *d_feeds[1:]),
    )
    n_two = shard_exchange(normed_two).reshape(seq, width)

    hid = struct((seq, ff_core), bf16)
    dgu = struct((seq, 2 * ff_core), bf16)
    ff_half = ff_core // 2
    hid_a, hid_b, dgu_a, dgu_b, d_feed = whole(
        feed_kernel,
        "feed",
        6,
        [hid, hid, dgu, dgu, wide],
        scal,
        n_two,
        *d_feeds,
        w_down,
        ff_ours,
        ff_theirs,
    )

    zsum = ChipSum((chip == 1) | (chip == 2))
    down_theirs = product_low(hid_b, d_feed)
    down_come = core_swap(down_theirs)
    ff_theirs_grad = product_low(n_two, after(dgu_b, down_theirs))
    ff_come = core_swap(ff_theirs_grad)
    (d_n_part,) = whole(
        feed_back_kernel,
        "feed_back",
        3,
        [wide],
        scal,
        after(dgu_a, ff_theirs_grad),
        dgu_b,
        ff_ours,
        ff_theirs,
    )
    tick = d_n_part
    for i in range(2):
        at = slice(i * (ff_core // 2), (i + 1) * (ff_core // 2))
        tick = product_low(after(hid_a, tick)[:, at], d_feed, down_come[at])
        zsum.send(f"down{i}", tick)
    for i in range(2):
        at = slice(i * 2 * part, (i + 1) * 2 * part)
        tick = product(f"ff{i}", n_two, after(dgu_a, tick), ff_come, i * 2 * part, 2 * part)
        zsum.send(f"ff{i}", tick)
    d_n_come = shard_exchange(after(d_n_part, tick).reshape(SHARDS, rows, width))

    d_stream, d_attn_own, part_gain_b = whole(
        norm_two_kernel,
        "norm_two_back",
        1,
        [row_f, blocks, line],
        scal,
        stream,
        cotangent,
        gain_b,
        d_n_come,
    )
    tick = zsum.play([("cross", "down0")], d_attn_own)
    d_attn = shard_exchange(after(d_attn_own, tick)).reshape(seq, width)

    d_mixed = dot_nt(d_attn, w_out).astype(bf16)
    d_query, d_key, d_value, d_raw, d_logit = attend_backward(
        scal, queries, keyset, values, raw, logit, inv, ctx, probs, d_mixed, heads
    )
    tick = zsum.play([("give", "down0"), ("cross", "down1"), ("cross", "ff0")], d_logit)

    qk = jnp.concatenate([d_query, d_key], 1)
    vp = jnp.concatenate([d_value, d_raw], 1)
    keep = after(jnp.where(first_core, vp, qk), tick)
    p_theirs = [product_low(normed[:, i * 2 * part : (i + 1) * 2 * part], keep) for i in range(2)]
    come = [core_swap(v) for v in p_theirs]
    g_out_theirs = product_low(
        mixed, lax.dynamic_slice_in_dim(after(d_attn, *p_theirs), (1 - core) * half, half, axis=1)
    )
    g_out_come = core_swap(g_out_theirs)
    tick = zsum.play([("give", "down1"), ("cross", "ff1")], g_out_theirs)
    keep = after(jnp.where(first_core, qk, vp), tick)
    grad = [
        product_low(normed[:, i * 2 * part : (i + 1) * 2 * part], keep, come[i]) for i in range(2)
    ]
    grad = jnp.concatenate(grad, 0)
    grad_home = shard_exchange(grad.reshape(SHARDS, part, 2 * part))
    last_part, part_gain_a = whole(
        input_kernel,
        "input_back",
        4,
        [struct((SHARDS, 2 * rows, width), bf16), line],
        scal,
        tok,
        d_query,
        d_key,
        d_value,
        d_raw,
        after(d_logit, grad),
        beta_rows,
        hid_a,
        hid_b,
        w_down,
        *own_w,
        *heads_ours,
        *heads_theirs,
    )
    g_out = product_low(
        mixed,
        lax.dynamic_slice_in_dim(after(d_attn, grad), core * half, half, axis=1),
        g_out_come,
    )
    tick = zsum.play([("result", "down0")], part_gain_a)
    grad_home = after(grad_home, tick)
    zsum.send("first", jnp.concatenate([g_out, grad_home[0]], 0))
    zsum.send("second", grad_home[1:3].reshape(2 * part, 2 * part))
    tick = zsum.play([("give", "ff0")], grad_home)
    last_come = shard_exchange(after(last_part, zsum.own["first"]))
    tick = zsum.play([("give", "ff1"), ("result", "down1"), ("cross", "first"), ("result", "ff0")], tick)
    input_grad, output, feed_square = whole(
        last_kernel,
        "last",
        1,
        [struct((rows, width), bf16), struct((rows, width), bf16), line],
        scal,
        tokens,
        gain_a,
        after(last_come, tick),
        d_stream,
        stream,
    )
    tick = zsum.play([("cross", "second"), ("give", "first"), ("result", "ff1")], feed_square)

    part_beta = dot_nn(d_logit[:, 0].astype(bf16), normed)
    pack = jnp.concatenate([part_beta, part_gain_a, part_gain_b], 0)
    pack = pack.reshape(heads + 2, SHARDS, part).transpose(1, 0, 2)
    own_tok = tokens.astype(f32)
    squares = jnp.stack(
        [
            jnp.sum(live * own_tok * own_tok),
            jnp.sum(attn_square),
            jnp.sum(feed_square),
            jnp.sum(live),
        ]
    )
    squares = jnp.concatenate([squares, jnp.zeros((part - 4,), f32)])
    pack = jnp.concatenate([pack, jnp.broadcast_to(squares, (SHARDS, 1, part))], 1)
    pack = shard_exchange(pack)
    pack = jnp.concatenate(
        [
            pack[:, :heads].reshape(head_count, part),
            jnp.sum(pack[:, heads:], axis=0),
            jnp.zeros((1, part), f32),
        ],
        0,
    )
    pack = pack + core_swap(pack)
    pack_hi = pack.astype(bf16)
    pack_lo = (pack - pack_hi.astype(f32)).astype(bf16)
    pack = jnp.concatenate([pack_hi, pack_lo], 1)
    zsum.send("third", jnp.concatenate([grad_home[SHARDS - 1], pack], 0))
    downs = [zsum.out["down0"], zsum.out["down1"]]
    others = [core_swap(v) for v in downs]
    (grad_down,) = whole(
        down_grads_kernel,
        "down_grads",
        2,
        [struct((ff_part, width), f32)],
        scal,
        after(downs[0], tick),
        downs[1],
        *others,
    )
    tick = zsum.play(
        [("cross", "third"), ("give", "second"), ("result", "first"), ("give", "third")], grad_down
    )
    ff_sum = jnp.concatenate([zsum.out["ff0"], zsum.out["ff1"]], 0)
    ff_sum = shard_exchange(ff_sum.reshape(SHARDS, part, 2 * ff_core))
    ff_sum = after(ff_sum, tick)
    ff_other = [core_swap(ff_sum[:2]), core_swap(ff_sum[2:])]
    tick = zsum.play([("result", "second")], ff_sum)
    ff_grad = struct((part, SHARDS * ff_part), f32)
    grad_gate, grad_up = whole(
        ff_grads_kernel, "ff_grads", 4, [ff_grad] * 2, scal, after(ff_sum, tick), *ff_other
    )
    tick = zsum.play([("result", "third")], grad_gate)
    last = zsum.out["third"]
    pack = last[part:, :part].astype(f32) + last[part:, part:].astype(f32)
    grad_beta = pack[:head_count].T
    grad_gain_a, grad_gain_b = pack[head_count], pack[head_count + 1]
    sq_input, sq_attn, sq_feed, live_total = (pack[head_count + 2, i] for i in range(4))
    denom = live_total * width

    ours = (zsum.out["first"], zsum.out["second"], last)
    theirs = [core_swap(v) for v in (zsum.out["first"], zsum.out["second"], last[:part])]
    head_grad = struct((part, width), f32)
    grad_query, grad_key, grad_value, grad_path, grad_out = whole(
        head_grads_kernel, "head_grads", 3, [head_grad] * 5, scal, *ours, *theirs
    )
    return (
        output,
        input_grad,
        grad_gain_a,
        grad_query,
        grad_key,
        grad_value,
        grad_path,
        grad_beta,
        grad_out,
        grad_gain_b,
        grad_gate,
        grad_up,
        grad_down,
        jnp.sqrt(sq_input / denom),
        jnp.sqrt(sq_attn / denom),
        jnp.sqrt(sq_feed / denom),
    )


def pick(mesh):
    def layer(*args):
        head_count, ff_part = args[8].shape[1], args[13].shape[0]
        fits = mesh.shape["shard"] == SHARDS and mesh.shape["rep"] == 2 * CHIPS
        fits = fits and head_count % SHARDS == 0 and ff_part % 256 == 0
        fits = fits and args[4].shape[1] == 128 * head_count and args[0].shape[0] == 128
        return (sharded_layer if fits else gathered_layer)(*args)

    return layer


def solution(mesh):
    return jax.shard_map(
        pick(mesh),
        mesh=mesh,
        in_specs=(
            P(("rep", "shard"), None),
            P(("rep", "shard"), None),
            P("rep"),
            P("shard"),
            P("shard", None),
            P("shard", None),
            P("shard", None),
            P("shard", None),
            P("shard", None),
            P("shard", None),
            P("shard"),
            P("shard", None),
            P("shard", None),
            P("shard", None),
        ),
        out_specs=(
            P(("rep", "shard"), None),
            P(("rep", "shard"), None),
            P("shard"),
            P("shard", None),
            P("shard", None),
            P("shard", None),
            P("shard", None),
            P("shard", None),
            P("shard", None),
            P("shard"),
            P("shard", None),
            P("shard", None),
            P("shard", None),
            P(),
            P(),
            P(),
        ),
        check_vma=False,
    )
```

```python
import functools

import jax
import jax.numpy as jnp
from jax import lax
from jax.experimental import pallas as pl
from jax.experimental.pallas import tpu as pltpu
from jax.sharding import PartitionSpec as P

f32 = jnp.float32
bf16 = jnp.bfloat16

eps = 1e-06
highest = lax.Precision.HIGHEST


def rms_norm(value, gain_vec):
    factor = lax.rsqrt(jnp.mean(value * value, axis=-1, keepdims=True) + eps)
    return value * factor * gain_vec


def unit_rows(raw):
    return raw * lax.rsqrt(jnp.sum(raw * raw, axis=-1, keepdims=True) + eps)


def rounded(value):
    return lax.optimization_barrier(value.astype(jnp.bfloat16)).astype(jnp.float32)


def round_pass(value):
    return value + lax.stop_gradient(rounded(value) - value)


def split_heads(matrix, head_count):
    return matrix.reshape(matrix.shape[0], head_count, -1).transpose(1, 0, 2)


def join_heads(matrix):
    return matrix.transpose(1, 0, 2).reshape(matrix.shape[1], -1)


def mul_low(left, right):
    return jnp.dot(left, right, preferred_element_type=jnp.float32)


def back_mul(grad_rows, weight):
    return jnp.einsum("tg,fg->tf", grad_rows, weight, preferred_element_type=jnp.float32)


def weight_grad(left, right):
    return jnp.einsum("tf,tg->fg", left, right, preferred_element_type=jnp.float32)


def masks(block_len):
    row_ids = jnp.arange(block_len)[:, None]
    col_ids = jnp.arange(block_len)[None, :]
    return (col_ids < row_ids, col_ids <= row_ids)


def block_system(direction, beta_rate):
    block_len = direction.shape[1]
    strictly, up_to = masks(block_len)
    gram = jnp.einsum("htd,hsd->hts", direction, direction, precision=highest)
    return jnp.eye(block_len, dtype=jnp.float32)[None] + jnp.where(
        strictly[None], gram * beta_rate[:, None, :], 0.0
    )


def own_context(keyset, values, direction, beta_rate):
    system = block_system(direction, beta_rate)
    strictly, up_to = masks(keyset.shape[1])
    coupled = jnp.where(
        strictly[None], jnp.einsum("htd,hjd->htj", direction, keyset, precision=highest), 0.0
    )
    solved = jax.scipy.linalg.solve_triangular(system, coupled, lower=True, unit_diagonal=True)
    scaled_dir = direction * beta_rate[:, :, None]
    key_end = keyset - jnp.einsum("htj,htd->hjd", solved, scaled_dir, precision=highest)
    through = jax.scipy.linalg.solve_triangular(system, direction, lower=True, unit_diagonal=True)
    block_map = jnp.eye(direction.shape[2], dtype=jnp.float32)[None] - jnp.einsum(
        "htm,htn->hmn", scaled_dir, through, precision=highest
    )
    return (join_heads(key_end), join_heads(values), block_map[None])


def attend(
    queries, keyset, values, direction, beta_rate, key_far, value_far, maps_far, my_block, length
):
    head_count, block_len, head_width = queries.shape
    blocks = maps_far.shape[0]
    score_scale = head_width ** (-0.5)
    strictly, up_to = masks(block_len)
    system = block_system(direction, beta_rate)
    coupled = jnp.where(
        strictly[None], jnp.einsum("htd,hjd->htj", direction, keyset, precision=highest), 0.0
    )
    solved = jax.scipy.linalg.solve_triangular(system, coupled, lower=True, unit_diagonal=True)
    crossing = (
        jnp.where(
            up_to[None], jnp.einsum("hid,htd->hit", queries, direction, precision=highest), 0.0
        )
        * beta_rate[:, None, :]
    )
    near_scores = (
        jnp.einsum("hid,hjd->hij", queries, keyset, precision=highest)
        - jnp.einsum("hit,htj->hij", crossing, solved, precision=highest)
    ) * score_scale
    back_solved = jax.scipy.linalg.solve_triangular(
        system, crossing.transpose(0, 2, 1), lower=True, trans=1, unit_diagonal=True
    )
    moved = queries - jnp.einsum("hti,htd->hid", back_solved, direction, precision=highest)

    def advance(carried, item_pair):
        block_map, index = item_pair
        updated = jnp.einsum("hid,hde->hie", carried, block_map, precision=highest)
        return (jnp.where(index < my_block, updated, carried), carried)

    unused, reached = lax.scan(advance, moved, (maps_far, jnp.arange(blocks)), reverse=True)
    far_keys = key_far.reshape(blocks, block_len, head_count, head_width)
    far_values = value_far.reshape(blocks, block_len, head_count, head_width)
    far_scores = jnp.einsum("ehid,ejhd->ehij", reached, far_keys, precision=highest) * score_scale
    positions = jnp.arange(block_len)
    near_ok = up_to[None] & ((my_block * block_len + positions)[None, None, :] < length)
    block_ids = jnp.arange(blocks)
    far_ok = (block_ids[:, None, None, None] < my_block) & (
        (block_ids[:, None] * block_len + positions[None, :])[:, None, None, :] < length
    )
    near_masked = jnp.where(near_ok, near_scores, -1e30)
    far_masked = jnp.where(far_ok, far_scores, -1e30)
    row_max = jnp.maximum(jnp.max(near_masked, axis=2), jnp.max(far_masked, axis=(0, 3)))[
        :, :, None
    ]
    row_total = jnp.sum(jnp.where(near_ok, jnp.exp(near_masked - row_max), 0.0), axis=2) + jnp.sum(
        jnp.where(far_ok, jnp.exp(far_masked - row_max[None]), 0.0), axis=(0, 3)
    )
    log_total = row_max + jnp.log(row_total)[:, :, None]
    near_probs = round_pass(jnp.where(near_ok, jnp.exp(near_masked - log_total), 0.0))
    far_probs = round_pass(jnp.where(far_ok, jnp.exp(far_masked - log_total[None]), 0.0))
    return jnp.einsum("hij,hjd->hid", near_probs, values, precision=highest) + jnp.einsum(
        "ehij,ejhd->hid", far_probs, far_values, precision=highest
    )


def gathered_layer(
    tokens,
    cotangent,
    lengths,
    gain_one,
    w_query,
    w_key,
    w_value,
    w_path,
    w_beta,
    w_out,
    gain_two,
    w_gate,
    w_up,
    w_down,
):
    gain_a, query_w, key_w, value_w, path_w, beta_w, out_w, gain_b, gate_w, up_w, down_w = (
        lax.all_gather(gain_one, "shard", axis=0, tiled=True),
        lax.all_gather(w_query, "shard", axis=0, tiled=True),
        lax.all_gather(w_key, "shard", axis=0, tiled=True),
        lax.all_gather(w_value, "shard", axis=0, tiled=True),
        lax.all_gather(w_path, "shard", axis=0, tiled=True),
        lax.all_gather(w_beta, "shard", axis=0, tiled=True),
        lax.all_gather(w_out, "shard", axis=0, tiled=True),
        lax.all_gather(gain_two, "shard", axis=0, tiled=True),
        lax.all_gather(w_gate, "shard", axis=0, tiled=True),
        lax.all_gather(w_up, "shard", axis=0, tiled=True),
        lax.all_gather(w_down, "shard", axis=0, tiled=True),
    )
    block_len = tokens.shape[0]
    width = tokens.shape[1]
    head_count = beta_w.shape[1]
    my_block = lax.axis_index("shard")
    length = lengths[0]
    live_mask = (my_block * block_len + jnp.arange(block_len) < length).astype(jnp.float32)[:, None]
    stream_in = tokens.astype(jnp.float32)
    normed_f, norm_pull = jax.vjp(rms_norm, stream_in, gain_a.astype(jnp.float32))
    normed = normed_f.astype(jnp.bfloat16)
    queries = split_heads(rounded(mul_low(normed, query_w)), head_count)
    keyset = split_heads(rounded(mul_low(normed, key_w)), head_count)
    values_h = split_heads(rounded(mul_low(normed, value_w)), head_count)
    raw = mul_low(normed, path_w).reshape(block_len, head_count, -1)
    direction_f, unit_pull = jax.vjp(unit_rows, raw)
    direction = rounded(direction_f).transpose(1, 0, 2)
    beta_rate = 2.0 * jax.nn.sigmoid(mul_low(normed, beta_w))
    (key_end, value_own, map_own), context_pull = jax.vjp(
        own_context, keyset, values_h, direction, beta_rate.T
    )
    key_far, value_far, maps_far = (
        lax.all_gather(key_end.astype(jnp.bfloat16), "shard", axis=0, tiled=True).astype(
            key_end.dtype
        ),
        lax.all_gather(value_own.astype(jnp.bfloat16), "shard", axis=0, tiled=True).astype(
            value_own.dtype
        ),
        lax.all_gather(map_own.astype(jnp.bfloat16), "shard", axis=0, tiled=True).astype(
            map_own.dtype
        ),
    )

    def local_attend(
        queries, keyset, values_h, direction, beta_heads, key_far, value_far, maps_far
    ):
        return attend(
            queries,
            keyset,
            values_h,
            direction,
            beta_heads,
            key_far,
            value_far,
            maps_far,
            my_block,
            length,
        )

    heads_out, attend_pull = jax.vjp(
        local_attend,
        queries,
        keyset,
        values_h,
        direction,
        beta_rate.T,
        key_far,
        value_far,
        maps_far,
    )
    mixed = join_heads(heads_out).astype(jnp.bfloat16)
    attn_out = mul_low(mixed, out_w)
    stream = stream_in + live_mask * attn_out
    normed_two_f, norm_two_pull = jax.vjp(rms_norm, stream, gain_b.astype(jnp.float32))
    normed_two = normed_two_f.astype(jnp.bfloat16)
    gate_pre = mul_low(normed_two, gate_w)
    up_pre = mul_low(normed_two, up_w)
    gate_sig = jax.nn.sigmoid(gate_pre)
    hidden = (gate_pre * gate_sig * up_pre).astype(jnp.bfloat16)
    feed_out = mul_low(hidden, down_w)
    output = (live_mask * (stream + feed_out)).astype(jnp.bfloat16)
    cot_rows = cotangent.astype(jnp.float32) * live_mask
    d_feed = cot_rows.astype(jnp.bfloat16)
    d_hidden = back_mul(d_feed, down_w)
    d_gate = (d_hidden * up_pre * gate_sig * (1.0 + gate_pre * (1.0 - gate_sig))).astype(
        jnp.bfloat16
    )
    d_up = (d_hidden * gate_pre * gate_sig).astype(jnp.bfloat16)
    d_normed_two = back_mul(d_gate, gate_w) + back_mul(d_up, up_w)
    d_stream_norm, grad_gain_b = norm_two_pull(d_normed_two)
    d_stream = cot_rows + d_stream_norm
    d_attn = (live_mask * d_stream).astype(jnp.bfloat16)
    d_mixed = split_heads(rounded(back_mul(d_attn, out_w)), head_count)
    (
        d_queries,
        d_keys_near,
        d_values_near,
        d_dir_near,
        d_beta_near,
        d_key_far,
        d_value_far,
        d_maps_far,
    ) = attend_pull(d_mixed)
    d_key_end, d_value_own, d_map_own = (
        lax.psum_scatter(
            d_key_far.astype(jnp.bfloat16), "shard", scatter_dimension=0, tiled=True
        ).astype(jnp.float32),
        lax.psum_scatter(
            d_value_far.astype(jnp.bfloat16), "shard", scatter_dimension=0, tiled=True
        ).astype(jnp.float32),
        lax.psum_scatter(
            d_maps_far.astype(jnp.bfloat16), "shard", scatter_dimension=0, tiled=True
        ).astype(jnp.float32),
    )
    d_keys_ctx, d_values_ctx, d_dir_ctx, d_beta_ctx = context_pull(
        (d_key_end, d_value_own, d_map_own)
    )
    d_query_b = join_heads(d_queries).astype(jnp.bfloat16)
    d_key_b = join_heads(d_keys_near + d_keys_ctx).astype(jnp.bfloat16)
    d_value_b = join_heads(d_values_near + d_values_ctx).astype(jnp.bfloat16)
    (d_raw,) = unit_pull((d_dir_near + d_dir_ctx).transpose(1, 0, 2))
    d_raw_b = d_raw.reshape(block_len, -1).astype(jnp.bfloat16)
    d_beta_total = (d_beta_near + d_beta_ctx).T
    d_logit_b = (d_beta_total * beta_rate * (1.0 - 0.5 * beta_rate)).astype(jnp.bfloat16)
    d_normed = (
        back_mul(d_query_b, query_w)
        + back_mul(d_key_b, key_w)
        + back_mul(d_value_b, value_w)
        + back_mul(d_raw_b, path_w)
        + back_mul(d_logit_b, beta_w)
    )
    d_stream_in, grad_gain_a = norm_pull(d_normed)
    input_grad = (d_stream_in + d_stream).astype(jnp.bfloat16)
    g_query = weight_grad(normed, d_query_b)
    g_key = weight_grad(normed, d_key_b)
    g_value = weight_grad(normed, d_value_b)
    g_path = weight_grad(normed, d_raw_b)
    g_beta = weight_grad(normed, d_logit_b)
    g_out = weight_grad(mixed, d_attn)
    g_gate = weight_grad(normed_two, d_gate)
    g_up = weight_grad(normed_two, d_up)
    g_down = weight_grad(hidden, d_feed)
    part_sums = (
        lax.psum_scatter(
            grad_gain_a.astype(jnp.bfloat16), "shard", scatter_dimension=0, tiled=True
        ).astype(jnp.float32),
        lax.psum_scatter(
            g_query.astype(jnp.bfloat16), "shard", scatter_dimension=0, tiled=True
        ).astype(jnp.float32),
        lax.psum_scatter(
            g_key.astype(jnp.bfloat16), "shard", scatter_dimension=0, tiled=True
        ).astype(jnp.float32),
        lax.psum_scatter(
            g_value.astype(jnp.bfloat16), "shard", scatter_dimension=0, tiled=True
        ).astype(jnp.float32),
        lax.psum_scatter(
            g_path.astype(jnp.bfloat16), "shard", scatter_dimension=0, tiled=True
        ).astype(jnp.float32),
        lax.psum_scatter(
            g_beta.astype(jnp.bfloat16), "shard", scatter_dimension=0, tiled=True
        ).astype(jnp.float32),
        lax.psum_scatter(
            g_out.astype(jnp.bfloat16), "shard", scatter_dimension=0, tiled=True
        ).astype(jnp.float32),
        lax.psum_scatter(
            grad_gain_b.astype(jnp.bfloat16), "shard", scatter_dimension=0, tiled=True
        ).astype(jnp.float32),
        lax.psum_scatter(
            g_gate.astype(jnp.bfloat16), "shard", scatter_dimension=0, tiled=True
        ).astype(jnp.float32),
        lax.psum_scatter(
            g_up.astype(jnp.bfloat16), "shard", scatter_dimension=0, tiled=True
        ).astype(jnp.float32),
        lax.psum_scatter(
            g_down.astype(jnp.bfloat16), "shard", scatter_dimension=0, tiled=True
        ).astype(jnp.float32),
    )
    owned = (
        lax.psum(part_sums[0].astype(jnp.bfloat16), "rep").astype(jnp.float32),
        lax.psum(part_sums[1].astype(jnp.bfloat16), "rep").astype(jnp.float32),
        lax.psum(part_sums[2].astype(jnp.bfloat16), "rep").astype(jnp.float32),
        lax.psum(part_sums[3].astype(jnp.bfloat16), "rep").astype(jnp.float32),
        lax.psum(part_sums[4].astype(jnp.bfloat16), "rep").astype(jnp.float32),
        lax.psum(part_sums[5].astype(jnp.bfloat16), "rep").astype(jnp.float32),
        lax.psum(part_sums[6].astype(jnp.bfloat16), "rep").astype(jnp.float32),
        lax.psum(part_sums[7].astype(jnp.bfloat16), "rep").astype(jnp.float32),
        lax.psum(part_sums[8].astype(jnp.bfloat16), "rep").astype(jnp.float32),
        lax.psum(part_sums[9].astype(jnp.bfloat16), "rep").astype(jnp.float32),
        lax.psum(part_sums[10].astype(jnp.bfloat16), "rep").astype(jnp.float32),
    )
    sq_input, sq_attn, sq_feed, live_total = lax.psum(
        (
            jnp.sum(live_mask * stream_in * stream_in),
            jnp.sum(live_mask * attn_out * attn_out),
            jnp.sum(live_mask * feed_out * feed_out),
            jnp.sum(live_mask),
        ),
        ("rep", "shard"),
    )
    denom = live_total * width
    return (
        output,
        input_grad,
        owned[0],
        owned[1],
        owned[2],
        owned[3],
        owned[4],
        owned[5],
        owned[6],
        owned[7],
        owned[8],
        owned[9],
        owned[10],
        jnp.sqrt(sq_input / denom),
        jnp.sqrt(sq_attn / denom),
        jnp.sqrt(sq_feed / denom),
    )


def dot_nn(a, b):
    return lax.dot_general(a, b, (((1,), (0,)), ((), ())), preferred_element_type=f32)


def dot_nt(a, b):
    return lax.dot_general(a, b, (((1,), (1,)), ((), ())), preferred_element_type=f32)


def dot_tn(a, b):
    return lax.dot_general(a, b, (((0,), (0,)), ((), ())), preferred_element_type=f32)


def halves(a):
    hi = a.astype(bf16)
    return hi, (a - hi.astype(f32)).astype(bf16)


def mul3(dot, a, b):
    return dot(a[0], b[0]) + (dot(a[0], b[1]) + dot(a[1], b[0]))


def mul2(dot, a, b):
    return dot(a[0], b) + dot(a[1], b)


def iota2(n, ax):
    return lax.broadcasted_iota(jnp.int32, (n, n), ax)


def tri_inverse(system, blk):
    n = system.shape[0]
    r, c = iota2(blk, 0), iota2(blk, 1)
    eye = jnp.where(r == c, 1.0, 0.0)
    tiles = [system[i * blk : (i + 1) * blk, i * blk : (i + 1) * blk] for i in range(n // blk)]
    pairs = ((r >> 1) == (c >> 1)) & ((r & 1) == 1) & ((c & 1) == 0)
    invs = [eye - jnp.where(pairs, t, 0.0) for t in tiles]
    b = 2
    while b < blk:
        m = ((r // (2 * b)) == (c // (2 * b))) & (((r // b) & 1) == 1) & (((c // b) & 1) == 0)
        new = []
        for t, v in zip(tiles, invs):
            vs = halves(v)
            low = mul3(dot_nn, halves(jnp.where(m, t, 0.0)), vs)
            new.append(v - mul3(dot_nn, vs, halves(low)))
        invs = new
        b *= 2
    size = blk
    while size < n:
        new = []
        for i in range(0, len(invs), 2):
            a, d = invs[i], invs[i + 1]
            off = system[(i + 1) * size : (i + 2) * size, i * size : (i + 1) * size]
            low = mul3(dot_nn, halves(off), halves(a))
            new.append(join(a, -mul3(dot_nn, halves(d), halves(low)), d))
        invs = new
        size *= 2
    return invs[0]


def quads(a):
    h = a.shape[0] // 2
    return a[:h, :h], a[h:, :h], a[h:, h:]


def join(a11, a21, a22):
    upper = jnp.concatenate([a11, jnp.zeros_like(a11)], 1)
    return jnp.concatenate([upper, jnp.concatenate([a21, a22], 1)], 0)


def low_nn(a, b):
    a11, a21, a22 = zip(*[quads(v) for v in a])
    b11, b21, b22 = zip(*[quads(v) for v in b])
    return join(
        mul3(dot_nn, a11, b11),
        mul3(dot_nn, a21, b11) + mul3(dot_nn, a22, b21),
        mul3(dot_nn, a22, b22),
    )


def low_nt(a, b):
    a11, a21, a22 = zip(*[quads(v) for v in a])
    b11, b21, b22 = zip(*[quads(v) for v in b])
    return join(
        mul3(dot_nt, a11, b11),
        mul3(dot_nt, a21, b11),
        mul3(dot_nt, a21, b21) + mul3(dot_nt, a22, b22),
    )


def low_tn(a, b):
    a11, a21, a22 = zip(*[quads(v) for v in a])
    b11, b21, b22 = zip(*[quads(v) for v in b])
    return join(
        mul3(dot_tn, a11, b11) + mul3(dot_tn, a21, b21),
        mul3(dot_tn, a22, b21),
        mul3(dot_tn, a22, b22),
    )


def aligned(at, size):
    return pl.ds(pl.multiple_of(at, 128), size)


def unit_factor(raw):
    return lax.rsqrt(jnp.sum(raw * raw, axis=-1, keepdims=True) + eps)


def forward_kernel(scal, q_ref, k_ref, v_ref, w_ref, b_ref, mixed_ref, inv_ref, ctx_ref, p_ref):
    length = scal[2]
    q, k, v, raw = q_ref[...], k_ref[...], v_ref[...], w_ref[...]
    w = (raw * unit_factor(raw)).astype(bf16)
    beta = 2.0 * jax.nn.sigmoid(b_ref[0])
    n = q.shape[0]
    r, c = iota2(n, 0), iota2(n, 1)
    strict, upto = c < r, c <= r
    inv = halves(tri_inverse(jnp.where(strict, dot_nt(w, w) * beta, 0.0), 128))
    ctx = halves(low_nn(inv, halves(jnp.where(strict, dot_nt(w, k), 0.0))))
    cross = jnp.where(upto, dot_nt(q, w) * beta, 0.0)
    scores = (dot_nt(q, k) - low_nn(halves(cross), ctx)) * (q.shape[1] ** -0.5)
    allowed = upto & (c < length)
    masked = jnp.where(allowed, scores, -1e30)
    top = jnp.max(masked, axis=1, keepdims=True)
    e = jnp.where(allowed, jnp.exp(masked - top), 0.0)
    log_total = top + jnp.log(jnp.sum(e, axis=1, keepdims=True))
    p = jnp.where(allowed, jnp.exp(masked - log_total), 0.0)
    mixed_ref[...] = dot_nn(p.astype(bf16), v).astype(bf16)
    for i in range(2):
        inv_ref[0, i] = inv[i]
        ctx_ref[0, i] = ctx[i]
    p_ref[0] = p


def backward_kernel(scal, *refs):
    q_ref, k_ref, v_ref, w_ref, b_ref, inv_ref, ctx_ref, p_ref, dm_ref = refs[:9]
    dq_ref, dk_ref, dv_ref, dr_ref, dl_ref = refs[9:]
    q, k, v, raw, dm = q_ref[...], k_ref[...], v_ref[...], w_ref[...], dm_ref[...]
    u = unit_factor(raw)
    w = (raw * u).astype(bf16)
    beta = 2.0 * jax.nn.sigmoid(b_ref[0])
    n = q.shape[0]
    r, c = iota2(n, 0), iota2(n, 1)
    strict, upto = c < r, c <= r
    inv = inv_ref[0, 0], inv_ref[0, 1]
    ctx = ctx_ref[0, 0], ctx_ref[0, 1]
    p = p_ref[0]
    d_v = dot_tn(p.astype(bf16), dm)
    dp = dot_nt(dm, v)
    g = p * (dp - jnp.sum(p * dp, axis=1, keepdims=True)) * (q.shape[1] ** -0.5)
    gs = halves(g)
    qw = dot_nt(q, w)
    cross = jnp.where(upto, qw * beta, 0.0)
    d_cross = jnp.where(upto, -low_nt(gs, ctx), 0.0)
    y = jnp.where(strict, -low_tn(inv, halves(low_tn(halves(cross), gs))), 0.0)
    ys = halves(y)
    d_sys = jnp.where(strict, -low_nt(ys, ctx), 0.0)
    d_beta = jnp.sum(d_cross * qw + d_sys * dot_nt(w, w), axis=0, keepdims=True)
    dx = halves(d_cross * beta)
    bm = halves(d_sys * beta)
    d_q = mul2(dot_nn, gs, k) + mul2(dot_nn, dx, w)
    d_k = mul2(dot_tn, gs, q) + mul2(dot_tn, ys, w)
    d_w = mul2(dot_tn, dx, q) + mul2(dot_nn, ys, k) + mul2(dot_nn, bm, w) + mul2(dot_tn, bm, w)
    d_raw = u * d_w - raw * (u * u * u) * jnp.sum(raw * d_w, axis=1, keepdims=True)
    for ref, val in ((dq_ref, d_q), (dk_ref, d_k), (dv_ref, d_v), (dr_ref, d_raw)):
        ref[...] = val.astype(bf16)
    dl_ref[0] = d_beta * beta * (1.0 - 0.5 * beta)


def grant():
    return pltpu.CompilerParams(vmem_limit_bytes=60 << 20)


def cost(micros):
    return pl.CostEstimate(flops=int(micros * 1e6), bytes_accessed=0, transcendentals=0)


def struct(shape, kind):
    return jax.ShapeDtypeStruct(shape, kind)


def head_specs(n, width):
    col = pl.BlockSpec((n, width), lambda h, s: (0, h))
    row = pl.BlockSpec((1, 1, n), lambda h, s: (h, 0, 0))
    pair = pl.BlockSpec((1, 2, n, n), lambda h, s: (h, 0, 0, 0))
    full = pl.BlockSpec((1, n, n), lambda h, s: (h, 0, 0))
    return col, row, pair, full


def attend_forward(scal, q, k, v, raw, logit, heads):
    n, width = q.shape[0], q.shape[1] // heads
    col, row, pair, full = head_specs(n, width)
    two = struct((heads, 2, n, n), bf16)
    return pl.pallas_call(
        forward_kernel,
        grid_spec=pltpu.PrefetchScalarGridSpec(
            num_scalar_prefetch=1,
            grid=(heads,),
            in_specs=[col] * 4 + [row],
            out_specs=[col, pair, pair, full],
        ),
        out_shape=[struct(q.shape, bf16), two, two, struct((heads, n, n), f32)],
        compiler_params=grant(),
        cost_estimate=cost(8),
        name="attend_forward",
    )(scal, q, k, v, raw, logit)


def attend_backward(scal, q, k, v, raw, logit, inv, ctx, p, dm, heads):
    n, width = q.shape[0], q.shape[1] // heads
    col, row, pair, full = head_specs(n, width)
    return pl.pallas_call(
        backward_kernel,
        grid_spec=pltpu.PrefetchScalarGridSpec(
            num_scalar_prefetch=1,
            grid=(heads,),
            in_specs=[col] * 4 + [row, pair, pair, full, col],
            out_specs=[col] * 4 + [row],
        ),
        out_shape=[struct(q.shape, bf16)] * 4 + [struct((heads, 1, n), f32)],
        compiler_params=grant(),
        cost_estimate=cost(4),
        name="attend_backward",
    )(scal, q, k, v, raw, logit, inv, ctx, p, dm)


def whole(kernel, name, micros, outs, scal, *args, scratch=()):
    vmem = pl.BlockSpec(memory_space=pltpu.VMEM)
    return pl.pallas_call(
        kernel,
        in_specs=[pl.BlockSpec(memory_space=pltpu.SMEM)] + [vmem] * len(args),
        out_specs=[vmem] * len(outs),
        out_shape=list(outs),
        scratch_shapes=list(scratch),
        compiler_params=grant(),
        cost_estimate=cost(micros),
        name=name,
    )(scal, *args)


def head_pick_kernel(scal, wq, wk, wv, wp, *outs):
    mine, first = scal[0], scal[1] == 0
    part = wq.shape[0]
    for k, out in enumerate(outs, 1):
        at = aligned((mine ^ k) * part, part)
        out[:, :part] = jnp.where(first, wq[:, at], wv[:, at])
        out[:, part:] = jnp.where(first, wk[:, at], wp[:, at])


def ff_pick_kernel(scal, wg, wu, out):
    half = out.shape[2] // 2
    for k in range(4):
        at = aligned((2 * k + scal[1]) * half, half)
        out[k, :, :half] = wg[:, at]
        out[k, :, half:] = wu[:, at]


def project_kernel(scal, *refs):
    toks, own_w, ours, theirs = refs[:4], refs[4:8], refs[8:11], refs[11:14]
    tok_ref, normed, q_ref, k_ref, v_ref, raw_ref = refs[14:20]
    logit_ref, beta_ref, gain_a, gain_b, small = refs[20:]
    mine, first = scal[0], scal[1] == 0
    part = own_w[0].shape[0]
    rows = tok_ref.shape[1]
    heads = beta_ref.shape[0]
    count = 4 * heads
    ats = [aligned((mine ^ k) * part, part) for k in range(4)]
    for k in range(4):
        lines = toks[k][rows : rows + 4, :].astype(f32)
        for r in range(count + 2):
            piece = lines[r // 4 : r // 4 + 1, (r % 4) * part : (r % 4 + 1) * part]
            small[r : r + 1, ats[k]] = piece
    gain_a[...] = small[count : count + 1, :]
    gain_b[...] = small[count + 1 : count + 2, :]
    for h in range(heads):
        beta_ref[h : h + 1, :] = small[pl.ds(mine * heads + h, 1), :]
    for b in range(4):
        tok_ref[mine ^ b] = toks[b][:rows, :]
        x = toks[b][:rows, :].astype(f32)
        factor = lax.rsqrt(jnp.mean(x * x, axis=-1, keepdims=True) + eps)
        normed[aligned((mine ^ b) * rows, rows), :] = (x * factor * gain_a[...]).astype(bf16)
    logit = dot_nt(beta_ref[...].astype(bf16), normed[...])
    for h in range(heads):
        logit_ref[h] = logit[h : h + 1]
    n_own = normed[:, ats[0]]
    sums = [dot_nn(n_own, w[:, ats[0]]) for w in own_w]
    left, right = jnp.concatenate(sums[:2], 1), jnp.concatenate(sums[2:], 1)
    a, b = jnp.where(first, left, right), jnp.where(first, right, left)
    for k in range(1, 4):
        n_k = normed[:, ats[k]]
        a = a + dot_nn(n_k, ours[k - 1][...])
        b = b + dot_nn(n_k, theirs[k - 1][...])
    qk, vp = jnp.where(first, a, b), jnp.where(first, b, a)
    q_ref[...] = qk[:, :part].astype(bf16)
    k_ref[...] = qk[:, part:].astype(bf16)
    v_ref[...] = vp[:, :part].astype(bf16)
    raw_ref[...] = vp[:, part:]


def live_rows(scal, rows):
    at = scal[0] * rows + lax.broadcasted_iota(jnp.int32, (rows, 1), 0)
    return jnp.where(at < scal[2], 1.0, 0.0)


def block_sum(ref):
    return (ref[0].astype(f32) + ref[1].astype(f32)) + (ref[2].astype(f32) + ref[3].astype(f32))


def middle_kernel(scal, tok, gain, come, stream_ref, normed_ref, square_ref):
    rows = stream_ref.shape[0]
    attn = live_rows(scal, rows) * block_sum(come)
    square_ref[...] = jnp.sum(attn * attn, axis=0, keepdims=True)
    stream = tok[...].astype(f32) + attn
    stream_ref[...] = stream
    factor = lax.rsqrt(jnp.mean(stream * stream, axis=-1, keepdims=True) + eps)
    normed = (stream * factor * gain[...]).astype(bf16)
    for k in range(4):
        normed_ref[k] = normed


def feed_kernel(scal, n_two, c0, c1, c2, c3, w_down, ours, theirs, *refs):
    hid_a, hid_b, dgu_a, dgu_b, d_feed = refs
    core = scal[1]
    rows = c0.shape[0]
    for k, piece in enumerate((c0, c1, c2, c3)):
        d_feed[aligned((scal[0] ^ k) * rows, rows), :] = piece[...]
    part = ours.shape[1]
    half = hid_a.shape[1]
    for which, ws, hid, dgu in ((core, ours, hid_a, dgu_a), (1 - core, theirs, hid_b, dgu_b)):
        gu = 0.0
        for k in range(4):
            gu = gu + dot_nn(n_two[:, k * part : (k + 1) * part], ws[k])
        gate, up = gu[:, :half], gu[:, half:]
        d_hid = dot_nt(d_feed[...], w_down[aligned(which * half, half), :])
        sig = jax.nn.sigmoid(gate)
        act = gate * sig
        hid[...] = (act * up).astype(bf16)
        dgu[:, :half] = (d_hid * up * sig * (1.0 + gate * (1.0 - sig))).astype(bf16)
        dgu[:, half:] = (d_hid * act).astype(bf16)


def feed_back_kernel(dgu_a, dgu_b, ours, theirs, out):
    d_n = dot_nt(dgu_a[...], ours[0]) + dot_nt(dgu_b[...], theirs[0])
    out[...] = d_n.astype(bf16)


def feed_back(dgu_a, dgu_b, ours, theirs):
    count, part, cols = ours.shape
    rows = dgu_a.shape[0]
    held = pl.BlockSpec((rows, cols), lambda k: (0, 0))
    block = pl.BlockSpec((1, part, cols), lambda k: (k, 0, 0))
    return pl.pallas_call(
        feed_back_kernel,
        grid=(count,),
        in_specs=[held, held, block, block],
        out_specs=pl.BlockSpec((rows, part), lambda k: (0, k)),
        out_shape=struct((rows, count * part), bf16),
        compiler_params=grant(),
        cost_estimate=cost(3),
        name="feed_back",
    )(dgu_a, dgu_b, ours, theirs)


def norm_two_kernel(scal, stream_ref, cot, gain, come, d_stream_ref, d_attn_ref, gain_ref):
    rows = stream_ref.shape[0]
    live = live_rows(scal, rows)
    d_n = block_sum(come)
    stream = stream_ref[...]
    factor = lax.rsqrt(jnp.mean(stream * stream, axis=-1, keepdims=True) + eps)
    scaled = d_n * gain[...]
    mean = jnp.mean(stream * scaled, axis=-1, keepdims=True)
    d_stream = cot[...].astype(f32) * live + factor * scaled - stream * (factor**3 * mean)
    d_stream_ref[...] = d_stream
    d_attn = (live * d_stream).astype(bf16)
    for k in range(4):
        d_attn_ref[k] = d_attn
    gain_ref[...] = jnp.sum(d_n * stream * factor, axis=0, keepdims=True)


def input_kernel(scal, tok, dq, dk, dv, dr, dl, beta, hid_a, hid_b, w_down, *refs):
    own_w, ours, theirs, (out, gain_ref) = refs[:4], refs[4:7], refs[7:10], refs[10:]
    mine, core = scal[0], scal[1]
    first = core == 0
    part = own_w[0].shape[0]
    rows = tok.shape[1]
    half = hid_a.shape[1]
    qk = jnp.concatenate([dq[...], dk[...]], 1)
    vp = jnp.concatenate([dv[...], dr[...]], 1)
    x, y = jnp.where(first, qk, vp), jnp.where(first, vp, qk)
    d_logit = jnp.concatenate([dl[h] for h in range(dl.shape[0])], 0).astype(bf16)
    factors = []
    for b in range(4):
        t = tok[b].astype(f32)
        factors.append(lax.rsqrt(jnp.mean(t * t, axis=-1, keepdims=True) + eps))
    for k in range(4):
        at = aligned((mine ^ k) * part, part)
        d_n = dot_tn(d_logit, beta[:, at].astype(bf16))
        if k == 0:
            for d, w in zip((dq, dk, dv, dr), own_w):
                d_n = d_n + dot_nt(d[...], w[:, at])
        else:
            d_n = d_n + dot_nt(x, ours[k - 1][...]) + dot_nt(y, theirs[k - 1][...])
        total = jnp.zeros((1, part), f32)
        for b in range(4):
            piece = d_n[b * rows : (b + 1) * rows]
            out[b, :rows, at] = piece.astype(bf16)
            piece = piece * tok[b, :, at].astype(f32) * factors[b]
            total = total + jnp.sum(piece, axis=0, keepdims=True)
        gain_ref[:, at] = total
        cols = slice(k * part, (k + 1) * part)
        feed = dot_nn(hid_a[...], w_down[aligned(core * half, half), cols])
        feed = feed + dot_nn(hid_b[...], w_down[aligned((1 - core) * half, half), cols])
        for b in range(4):
            out[b, rows:, cols] = feed[b * rows : (b + 1) * rows].astype(bf16)


def last_kernel(scal, tok, gain, come, d_stream, stream, grad_out, out, square_ref):
    rows = tok.shape[0]
    live = live_rows(scal, rows)
    x = tok[...].astype(f32)
    both = block_sum(come)
    d_n, feed = both[:rows], live * both[rows:]
    factor = lax.rsqrt(jnp.mean(x * x, axis=-1, keepdims=True) + eps)
    scaled = d_n * gain[...]
    mean = jnp.mean(x * scaled, axis=-1, keepdims=True)
    grad_out[...] = (d_stream[...] + factor * scaled - x * (factor**3 * mean)).astype(bf16)
    square_ref[...] = jnp.sum(feed * feed, axis=0, keepdims=True)
    out[...] = (live * stream[...] + feed).astype(bf16)


def head_grads_kernel(scal, *refs):
    ours, theirs, outs = refs[:3], refs[3:6], refs[6:]
    first = scal[1] == 0
    part, width = outs[0].shape
    for k in range(5):
        at = slice((k % 2) * part, (k % 2 + 1) * part)
        a, b = ours[k // 2][at, :], theirs[k // 2][at, :]
        low, high = jnp.where(first, a, b).astype(f32), jnp.where(first, b, a).astype(f32)
        if k == 0:
            outs[4][:, : width // 2] = low
            outs[4][:, width // 2 :] = high
        else:
            at = slice((k - 1) * part, k * part)
            outs[0][:, at] = low[:, :part]
            outs[1][:, at] = low[:, part:]
            outs[2][:, at] = high[:, :part]
            outs[3][:, at] = high[:, part:]


def ff_grads_kernel(scal, ours, low, high, gate, up):
    first = scal[1] == 0
    half = ours.shape[2] // 2
    a, b = ours[0], jnp.where(pl.program_id(0) < 2, low[0], high[0])
    for i, v in enumerate((jnp.where(first, a, b), jnp.where(first, b, a))):
        at = slice(i * half, (i + 1) * half)
        gate[:, at] = v[:, :half].astype(f32)
        up[:, at] = v[:, half:].astype(f32)


def ff_grads(scal, ours, low, high):
    count, part, cols = ours.shape
    shape = (1, part, cols)
    out = pl.BlockSpec((part, cols), lambda k: (0, k))
    return pl.pallas_call(
        ff_grads_kernel,
        grid=(count,),
        in_specs=[
            pl.BlockSpec(memory_space=pltpu.SMEM),
            pl.BlockSpec(shape, lambda k: (k, 0, 0)),
            pl.BlockSpec(shape, lambda k: (jnp.minimum(k, 1), 0, 0)),
            pl.BlockSpec(shape, lambda k: (jnp.maximum(k - 2, 0), 0, 0)),
        ],
        out_specs=[out, out],
        out_shape=[struct((part, count * cols), f32)] * 2,
        compiler_params=grant(),
        cost_estimate=cost(4),
        name="ff_grads",
    )(scal, ours, low, high)


def product_kernel(a, b, c, out):
    out[...] = (dot_tn(a[...], b[...]) + c[...].astype(f32)).astype(bf16)


def product(name, left, right, add, start, size):
    step = 384
    rows, width = right.shape
    line = pl.BlockSpec((step, width), lambda i: (start // step + i, 0))
    return pl.pallas_call(
        product_kernel,
        grid=(size // step,),
        in_specs=[
            pl.BlockSpec((rows, step), lambda i: (0, start // step + i)),
            pl.BlockSpec((rows, width), lambda i: (0, 0)),
            line,
        ],
        out_specs=pl.BlockSpec((step, width), lambda i: (i, 0)),
        out_shape=struct((size, width), bf16),
        compiler_params=grant(),
        cost_estimate=cost(1),
        name=name,
    )(left, right, add)


def blocked(kernel, name, flag, *args):
    rows, width = args[0].shape
    step = max(s for s in (384, 256, 208, 200, 192, 128, 80) if rows % s == 0)
    spec = pl.BlockSpec((step, width), lambda i: (i, 0))
    return pl.pallas_call(
        kernel,
        grid=(rows // step,),
        in_specs=[pl.BlockSpec(memory_space=pltpu.SMEM)] + [spec] * len(args),
        out_specs=spec,
        out_shape=struct((rows, width), bf16),
        compiler_params=grant(),
        cost_estimate=cost(1),
        name=name,
    )(flag, *args)


def add_kernel(flag, a, b, out):
    out[...] = (a[...].astype(f32) + b[...].astype(f32)).astype(bf16)


def choose_kernel(flag, a, b, out):
    out[...] = jnp.where(flag[0] == 1, a[...], b[...])


def down_grads_kernel(scal, a0, a1, b0, b1, out):
    first = scal[1] == 0
    rows = a0.shape[0]
    for i, (a, b) in enumerate(((a0, b0), (a1, b1))):
        a, b = a[...], b[...]
        out[i * rows : (i + 1) * rows, :] = jnp.where(first, a, b).astype(f32)
        out[(i + 2) * rows : (i + 3) * rows, :] = jnp.where(first, b, a).astype(f32)


def out_kernel(scal, mixed, w_out, out):
    out[...] = dot_nn(mixed[...], w_out[...]).astype(bf16)

SHARDS = 4
CHIPS = 4


def shard_exchange(blocks):
    return lax.all_to_all(blocks, "shard", 0, 0)


def shard_gather(value):
    return shard_exchange(jnp.broadcast_to(value[None], (SHARDS,) + value.shape))


def shard_swap(value, k):
    return lax.ppermute(value, "shard", [(i, i ^ k) for i in range(SHARDS)])


def core_swap(value):
    return lax.ppermute(value, "rep", [(i, i ^ 1) for i in range(2 * CHIPS)])


def chip_send(value, pairs):
    return lax.ppermute(value, "rep", [(2 * a + c, 2 * b + c) for a, b in pairs for c in (0, 1)])


def take_rows(value, at, size):
    return lax.dynamic_slice_in_dim(value, at, size, axis=0)


def after(value, *others):
    return lax.optimization_barrier((value,) + others)[0]


def product_low(left, right, add=None):
    total = dot_tn(left, right)
    return (total if add is None else total + add.astype(f32)).astype(bf16)


class ChipSum:
    def __init__(self, hub):
        self.hub = hub.astype(jnp.int32).reshape(1)
        self.own, self.come, self.pair, self.other, self.total, self.back, self.out = (
            {} for _ in range(7)
        )

    def send(self, name, value, *deps):
        self.own[name] = value
        self.come[name] = chip_send(after(value, *deps) if deps else value, [(0, 1), (3, 2)])

    def cross(self, name, *deps):
        come = after(self.come[name], *deps) if deps else self.come[name]
        self.pair[name] = blocked(add_kernel, "pair", self.hub, self.own[name], come)
        self.other[name] = chip_send(self.pair[name], [(1, 2), (2, 1)])
        return self.pair[name]

    def give(self, name, *deps):
        other = after(self.other[name], *deps) if deps else self.other[name]
        self.total[name] = blocked(add_kernel, "total", self.hub, self.pair[name], other)
        self.back[name] = chip_send(self.total[name], [(1, 0), (2, 3)])
        return self.total[name]

    def result(self, name, *deps):
        back = after(self.back[name], *deps) if deps else self.back[name]
        self.out[name] = blocked(choose_kernel, "result", self.hub, self.total[name], back)
        return self.out[name]

    def play(self, events, tick):
        for what, name in events:
            tick = getattr(self, what)(name, tick)
        return tick


def sharded_layer(
    tokens,
    cotangent,
    lengths,
    gain_one,
    w_query,
    w_key,
    w_value,
    w_path,
    w_beta,
    w_out,
    gain_two,
    w_gate,
    w_up,
    w_down,
):
    rows, width = tokens.shape
    part = w_query.shape[0]
    head_count = w_beta.shape[1]
    heads = head_count // SHARDS
    ff_part = w_down.shape[0]
    ff_core = ff_part // 2
    seq = rows * SHARDS
    mine = lax.axis_index("shard")
    rep = lax.axis_index("rep")
    core = rep % 2
    chip = rep // 2
    first_core = core == 0
    length = lengths[0]
    scal = jnp.stack([mine, core, length]).astype(jnp.int32)
    live = (mine * rows + jnp.arange(rows) < length).astype(f32)[:, None]
    row_f = struct((rows, width), f32)
    blocks = struct((SHARDS, rows, width), bf16)
    half = width // 2
    line = struct((1, width), f32)
    wide = struct((seq, width), bf16)

    small = jnp.concatenate(
        [w_beta.T, gain_one[None], gain_two[None], jnp.zeros((2, part), bf16)], 0
    )
    extra = small.size // width
    pad = jnp.zeros((16 - extra, width), bf16)
    tok = jnp.concatenate([tokens, small.reshape(extra, width), pad], 0)
    toks = [tok] + [shard_swap(tok, k) for k in range(1, SHARDS)]
    own_w = (w_query, w_key, w_value, w_path)
    picked = whole(
        head_pick_kernel,
        "pick_heads",
        1,
        [struct((part, 2 * part), bf16)] * 3,
        scal,
        w_query,
        w_key,
        w_value,
        w_path,
    )
    heads_ours = [shard_swap(v, k) for k, v in enumerate(picked, 1)]
    heads_theirs = [core_swap(v) for v in heads_ours]

    low = struct((seq, part), bf16)
    tok, normed, queries, keyset, values, raw, logit, beta_rows, gain_a, gain_b = whole(
        project_kernel,
        "project",
        4,
        [
            blocks,
            wide,
            low,
            low,
            low,
            struct((seq, part), f32),
            struct((heads, 1, seq), f32),
            struct((heads, width), f32),
            line,
            line,
        ],
        scal,
        *toks,
        *own_w,
        *heads_ours,
        *heads_theirs,
        scratch=[pltpu.VMEM((16, width), f32)],
    )

    d_feed_own = (cotangent.astype(f32) * live).astype(bf16)
    d_feeds = [d_feed_own] + [
        shard_swap(after(d_feed_own, *toks[1:], *heads_ours), k) for k in range(1, SHARDS)
    ]
    (picked,) = whole(
        ff_pick_kernel,
        "pick_hidden",
        1,
        [struct((SHARDS, part, 2 * ff_core), bf16)],
        scal,
        w_gate,
        w_up,
    )
    ff_ours = shard_exchange(after(picked, *toks[1:], *heads_ours))
    mixed, inv, ctx, probs = attend_forward(
        scal, queries, keyset, values, raw, logit, heads
    )
    (attn_part,) = whole(
        out_kernel, "out_project", 1, [wide], scal, after(mixed, ff_ours), w_out
    )

    attn_come = shard_exchange(attn_part.reshape(SHARDS, rows, width))
    ff_theirs = core_swap(after(ff_ours, attn_part))
    stream, normed_two, attn_square = whole(
        middle_kernel,
        "residual_norm",
        1,
        [row_f, blocks, line],
        scal,
        tokens,
        gain_b,
        after(attn_come, *d_feeds[1:]),
    )
    n_two = shard_exchange(normed_two).reshape(seq, width)

    hid = struct((seq, ff_core), bf16)
    dgu = struct((seq, 2 * ff_core), bf16)
    ff_half = ff_core // 2
    hid_a, hid_b, dgu_a, dgu_b, d_feed = whole(
        feed_kernel,
        "feed",
        6,
        [hid, hid, dgu, dgu, wide],
        scal,
        n_two,
        *d_feeds,
        w_down,
        ff_ours,
        ff_theirs,
    )

    zsum = ChipSum((chip == 1) | (chip == 2))
    down_theirs = product_low(hid_b, d_feed)
    down_come = core_swap(down_theirs)
    ff_theirs_grad = product_low(n_two, after(dgu_b, down_theirs))
    ff_come = core_swap(ff_theirs_grad)
    d_n_part = feed_back(after(dgu_a, ff_theirs_grad), dgu_b, ff_ours, ff_theirs)
    tick = d_n_part
    for i in range(2):
        at = slice(i * (ff_core // 2), (i + 1) * (ff_core // 2))
        tick = product_low(after(hid_a, tick)[:, at], d_feed, down_come[at])
        zsum.send(f"down{i}", tick)
    for i in range(2):
        at = slice(i * 2 * part, (i + 1) * 2 * part)
        tick = product(f"ff{i}", n_two, after(dgu_a, tick), ff_come, i * 2 * part, 2 * part)
        zsum.send(f"ff{i}", tick)
    d_n_come = shard_exchange(after(d_n_part, tick).reshape(SHARDS, rows, width))

    d_stream, d_attn_own, part_gain_b = whole(
        norm_two_kernel,
        "norm_two_back",
        1,
        [row_f, blocks, line],
        scal,
        stream,
        cotangent,
        gain_b,
        d_n_come,
    )
    tick = zsum.play([("cross", "down0")], d_attn_own)
    d_attn = shard_exchange(after(d_attn_own, tick)).reshape(seq, width)

    d_mixed = dot_nt(d_attn, w_out).astype(bf16)
    d_query, d_key, d_value, d_raw, d_logit = attend_backward(
        scal, queries, keyset, values, raw, logit, inv, ctx, probs, d_mixed, heads
    )
    tick = zsum.play([("give", "down0"), ("cross", "down1"), ("cross", "ff0")], d_logit)

    qk = jnp.concatenate([d_query, d_key], 1)
    vp = jnp.concatenate([d_value, d_raw], 1)
    keep = after(jnp.where(first_core, vp, qk), tick)
    p_theirs = [product_low(normed[:, i * 2 * part : (i + 1) * 2 * part], keep) for i in range(2)]
    come = [core_swap(v) for v in p_theirs]
    g_out_theirs = product_low(
        mixed, lax.dynamic_slice_in_dim(after(d_attn, *p_theirs), (1 - core) * half, half, axis=1)
    )
    g_out_come = core_swap(g_out_theirs)
    tick = zsum.play([("give", "down1"), ("cross", "ff1")], g_out_theirs)
    keep = after(jnp.where(first_core, qk, vp), tick)
    grad = [
        product_low(normed[:, i * 2 * part : (i + 1) * 2 * part], keep, come[i]) for i in range(2)
    ]
    grad = jnp.concatenate(grad, 0)
    grad_home = shard_exchange(grad.reshape(SHARDS, part, 2 * part))
    last_part, part_gain_a = whole(
        input_kernel,
        "input_back",
        4,
        [struct((SHARDS, 2 * rows, width), bf16), line],
        scal,
        tok,
        d_query,
        d_key,
        d_value,
        d_raw,
        after(d_logit, grad),
        beta_rows,
        hid_a,
        hid_b,
        w_down,
        *own_w,
        *heads_ours,
        *heads_theirs,
    )
    g_out = product_low(
        mixed,
        lax.dynamic_slice_in_dim(after(d_attn, grad), core * half, half, axis=1),
        g_out_come,
    )
    tick = zsum.play([("result", "down0")], part_gain_a)
    grad_home = after(grad_home, tick)
    zsum.send("first", jnp.concatenate([g_out, grad_home[0]], 0))
    zsum.send("second", grad_home[1:3].reshape(2 * part, 2 * part))
    tick = zsum.play([("give", "ff0")], grad_home)
    last_come = shard_exchange(after(last_part, zsum.own["first"]))
    tick = zsum.play([("give", "ff1"), ("result", "down1"), ("cross", "first"), ("result", "ff0")], tick)
    input_grad, output, feed_square = whole(
        last_kernel,
        "last",
        1,
        [struct((rows, width), bf16), struct((rows, width), bf16), line],
        scal,
        tokens,
        gain_a,
        after(last_come, tick),
        d_stream,
        stream,
    )
    tick = zsum.play([("cross", "second"), ("give", "first"), ("result", "ff1")], feed_square)

    part_beta = dot_nn(d_logit[:, 0].astype(bf16), normed)
    pack = jnp.concatenate([part_beta, part_gain_a, part_gain_b], 0)
    pack = pack.reshape(heads + 2, SHARDS, part).transpose(1, 0, 2)
    own_tok = tokens.astype(f32)
    squares = jnp.stack(
        [
            jnp.sum(live * own_tok * own_tok),
            jnp.sum(attn_square),
            jnp.sum(feed_square),
            jnp.sum(live),
        ]
    )
    squares = jnp.concatenate([squares, jnp.zeros((part - 4,), f32)])
    pack = jnp.concatenate([pack, jnp.broadcast_to(squares, (SHARDS, 1, part))], 1)
    pack = shard_exchange(pack)
    pack = jnp.concatenate(
        [
            pack[:, :heads].reshape(head_count, part),
            jnp.sum(pack[:, heads:], axis=0),
            jnp.zeros((1, part), f32),
        ],
        0,
    )
    pack = pack + core_swap(pack)
    pack_hi = pack.astype(bf16)
    pack_lo = (pack - pack_hi.astype(f32)).astype(bf16)
    pack = jnp.concatenate([pack_hi, pack_lo], 1)
    zsum.send("third", jnp.concatenate([grad_home[SHARDS - 1], pack], 0))
    downs = [zsum.out["down0"], zsum.out["down1"]]
    others = [core_swap(v) for v in downs]
    (grad_down,) = whole(
        down_grads_kernel,
        "down_grads",
        2,
        [struct((ff_part, width), f32)],
        scal,
        after(downs[0], tick),
        downs[1],
        *others,
    )
    tick = zsum.play(
        [("cross", "third"), ("give", "second"), ("result", "first"), ("give", "third")], grad_down
    )
    ff_sum = jnp.concatenate([zsum.out["ff0"], zsum.out["ff1"]], 0)
    ff_sum = shard_exchange(ff_sum.reshape(SHARDS, part, 2 * ff_core))
    ff_sum = after(ff_sum, tick)
    ff_other = [core_swap(ff_sum[:2]), core_swap(ff_sum[2:])]
    tick = zsum.play([("result", "second")], ff_sum)
    grad_gate, grad_up = ff_grads(scal, after(ff_sum, tick), *ff_other)
    tick = zsum.play([("result", "third")], grad_gate)
    last = zsum.out["third"]
    pack = last[part:, :part].astype(f32) + last[part:, part:].astype(f32)
    grad_beta = pack[:head_count].T
    grad_gain_a, grad_gain_b = pack[head_count], pack[head_count + 1]
    sq_input, sq_attn, sq_feed, live_total = (pack[head_count + 2, i] for i in range(4))
    denom = live_total * width

    ours = (zsum.out["first"], zsum.out["second"], last)
    theirs = [core_swap(v) for v in (zsum.out["first"], zsum.out["second"], last[:part])]
    head_grad = struct((part, width), f32)
    grad_query, grad_key, grad_value, grad_path, grad_out = whole(
        head_grads_kernel, "head_grads", 3, [head_grad] * 5, scal, *ours, *theirs
    )
    return (
        output,
        input_grad,
        grad_gain_a,
        grad_query,
        grad_key,
        grad_value,
        grad_path,
        grad_beta,
        grad_out,
        grad_gain_b,
        grad_gate,
        grad_up,
        grad_down,
        jnp.sqrt(sq_input / denom),
        jnp.sqrt(sq_attn / denom),
        jnp.sqrt(sq_feed / denom),
    )


def pick(mesh):
    def layer(*args):
        head_count, ff_part = args[8].shape[1], args[13].shape[0]
        fits = mesh.shape["shard"] == SHARDS and mesh.shape["rep"] == 2 * CHIPS
        fits = fits and head_count % SHARDS == 0 and ff_part % 256 == 0
        fits = fits and args[4].shape[1] == 128 * head_count and args[0].shape[0] == 128
        return (sharded_layer if fits else gathered_layer)(*args)

    return layer


def solution(mesh):
    return jax.shard_map(
        pick(mesh),
        mesh=mesh,
        in_specs=(
            P(("rep", "shard"), None),
            P(("rep", "shard"), None),
            P("rep"),
            P("shard"),
            P("shard", None),
            P("shard", None),
            P("shard", None),
            P("shard", None),
            P("shard", None),
            P("shard", None),
            P("shard"),
            P("shard", None),
            P("shard", None),
            P("shard", None),
        ),
        out_specs=(
            P(("rep", "shard"), None),
            P(("rep", "shard"), None),
            P("shard"),
            P("shard", None),
            P("shard", None),
            P("shard", None),
            P("shard", None),
            P("shard", None),
            P("shard", None),
            P("shard"),
            P("shard", None),
            P("shard", None),
            P("shard", None),
            P(),
            P(),
            P(),
        ),
        check_vma=False,
    )
```

```python
import functools

import jax
import jax.numpy as jnp
from jax import lax
from jax.experimental import pallas as pl
from jax.experimental.pallas import tpu as pltpu
from jax.sharding import PartitionSpec as P

f32 = jnp.float32
bf16 = jnp.bfloat16

eps = 1e-06
highest = lax.Precision.HIGHEST


def rms_norm(value, gain_vec):
    factor = lax.rsqrt(jnp.mean(value * value, axis=-1, keepdims=True) + eps)
    return value * factor * gain_vec


def unit_rows(raw):
    return raw * lax.rsqrt(jnp.sum(raw * raw, axis=-1, keepdims=True) + eps)


def rounded(value):
    return lax.optimization_barrier(value.astype(jnp.bfloat16)).astype(jnp.float32)


def round_pass(value):
    return value + lax.stop_gradient(rounded(value) - value)


def split_heads(matrix, head_count):
    return matrix.reshape(matrix.shape[0], head_count, -1).transpose(1, 0, 2)


def join_heads(matrix):
    return matrix.transpose(1, 0, 2).reshape(matrix.shape[1], -1)


def mul_low(left, right):
    return jnp.dot(left, right, preferred_element_type=jnp.float32)


def back_mul(grad_rows, weight):
    return jnp.einsum("tg,fg->tf", grad_rows, weight, preferred_element_type=jnp.float32)


def weight_grad(left, right):
    return jnp.einsum("tf,tg->fg", left, right, preferred_element_type=jnp.float32)


def masks(block_len):
    row_ids = jnp.arange(block_len)[:, None]
    col_ids = jnp.arange(block_len)[None, :]
    return (col_ids < row_ids, col_ids <= row_ids)


def block_system(direction, beta_rate):
    block_len = direction.shape[1]
    strictly, up_to = masks(block_len)
    gram = jnp.einsum("htd,hsd->hts", direction, direction, precision=highest)
    return jnp.eye(block_len, dtype=jnp.float32)[None] + jnp.where(
        strictly[None], gram * beta_rate[:, None, :], 0.0
    )


def own_context(keyset, values, direction, beta_rate):
    system = block_system(direction, beta_rate)
    strictly, up_to = masks(keyset.shape[1])
    coupled = jnp.where(
        strictly[None], jnp.einsum("htd,hjd->htj", direction, keyset, precision=highest), 0.0
    )
    solved = jax.scipy.linalg.solve_triangular(system, coupled, lower=True, unit_diagonal=True)
    scaled_dir = direction * beta_rate[:, :, None]
    key_end = keyset - jnp.einsum("htj,htd->hjd", solved, scaled_dir, precision=highest)
    through = jax.scipy.linalg.solve_triangular(system, direction, lower=True, unit_diagonal=True)
    block_map = jnp.eye(direction.shape[2], dtype=jnp.float32)[None] - jnp.einsum(
        "htm,htn->hmn", scaled_dir, through, precision=highest
    )
    return (join_heads(key_end), join_heads(values), block_map[None])


def attend(
    queries, keyset, values, direction, beta_rate, key_far, value_far, maps_far, my_block, length
):
    head_count, block_len, head_width = queries.shape
    blocks = maps_far.shape[0]
    score_scale = head_width ** (-0.5)
    strictly, up_to = masks(block_len)
    system = block_system(direction, beta_rate)
    coupled = jnp.where(
        strictly[None], jnp.einsum("htd,hjd->htj", direction, keyset, precision=highest), 0.0
    )
    solved = jax.scipy.linalg.solve_triangular(system, coupled, lower=True, unit_diagonal=True)
    crossing = (
        jnp.where(
            up_to[None], jnp.einsum("hid,htd->hit", queries, direction, precision=highest), 0.0
        )
        * beta_rate[:, None, :]
    )
    near_scores = (
        jnp.einsum("hid,hjd->hij", queries, keyset, precision=highest)
        - jnp.einsum("hit,htj->hij", crossing, solved, precision=highest)
    ) * score_scale
    back_solved = jax.scipy.linalg.solve_triangular(
        system, crossing.transpose(0, 2, 1), lower=True, trans=1, unit_diagonal=True
    )
    moved = queries - jnp.einsum("hti,htd->hid", back_solved, direction, precision=highest)

    def advance(carried, item_pair):
        block_map, index = item_pair
        updated = jnp.einsum("hid,hde->hie", carried, block_map, precision=highest)
        return (jnp.where(index < my_block, updated, carried), carried)

    unused, reached = lax.scan(advance, moved, (maps_far, jnp.arange(blocks)), reverse=True)
    far_keys = key_far.reshape(blocks, block_len, head_count, head_width)
    far_values = value_far.reshape(blocks, block_len, head_count, head_width)
    far_scores = jnp.einsum("ehid,ejhd->ehij", reached, far_keys, precision=highest) * score_scale
    positions = jnp.arange(block_len)
    near_ok = up_to[None] & ((my_block * block_len + positions)[None, None, :] < length)
    block_ids = jnp.arange(blocks)
    far_ok = (block_ids[:, None, None, None] < my_block) & (
        (block_ids[:, None] * block_len + positions[None, :])[:, None, None, :] < length
    )
    near_masked = jnp.where(near_ok, near_scores, -1e30)
    far_masked = jnp.where(far_ok, far_scores, -1e30)
    row_max = jnp.maximum(jnp.max(near_masked, axis=2), jnp.max(far_masked, axis=(0, 3)))[
        :, :, None
    ]
    row_total = jnp.sum(jnp.where(near_ok, jnp.exp(near_masked - row_max), 0.0), axis=2) + jnp.sum(
        jnp.where(far_ok, jnp.exp(far_masked - row_max[None]), 0.0), axis=(0, 3)
    )
    log_total = row_max + jnp.log(row_total)[:, :, None]
    near_probs = round_pass(jnp.where(near_ok, jnp.exp(near_masked - log_total), 0.0))
    far_probs = round_pass(jnp.where(far_ok, jnp.exp(far_masked - log_total[None]), 0.0))
    return jnp.einsum("hij,hjd->hid", near_probs, values, precision=highest) + jnp.einsum(
        "ehij,ejhd->hid", far_probs, far_values, precision=highest
    )


def gathered_layer(
    tokens,
    cotangent,
    lengths,
    gain_one,
    w_query,
    w_key,
    w_value,
    w_path,
    w_beta,
    w_out,
    gain_two,
    w_gate,
    w_up,
    w_down,
):
    gain_a, query_w, key_w, value_w, path_w, beta_w, out_w, gain_b, gate_w, up_w, down_w = (
        lax.all_gather(gain_one, "shard", axis=0, tiled=True),
        lax.all_gather(w_query, "shard", axis=0, tiled=True),
        lax.all_gather(w_key, "shard", axis=0, tiled=True),
        lax.all_gather(w_value, "shard", axis=0, tiled=True),
        lax.all_gather(w_path, "shard", axis=0, tiled=True),
        lax.all_gather(w_beta, "shard", axis=0, tiled=True),
        lax.all_gather(w_out, "shard", axis=0, tiled=True),
        lax.all_gather(gain_two, "shard", axis=0, tiled=True),
        lax.all_gather(w_gate, "shard", axis=0, tiled=True),
        lax.all_gather(w_up, "shard", axis=0, tiled=True),
        lax.all_gather(w_down, "shard", axis=0, tiled=True),
    )
    block_len = tokens.shape[0]
    width = tokens.shape[1]
    head_count = beta_w.shape[1]
    my_block = lax.axis_index("shard")
    length = lengths[0]
    live_mask = (my_block * block_len + jnp.arange(block_len) < length).astype(jnp.float32)[:, None]
    stream_in = tokens.astype(jnp.float32)
    normed_f, norm_pull = jax.vjp(rms_norm, stream_in, gain_a.astype(jnp.float32))
    normed = normed_f.astype(jnp.bfloat16)
    queries = split_heads(rounded(mul_low(normed, query_w)), head_count)
    keyset = split_heads(rounded(mul_low(normed, key_w)), head_count)
    values_h = split_heads(rounded(mul_low(normed, value_w)), head_count)
    raw = mul_low(normed, path_w).reshape(block_len, head_count, -1)
    direction_f, unit_pull = jax.vjp(unit_rows, raw)
    direction = rounded(direction_f).transpose(1, 0, 2)
    beta_rate = 2.0 * jax.nn.sigmoid(mul_low(normed, beta_w))
    (key_end, value_own, map_own), context_pull = jax.vjp(
        own_context, keyset, values_h, direction, beta_rate.T
    )
    key_far, value_far, maps_far = (
        lax.all_gather(key_end.astype(jnp.bfloat16), "shard", axis=0, tiled=True).astype(
            key_end.dtype
        ),
        lax.all_gather(value_own.astype(jnp.bfloat16), "shard", axis=0, tiled=True).astype(
            value_own.dtype
        ),
        lax.all_gather(map_own.astype(jnp.bfloat16), "shard", axis=0, tiled=True).astype(
            map_own.dtype
        ),
    )

    def local_attend(
        queries, keyset, values_h, direction, beta_heads, key_far, value_far, maps_far
    ):
        return attend(
            queries,
            keyset,
            values_h,
            direction,
            beta_heads,
            key_far,
            value_far,
            maps_far,
            my_block,
            length,
        )

    heads_out, attend_pull = jax.vjp(
        local_attend,
        queries,
        keyset,
        values_h,
        direction,
        beta_rate.T,
        key_far,
        value_far,
        maps_far,
    )
    mixed = join_heads(heads_out).astype(jnp.bfloat16)
    attn_out = mul_low(mixed, out_w)
    stream = stream_in + live_mask * attn_out
    normed_two_f, norm_two_pull = jax.vjp(rms_norm, stream, gain_b.astype(jnp.float32))
    normed_two = normed_two_f.astype(jnp.bfloat16)
    gate_pre = mul_low(normed_two, gate_w)
    up_pre = mul_low(normed_two, up_w)
    gate_sig = jax.nn.sigmoid(gate_pre)
    hidden = (gate_pre * gate_sig * up_pre).astype(jnp.bfloat16)
    feed_out = mul_low(hidden, down_w)
    output = (live_mask * (stream + feed_out)).astype(jnp.bfloat16)
    cot_rows = cotangent.astype(jnp.float32) * live_mask
    d_feed = cot_rows.astype(jnp.bfloat16)
    d_hidden = back_mul(d_feed, down_w)
    d_gate = (d_hidden * up_pre * gate_sig * (1.0 + gate_pre * (1.0 - gate_sig))).astype(
        jnp.bfloat16
    )
    d_up = (d_hidden * gate_pre * gate_sig).astype(jnp.bfloat16)
    d_normed_two = back_mul(d_gate, gate_w) + back_mul(d_up, up_w)
    d_stream_norm, grad_gain_b = norm_two_pull(d_normed_two)
    d_stream = cot_rows + d_stream_norm
    d_attn = (live_mask * d_stream).astype(jnp.bfloat16)
    d_mixed = split_heads(rounded(back_mul(d_attn, out_w)), head_count)
    (
        d_queries,
        d_keys_near,
        d_values_near,
        d_dir_near,
        d_beta_near,
        d_key_far,
        d_value_far,
        d_maps_far,
    ) = attend_pull(d_mixed)
    d_key_end, d_value_own, d_map_own = (
        lax.psum_scatter(
            d_key_far.astype(jnp.bfloat16), "shard", scatter_dimension=0, tiled=True
        ).astype(jnp.float32),
        lax.psum_scatter(
            d_value_far.astype(jnp.bfloat16), "shard", scatter_dimension=0, tiled=True
        ).astype(jnp.float32),
        lax.psum_scatter(
            d_maps_far.astype(jnp.bfloat16), "shard", scatter_dimension=0, tiled=True
        ).astype(jnp.float32),
    )
    d_keys_ctx, d_values_ctx, d_dir_ctx, d_beta_ctx = context_pull(
        (d_key_end, d_value_own, d_map_own)
    )
    d_query_b = join_heads(d_queries).astype(jnp.bfloat16)
    d_key_b = join_heads(d_keys_near + d_keys_ctx).astype(jnp.bfloat16)
    d_value_b = join_heads(d_values_near + d_values_ctx).astype(jnp.bfloat16)
    (d_raw,) = unit_pull((d_dir_near + d_dir_ctx).transpose(1, 0, 2))
    d_raw_b = d_raw.reshape(block_len, -1).astype(jnp.bfloat16)
    d_beta_total = (d_beta_near + d_beta_ctx).T
    d_logit_b = (d_beta_total * beta_rate * (1.0 - 0.5 * beta_rate)).astype(jnp.bfloat16)
    d_normed = (
        back_mul(d_query_b, query_w)
        + back_mul(d_key_b, key_w)
        + back_mul(d_value_b, value_w)
        + back_mul(d_raw_b, path_w)
        + back_mul(d_logit_b, beta_w)
    )
    d_stream_in, grad_gain_a = norm_pull(d_normed)
    input_grad = (d_stream_in + d_stream).astype(jnp.bfloat16)
    g_query = weight_grad(normed, d_query_b)
    g_key = weight_grad(normed, d_key_b)
    g_value = weight_grad(normed, d_value_b)
    g_path = weight_grad(normed, d_raw_b)
    g_beta = weight_grad(normed, d_logit_b)
    g_out = weight_grad(mixed, d_attn)
    g_gate = weight_grad(normed_two, d_gate)
    g_up = weight_grad(normed_two, d_up)
    g_down = weight_grad(hidden, d_feed)
    part_sums = (
        lax.psum_scatter(
            grad_gain_a.astype(jnp.bfloat16), "shard", scatter_dimension=0, tiled=True
        ).astype(jnp.float32),
        lax.psum_scatter(
            g_query.astype(jnp.bfloat16), "shard", scatter_dimension=0, tiled=True
        ).astype(jnp.float32),
        lax.psum_scatter(
            g_key.astype(jnp.bfloat16), "shard", scatter_dimension=0, tiled=True
        ).astype(jnp.float32),
        lax.psum_scatter(
            g_value.astype(jnp.bfloat16), "shard", scatter_dimension=0, tiled=True
        ).astype(jnp.float32),
        lax.psum_scatter(
            g_path.astype(jnp.bfloat16), "shard", scatter_dimension=0, tiled=True
        ).astype(jnp.float32),
        lax.psum_scatter(
            g_beta.astype(jnp.bfloat16), "shard", scatter_dimension=0, tiled=True
        ).astype(jnp.float32),
        lax.psum_scatter(
            g_out.astype(jnp.bfloat16), "shard", scatter_dimension=0, tiled=True
        ).astype(jnp.float32),
        lax.psum_scatter(
            grad_gain_b.astype(jnp.bfloat16), "shard", scatter_dimension=0, tiled=True
        ).astype(jnp.float32),
        lax.psum_scatter(
            g_gate.astype(jnp.bfloat16), "shard", scatter_dimension=0, tiled=True
        ).astype(jnp.float32),
        lax.psum_scatter(
            g_up.astype(jnp.bfloat16), "shard", scatter_dimension=0, tiled=True
        ).astype(jnp.float32),
        lax.psum_scatter(
            g_down.astype(jnp.bfloat16), "shard", scatter_dimension=0, tiled=True
        ).astype(jnp.float32),
    )
    owned = (
        lax.psum(part_sums[0].astype(jnp.bfloat16), "rep").astype(jnp.float32),
        lax.psum(part_sums[1].astype(jnp.bfloat16), "rep").astype(jnp.float32),
        lax.psum(part_sums[2].astype(jnp.bfloat16), "rep").astype(jnp.float32),
        lax.psum(part_sums[3].astype(jnp.bfloat16), "rep").astype(jnp.float32),
        lax.psum(part_sums[4].astype(jnp.bfloat16), "rep").astype(jnp.float32),
        lax.psum(part_sums[5].astype(jnp.bfloat16), "rep").astype(jnp.float32),
        lax.psum(part_sums[6].astype(jnp.bfloat16), "rep").astype(jnp.float32),
        lax.psum(part_sums[7].astype(jnp.bfloat16), "rep").astype(jnp.float32),
        lax.psum(part_sums[8].astype(jnp.bfloat16), "rep").astype(jnp.float32),
        lax.psum(part_sums[9].astype(jnp.bfloat16), "rep").astype(jnp.float32),
        lax.psum(part_sums[10].astype(jnp.bfloat16), "rep").astype(jnp.float32),
    )
    sq_input, sq_attn, sq_feed, live_total = lax.psum(
        (
            jnp.sum(live_mask * stream_in * stream_in),
            jnp.sum(live_mask * attn_out * attn_out),
            jnp.sum(live_mask * feed_out * feed_out),
            jnp.sum(live_mask),
        ),
        ("rep", "shard"),
    )
    denom = live_total * width
    return (
        output,
        input_grad,
        owned[0],
        owned[1],
        owned[2],
        owned[3],
        owned[4],
        owned[5],
        owned[6],
        owned[7],
        owned[8],
        owned[9],
        owned[10],
        jnp.sqrt(sq_input / denom),
        jnp.sqrt(sq_attn / denom),
        jnp.sqrt(sq_feed / denom),
    )


def dot_nn(a, b):
    return lax.dot_general(a, b, (((1,), (0,)), ((), ())), preferred_element_type=f32)


def dot_nt(a, b):
    return lax.dot_general(a, b, (((1,), (1,)), ((), ())), preferred_element_type=f32)


def dot_tn(a, b):
    return lax.dot_general(a, b, (((0,), (0,)), ((), ())), preferred_element_type=f32)


def halves(a):
    hi = a.astype(bf16)
    return hi, (a - hi.astype(f32)).astype(bf16)


def mul3(dot, a, b):
    return dot(a[0], b[0]) + (dot(a[0], b[1]) + dot(a[1], b[0]))


def mul2(dot, a, b):
    return dot(a[0], b) + dot(a[1], b)


def iota2(n, ax):
    return lax.broadcasted_iota(jnp.int32, (n, n), ax)


def tri_inverse(system, blk):
    n = system.shape[0]
    r, c = iota2(blk, 0), iota2(blk, 1)
    eye = jnp.where(r == c, 1.0, 0.0)
    tiles = [system[i * blk : (i + 1) * blk, i * blk : (i + 1) * blk] for i in range(n // blk)]
    pairs = ((r >> 1) == (c >> 1)) & ((r & 1) == 1) & ((c & 1) == 0)
    invs = [eye - jnp.where(pairs, t, 0.0) for t in tiles]
    b = 2
    while b < blk:
        m = ((r // (2 * b)) == (c // (2 * b))) & (((r // b) & 1) == 1) & (((c // b) & 1) == 0)
        new = []
        for t, v in zip(tiles, invs):
            vs = halves(v)
            low = mul3(dot_nn, halves(jnp.where(m, t, 0.0)), vs)
            new.append(v - mul3(dot_nn, vs, halves(low)))
        invs = new
        b *= 2
    size = blk
    while size < n:
        new = []
        for i in range(0, len(invs), 2):
            a, d = invs[i], invs[i + 1]
            off = system[(i + 1) * size : (i + 2) * size, i * size : (i + 1) * size]
            low = mul3(dot_nn, halves(off), halves(a))
            new.append(join(a, -mul3(dot_nn, halves(d), halves(low)), d))
        invs = new
        size *= 2
    return invs[0]


def quads(a):
    h = a.shape[0] // 2
    return a[:h, :h], a[h:, :h], a[h:, h:]


def join(a11, a21, a22):
    upper = jnp.concatenate([a11, jnp.zeros_like(a11)], 1)
    return jnp.concatenate([upper, jnp.concatenate([a21, a22], 1)], 0)


def low_nn(a, b):
    a11, a21, a22 = zip(*[quads(v) for v in a])
    b11, b21, b22 = zip(*[quads(v) for v in b])
    return join(
        mul3(dot_nn, a11, b11),
        mul3(dot_nn, a21, b11) + mul3(dot_nn, a22, b21),
        mul3(dot_nn, a22, b22),
    )


def low_nt(a, b):
    a11, a21, a22 = zip(*[quads(v) for v in a])
    b11, b21, b22 = zip(*[quads(v) for v in b])
    return join(
        mul3(dot_nt, a11, b11),
        mul3(dot_nt, a21, b11),
        mul3(dot_nt, a21, b21) + mul3(dot_nt, a22, b22),
    )


def low_tn(a, b):
    a11, a21, a22 = zip(*[quads(v) for v in a])
    b11, b21, b22 = zip(*[quads(v) for v in b])
    return join(
        mul3(dot_tn, a11, b11) + mul3(dot_tn, a21, b21),
        mul3(dot_tn, a22, b21),
        mul3(dot_tn, a22, b22),
    )


def aligned(at, size):
    return pl.ds(pl.multiple_of(at, 128), size)


def unit_factor(raw):
    return lax.rsqrt(jnp.sum(raw * raw, axis=-1, keepdims=True) + eps)


def forward_kernel(scal, q_ref, k_ref, v_ref, w_ref, b_ref, mixed_ref, inv_ref, ctx_ref, p_ref):
    length = scal[2]
    q, k, v, raw = q_ref[...], k_ref[...], v_ref[...], w_ref[...]
    w = (raw * unit_factor(raw)).astype(bf16)
    beta = 2.0 * jax.nn.sigmoid(b_ref[0])
    n = q.shape[0]
    r, c = iota2(n, 0), iota2(n, 1)
    strict, upto = c < r, c <= r
    inv = halves(tri_inverse(jnp.where(strict, dot_nt(w, w) * beta, 0.0), 128))
    ctx = halves(low_nn(inv, halves(jnp.where(strict, dot_nt(w, k), 0.0))))
    cross = jnp.where(upto, dot_nt(q, w) * beta, 0.0)
    scores = (dot_nt(q, k) - low_nn(halves(cross), ctx)) * (q.shape[1] ** -0.5)
    allowed = upto & (c < length)
    masked = jnp.where(allowed, scores, -1e30)
    top = jnp.max(masked, axis=1, keepdims=True)
    e = jnp.where(allowed, jnp.exp(masked - top), 0.0)
    log_total = top + jnp.log(jnp.sum(e, axis=1, keepdims=True))
    p = jnp.where(allowed, jnp.exp(masked - log_total), 0.0)
    mixed_ref[...] = dot_nn(p.astype(bf16), v).astype(bf16)
    for i in range(2):
        inv_ref[0, i] = inv[i]
        ctx_ref[0, i] = ctx[i]
    p_ref[0] = p


def backward_kernel(scal, *refs):
    q_ref, k_ref, v_ref, w_ref, b_ref, inv_ref, ctx_ref, p_ref, dm_ref = refs[:9]
    dq_ref, dk_ref, dv_ref, dr_ref, dl_ref = refs[9:]
    q, k, v, raw, dm = q_ref[...], k_ref[...], v_ref[...], w_ref[...], dm_ref[...]
    u = unit_factor(raw)
    w = (raw * u).astype(bf16)
    beta = 2.0 * jax.nn.sigmoid(b_ref[0])
    n = q.shape[0]
    r, c = iota2(n, 0), iota2(n, 1)
    strict, upto = c < r, c <= r
    inv = inv_ref[0, 0], inv_ref[0, 1]
    ctx = ctx_ref[0, 0], ctx_ref[0, 1]
    p = p_ref[0]
    d_v = dot_tn(p.astype(bf16), dm)
    dp = dot_nt(dm, v)
    g = p * (dp - jnp.sum(p * dp, axis=1, keepdims=True)) * (q.shape[1] ** -0.5)
    gs = halves(g)
    qw = dot_nt(q, w)
    cross = jnp.where(upto, qw * beta, 0.0)
    d_cross = jnp.where(upto, -low_nt(gs, ctx), 0.0)
    y = jnp.where(strict, -low_tn(inv, halves(low_tn(halves(cross), gs))), 0.0)
    ys = halves(y)
    d_sys = jnp.where(strict, -low_nt(ys, ctx), 0.0)
    d_beta = jnp.sum(d_cross * qw + d_sys * dot_nt(w, w), axis=0, keepdims=True)
    dx = halves(d_cross * beta)
    bm = halves(d_sys * beta)
    d_q = mul2(dot_nn, gs, k) + mul2(dot_nn, dx, w)
    d_k = mul2(dot_tn, gs, q) + mul2(dot_tn, ys, w)
    d_w = mul2(dot_tn, dx, q) + mul2(dot_nn, ys, k) + mul2(dot_nn, bm, w) + mul2(dot_tn, bm, w)
    d_raw = u * d_w - raw * (u * u * u) * jnp.sum(raw * d_w, axis=1, keepdims=True)
    for ref, val in ((dq_ref, d_q), (dk_ref, d_k), (dv_ref, d_v), (dr_ref, d_raw)):
        ref[...] = val.astype(bf16)
    dl_ref[0] = d_beta * beta * (1.0 - 0.5 * beta)


def grant():
    return pltpu.CompilerParams(vmem_limit_bytes=60 << 20)


def cost(micros):
    return pl.CostEstimate(flops=int(micros * 1e6), bytes_accessed=0, transcendentals=0)


def struct(shape, kind):
    return jax.ShapeDtypeStruct(shape, kind)


def head_specs(n, width):
    col = pl.BlockSpec((n, width), lambda h, s: (0, h))
    row = pl.BlockSpec((1, 1, n), lambda h, s: (h, 0, 0))
    pair = pl.BlockSpec((1, 2, n, n), lambda h, s: (h, 0, 0, 0))
    full = pl.BlockSpec((1, n, n), lambda h, s: (h, 0, 0))
    return col, row, pair, full


def attend_forward(scal, q, k, v, raw, logit, heads):
    n, width = q.shape[0], q.shape[1] // heads
    col, row, pair, full = head_specs(n, width)
    two = struct((heads, 2, n, n), bf16)
    return pl.pallas_call(
        forward_kernel,
        grid_spec=pltpu.PrefetchScalarGridSpec(
            num_scalar_prefetch=1,
            grid=(heads,),
            in_specs=[col] * 4 + [row],
            out_specs=[col, pair, pair, full],
        ),
        out_shape=[struct(q.shape, bf16), two, two, struct((heads, n, n), f32)],
        compiler_params=grant(),
        cost_estimate=cost(8),
        name="attend_forward",
    )(scal, q, k, v, raw, logit)


def attend_backward(scal, q, k, v, raw, logit, inv, ctx, p, dm, heads):
    n, width = q.shape[0], q.shape[1] // heads
    col, row, pair, full = head_specs(n, width)
    return pl.pallas_call(
        backward_kernel,
        grid_spec=pltpu.PrefetchScalarGridSpec(
            num_scalar_prefetch=1,
            grid=(heads,),
            in_specs=[col] * 4 + [row, pair, pair, full, col],
            out_specs=[col] * 4 + [row],
        ),
        out_shape=[struct(q.shape, bf16)] * 4 + [struct((heads, 1, n), f32)],
        compiler_params=grant(),
        cost_estimate=cost(4),
        name="attend_backward",
    )(scal, q, k, v, raw, logit, inv, ctx, p, dm)


def whole(kernel, name, micros, outs, scal, *args, scratch=()):
    vmem = pl.BlockSpec(memory_space=pltpu.VMEM)
    return pl.pallas_call(
        kernel,
        in_specs=[pl.BlockSpec(memory_space=pltpu.SMEM)] + [vmem] * len(args),
        out_specs=[vmem] * len(outs),
        out_shape=list(outs),
        scratch_shapes=list(scratch),
        compiler_params=grant(),
        cost_estimate=cost(micros),
        name=name,
    )(scal, *args)


def head_pick_kernel(scal, wq, wk, wv, wp, *outs):
    mine, first = scal[0], scal[1] == 0
    part = wq.shape[0]
    for k, out in enumerate(outs, 1):
        at = aligned((mine ^ k) * part, part)
        out[:, :part] = jnp.where(first, wq[:, at], wv[:, at])
        out[:, part:] = jnp.where(first, wk[:, at], wp[:, at])


def ff_pick_kernel(scal, wg, wu, out):
    half = out.shape[2] // 2
    for k in range(4):
        at = aligned((2 * k + scal[1]) * half, half)
        out[k, :, :half] = wg[:, at]
        out[k, :, half:] = wu[:, at]


def project_kernel(scal, *refs):
    toks, own_w, ours, theirs = refs[:4], refs[4:8], refs[8:11], refs[11:14]
    tok_ref, normed, q_ref, k_ref, v_ref, raw_ref = refs[14:20]
    logit_ref, beta_ref, gain_a, gain_b, small = refs[20:]
    mine, first = scal[0], scal[1] == 0
    part = own_w[0].shape[0]
    rows = tok_ref.shape[1]
    heads = beta_ref.shape[0]
    count = 4 * heads
    ats = [aligned((mine ^ k) * part, part) for k in range(4)]
    for k in range(4):
        lines = toks[k][rows : rows + 4, :].astype(f32)
        for r in range(count + 2):
            piece = lines[r // 4 : r // 4 + 1, (r % 4) * part : (r % 4 + 1) * part]
            small[r : r + 1, ats[k]] = piece
    gain_a[...] = small[count : count + 1, :]
    gain_b[...] = small[count + 1 : count + 2, :]
    for h in range(heads):
        beta_ref[h : h + 1, :] = small[pl.ds(mine * heads + h, 1), :]
    for b in range(4):
        tok_ref[mine ^ b] = toks[b][:rows, :]
        x = toks[b][:rows, :].astype(f32)
        factor = lax.rsqrt(jnp.mean(x * x, axis=-1, keepdims=True) + eps)
        normed[aligned((mine ^ b) * rows, rows), :] = (x * factor * gain_a[...]).astype(bf16)
    logit = dot_nt(beta_ref[...].astype(bf16), normed[...])
    for h in range(heads):
        logit_ref[h] = logit[h : h + 1]
    n_own = normed[:, ats[0]]
    sums = [dot_nn(n_own, w[:, ats[0]]) for w in own_w]
    left, right = jnp.concatenate(sums[:2], 1), jnp.concatenate(sums[2:], 1)
    a, b = jnp.where(first, left, right), jnp.where(first, right, left)
    for k in range(1, 4):
        n_k = normed[:, ats[k]]
        a = a + dot_nn(n_k, ours[k - 1][...])
        b = b + dot_nn(n_k, theirs[k - 1][...])
    qk, vp = jnp.where(first, a, b), jnp.where(first, b, a)
    q_ref[...] = qk[:, :part].astype(bf16)
    k_ref[...] = qk[:, part:].astype(bf16)
    v_ref[...] = vp[:, :part].astype(bf16)
    raw_ref[...] = vp[:, part:]


def live_rows(scal, rows):
    at = scal[0] * rows + lax.broadcasted_iota(jnp.int32, (rows, 1), 0)
    return jnp.where(at < scal[2], 1.0, 0.0)


def block_sum(ref):
    return (ref[0].astype(f32) + ref[1].astype(f32)) + (ref[2].astype(f32) + ref[3].astype(f32))


def middle_kernel(scal, tok, gain, come, stream_ref, normed_ref, square_ref):
    rows = stream_ref.shape[0]
    attn = live_rows(scal, rows) * block_sum(come)
    square_ref[...] = jnp.sum(attn * attn, axis=0, keepdims=True)
    stream = tok[...].astype(f32) + attn
    stream_ref[...] = stream
    factor = lax.rsqrt(jnp.mean(stream * stream, axis=-1, keepdims=True) + eps)
    normed = (stream * factor * gain[...]).astype(bf16)
    for k in range(4):
        normed_ref[k] = normed


def feed_kernel(scal, n_two, c0, c1, c2, c3, w_down, ours, theirs, *refs):
    hid_a, hid_b, dgu_a, dgu_b, d_feed = refs
    core = scal[1]
    rows = c0.shape[0]
    for k, piece in enumerate((c0, c1, c2, c3)):
        d_feed[aligned((scal[0] ^ k) * rows, rows), :] = piece[...]
    part = ours.shape[1]
    half = hid_a.shape[1]
    for which, ws, hid, dgu in ((core, ours, hid_a, dgu_a), (1 - core, theirs, hid_b, dgu_b)):
        gu = 0.0
        for k in range(4):
            gu = gu + dot_nn(n_two[:, k * part : (k + 1) * part], ws[k])
        gate, up = gu[:, :half], gu[:, half:]
        d_hid = dot_nt(d_feed[...], w_down[aligned(which * half, half), :])
        sig = jax.nn.sigmoid(gate)
        act = gate * sig
        hid[...] = (act * up).astype(bf16)
        dgu[:, :half] = (d_hid * up * sig * (1.0 + gate * (1.0 - sig))).astype(bf16)
        dgu[:, half:] = (d_hid * act).astype(bf16)


def feed_back_kernel(dgu_a, dgu_b, ours, theirs, out):
    d_n = dot_nt(dgu_a[...], ours[0]) + dot_nt(dgu_b[...], theirs[0])
    out[...] = d_n.astype(bf16)


def feed_back(dgu_a, dgu_b, ours, theirs):
    count, part, cols = ours.shape
    rows = dgu_a.shape[0]
    held = pl.BlockSpec((rows, cols), lambda k: (0, 0))
    block = pl.BlockSpec((1, part, cols), lambda k: (k, 0, 0))
    return pl.pallas_call(
        feed_back_kernel,
        grid=(count,),
        in_specs=[held, held, block, block],
        out_specs=pl.BlockSpec((rows, part), lambda k: (0, k)),
        out_shape=struct((rows, count * part), bf16),
        compiler_params=grant(),
        cost_estimate=cost(3),
        name="feed_back",
    )(dgu_a, dgu_b, ours, theirs)


def norm_two_kernel(scal, stream_ref, cot, gain, come, d_stream_ref, d_attn_ref, gain_ref):
    rows = stream_ref.shape[0]
    live = live_rows(scal, rows)
    d_n = block_sum(come)
    stream = stream_ref[...]
    factor = lax.rsqrt(jnp.mean(stream * stream, axis=-1, keepdims=True) + eps)
    scaled = d_n * gain[...]
    mean = jnp.mean(stream * scaled, axis=-1, keepdims=True)
    d_stream = cot[...].astype(f32) * live + factor * scaled - stream * (factor**3 * mean)
    d_stream_ref[...] = d_stream
    d_attn = (live * d_stream).astype(bf16)
    for k in range(4):
        d_attn_ref[k] = d_attn
    gain_ref[...] = jnp.sum(d_n * stream * factor, axis=0, keepdims=True)


def input_kernel(scal, tok, dq, dk, dv, dr, dl, beta, hid_a, hid_b, w_down, *refs):
    own_w, ours, theirs, (out, gain_ref) = refs[:4], refs[4:7], refs[7:10], refs[10:]
    mine, core = scal[0], scal[1]
    first = core == 0
    part = own_w[0].shape[0]
    rows = tok.shape[1]
    half = hid_a.shape[1]
    qk = jnp.concatenate([dq[...], dk[...]], 1)
    vp = jnp.concatenate([dv[...], dr[...]], 1)
    x, y = jnp.where(first, qk, vp), jnp.where(first, vp, qk)
    d_logit = jnp.concatenate([dl[h] for h in range(dl.shape[0])], 0).astype(bf16)
    factors = []
    for b in range(4):
        t = tok[b].astype(f32)
        factors.append(lax.rsqrt(jnp.mean(t * t, axis=-1, keepdims=True) + eps))
    for k in range(4):
        at = aligned((mine ^ k) * part, part)
        d_n = dot_tn(d_logit, beta[:, at].astype(bf16))
        if k == 0:
            for d, w in zip((dq, dk, dv, dr), own_w):
                d_n = d_n + dot_nt(d[...], w[:, at])
        else:
            d_n = d_n + dot_nt(x, ours[k - 1][...]) + dot_nt(y, theirs[k - 1][...])
        total = jnp.zeros((1, part), f32)
        for b in range(4):
            piece = d_n[b * rows : (b + 1) * rows]
            out[b, :rows, at] = piece.astype(bf16)
            piece = piece * tok[b, :, at].astype(f32) * factors[b]
            total = total + jnp.sum(piece, axis=0, keepdims=True)
        gain_ref[:, at] = total
        cols = slice(k * part, (k + 1) * part)
        feed = dot_nn(hid_a[...], w_down[aligned(core * half, half), cols])
        feed = feed + dot_nn(hid_b[...], w_down[aligned((1 - core) * half, half), cols])
        for b in range(4):
            out[b, rows:, cols] = feed[b * rows : (b + 1) * rows].astype(bf16)


def last_kernel(scal, tok, gain, come, d_stream, stream, grad_out, out, square_ref):
    rows = tok.shape[0]
    live = live_rows(scal, rows)
    x = tok[...].astype(f32)
    both = block_sum(come)
    d_n, feed = both[:rows], live * both[rows:]
    factor = lax.rsqrt(jnp.mean(x * x, axis=-1, keepdims=True) + eps)
    scaled = d_n * gain[...]
    mean = jnp.mean(x * scaled, axis=-1, keepdims=True)
    grad_out[...] = (d_stream[...] + factor * scaled - x * (factor**3 * mean)).astype(bf16)
    square_ref[...] = jnp.sum(feed * feed, axis=0, keepdims=True)
    out[...] = (live * stream[...] + feed).astype(bf16)


def head_grads_kernel(scal, *refs):
    ours, theirs, outs = refs[:5], refs[5:10], refs[10:]
    first = scal[1] == 0
    part = ours[0].shape[1] // 2
    for k in range(5):
        a, b = ours[k][...], theirs[k][...]
        low, high = jnp.where(first, a, b).astype(f32), jnp.where(first, b, a).astype(f32)
        if k == 0:
            outs[4][:, : 2 * part] = low
            outs[4][:, 2 * part :] = high
        else:
            at = slice((k - 1) * part, k * part)
            outs[0][:, at] = low[:, :part]
            outs[1][:, at] = low[:, part:]
            outs[2][:, at] = high[:, :part]
            outs[3][:, at] = high[:, part:]


def head_grads(scal, ours, theirs, rows):
    cols = ours[0].shape[1]
    steps = rows // 128
    low = pl.BlockSpec((128, cols), lambda i: (i, 0))
    high = pl.BlockSpec((128, cols), lambda i: (steps + i, 0))
    out = pl.BlockSpec((128, 2 * cols), lambda i: (i, 0))

    def five(group):
        first, second, third = group
        return (first, first, second, second, third)

    return pl.pallas_call(
        head_grads_kernel,
        grid=(steps,),
        in_specs=[pl.BlockSpec(memory_space=pltpu.SMEM)] + [low, high, low, high, low] * 2,
        out_specs=[out] * 5,
        out_shape=[struct((rows, 2 * cols), f32)] * 5,
        compiler_params=grant(),
        cost_estimate=cost(3),
        name="head_grads",
    )(scal, *five(ours), *five(theirs))


def ff_grads_kernel(scal, ours, low, high, gate, up):
    first = scal[1] == 0
    half = ours.shape[2] // 2
    a, b = ours[0], jnp.where(pl.program_id(0) < 2, low[0], high[0])
    for i, v in enumerate((jnp.where(first, a, b), jnp.where(first, b, a))):
        at = slice(i * half, (i + 1) * half)
        gate[:, at] = v[:, :half].astype(f32)
        up[:, at] = v[:, half:].astype(f32)


def ff_grads(scal, ours, low, high):
    count, part, cols = ours.shape
    shape = (1, part, cols)
    out = pl.BlockSpec((part, cols), lambda k: (0, k))
    return pl.pallas_call(
        ff_grads_kernel,
        grid=(count,),
        in_specs=[
            pl.BlockSpec(memory_space=pltpu.SMEM),
            pl.BlockSpec(shape, lambda k: (k, 0, 0)),
            pl.BlockSpec(shape, lambda k: (jnp.minimum(k, 1), 0, 0)),
            pl.BlockSpec(shape, lambda k: (jnp.maximum(k - 2, 0), 0, 0)),
        ],
        out_specs=[out, out],
        out_shape=[struct((part, count * cols), f32)] * 2,
        compiler_params=grant(),
        cost_estimate=cost(4),
        name="ff_grads",
    )(scal, ours, low, high)


def product_kernel(a, b, c, out):
    out[...] = (dot_tn(a[...], b[...]) + c[...].astype(f32)).astype(bf16)


def product(name, left, right, add, start, size):
    step = 384
    rows, width = right.shape
    line = pl.BlockSpec((step, width), lambda i: (start // step + i, 0))
    return pl.pallas_call(
        product_kernel,
        grid=(size // step,),
        in_specs=[
            pl.BlockSpec((rows, step), lambda i: (0, start // step + i)),
            pl.BlockSpec((rows, width), lambda i: (0, 0)),
            line,
        ],
        out_specs=pl.BlockSpec((step, width), lambda i: (i, 0)),
        out_shape=struct((size, width), bf16),
        compiler_params=grant(),
        cost_estimate=cost(1),
        name=name,
    )(left, right, add)


def blocked(kernel, name, flag, *args):
    rows, width = args[0].shape
    step = max(s for s in (384, 256, 208, 200, 192, 128, 80) if rows % s == 0)
    spec = pl.BlockSpec((step, width), lambda i: (i, 0))
    return pl.pallas_call(
        kernel,
        grid=(rows // step,),
        in_specs=[pl.BlockSpec(memory_space=pltpu.SMEM)] + [spec] * len(args),
        out_specs=spec,
        out_shape=struct((rows, width), bf16),
        compiler_params=grant(),
        cost_estimate=cost(1),
        name=name,
    )(flag, *args)


def add_kernel(flag, a, b, out):
    out[...] = (a[...].astype(f32) + b[...].astype(f32)).astype(bf16)


def choose_kernel(flag, a, b, out):
    out[...] = jnp.where(flag[0] == 1, a[...], b[...])


def down_grads_kernel(scal, a0, a1, b0, b1, out):
    first = scal[1] == 0
    rows = a0.shape[0]
    for i, (a, b) in enumerate(((a0, b0), (a1, b1))):
        a, b = a[...], b[...]
        out[i * rows : (i + 1) * rows, :] = jnp.where(first, a, b).astype(f32)
        out[(i + 2) * rows : (i + 3) * rows, :] = jnp.where(first, b, a).astype(f32)


def out_kernel(scal, mixed, w_out, out):
    out[...] = dot_nn(mixed[...], w_out[...]).astype(bf16)

SHARDS = 4
CHIPS = 4


def shard_exchange(blocks):
    return lax.all_to_all(blocks, "shard", 0, 0)


def shard_gather(value):
    return shard_exchange(jnp.broadcast_to(value[None], (SHARDS,) + value.shape))


def shard_swap(value, k):
    return lax.ppermute(value, "shard", [(i, i ^ k) for i in range(SHARDS)])


def core_swap(value):
    return lax.ppermute(value, "rep", [(i, i ^ 1) for i in range(2 * CHIPS)])


def chip_send(value, pairs):
    return lax.ppermute(value, "rep", [(2 * a + c, 2 * b + c) for a, b in pairs for c in (0, 1)])


def take_rows(value, at, size):
    return lax.dynamic_slice_in_dim(value, at, size, axis=0)


def after(value, *others):
    return lax.optimization_barrier((value,) + others)[0]


def product_low(left, right, add=None):
    total = dot_tn(left, right)
    return (total if add is None else total + add.astype(f32)).astype(bf16)


class ChipSum:
    def __init__(self, hub):
        self.hub = hub.astype(jnp.int32).reshape(1)
        self.own, self.come, self.pair, self.other, self.total, self.back, self.out = (
            {} for _ in range(7)
        )

    def send(self, name, value, *deps):
        self.own[name] = value
        self.come[name] = chip_send(after(value, *deps) if deps else value, [(0, 1), (3, 2)])

    def cross(self, name, *deps):
        come = after(self.come[name], *deps) if deps else self.come[name]
        self.pair[name] = blocked(add_kernel, "pair", self.hub, self.own[name], come)
        self.other[name] = chip_send(self.pair[name], [(1, 2), (2, 1)])
        return self.pair[name]

    def give(self, name, *deps):
        other = after(self.other[name], *deps) if deps else self.other[name]
        self.total[name] = blocked(add_kernel, "total", self.hub, self.pair[name], other)
        self.back[name] = chip_send(self.total[name], [(1, 0), (2, 3)])
        return self.total[name]

    def result(self, name, *deps):
        back = after(self.back[name], *deps) if deps else self.back[name]
        self.out[name] = blocked(choose_kernel, "result", self.hub, self.total[name], back)
        return self.out[name]

    def play(self, events, tick):
        for what, name in events:
            tick = getattr(self, what)(name, tick)
        return tick


def sharded_layer(
    tokens,
    cotangent,
    lengths,
    gain_one,
    w_query,
    w_key,
    w_value,
    w_path,
    w_beta,
    w_out,
    gain_two,
    w_gate,
    w_up,
    w_down,
):
    rows, width = tokens.shape
    part = w_query.shape[0]
    head_count = w_beta.shape[1]
    heads = head_count // SHARDS
    ff_part = w_down.shape[0]
    ff_core = ff_part // 2
    seq = rows * SHARDS
    mine = lax.axis_index("shard")
    rep = lax.axis_index("rep")
    core = rep % 2
    chip = rep // 2
    first_core = core == 0
    length = lengths[0]
    scal = jnp.stack([mine, core, length]).astype(jnp.int32)
    live = (mine * rows + jnp.arange(rows) < length).astype(f32)[:, None]
    row_f = struct((rows, width), f32)
    blocks = struct((SHARDS, rows, width), bf16)
    half = width // 2
    line = struct((1, width), f32)
    wide = struct((seq, width), bf16)

    small = jnp.concatenate(
        [w_beta.T, gain_one[None], gain_two[None], jnp.zeros((2, part), bf16)], 0
    )
    extra = small.size // width
    pad = jnp.zeros((16 - extra, width), bf16)
    tok = jnp.concatenate([tokens, small.reshape(extra, width), pad], 0)
    toks = [tok] + [shard_swap(tok, k) for k in range(1, SHARDS)]
    own_w = (w_query, w_key, w_value, w_path)
    picked = whole(
        head_pick_kernel,
        "pick_heads",
        1,
        [struct((part, 2 * part), bf16)] * 3,
        scal,
        w_query,
        w_key,
        w_value,
        w_path,
    )
    heads_ours = [shard_swap(v, k) for k, v in enumerate(picked, 1)]
    heads_theirs = [core_swap(v) for v in heads_ours]

    low = struct((seq, part), bf16)
    tok, normed, queries, keyset, values, raw, logit, beta_rows, gain_a, gain_b = whole(
        project_kernel,
        "project",
        4,
        [
            blocks,
            wide,
            low,
            low,
            low,
            struct((seq, part), f32),
            struct((heads, 1, seq), f32),
            struct((heads, width), f32),
            line,
            line,
        ],
        scal,
        *toks,
        *own_w,
        *heads_ours,
        *heads_theirs,
        scratch=[pltpu.VMEM((16, width), f32)],
    )

    d_feed_own = (cotangent.astype(f32) * live).astype(bf16)
    d_feeds = [d_feed_own] + [
        shard_swap(after(d_feed_own, *toks[1:], *heads_ours), k) for k in range(1, SHARDS)
    ]
    (picked,) = whole(
        ff_pick_kernel,
        "pick_hidden",
        1,
        [struct((SHARDS, part, 2 * ff_core), bf16)],
        scal,
        w_gate,
        w_up,
    )
    ff_ours = shard_exchange(after(picked, *toks[1:], *heads_ours))
    mixed, inv, ctx, probs = attend_forward(
        scal, queries, keyset, values, raw, logit, heads
    )
    (attn_part,) = whole(
        out_kernel, "out_project", 1, [wide], scal, after(mixed, ff_ours), w_out
    )

    attn_come = shard_exchange(attn_part.reshape(SHARDS, rows, width))
    ff_theirs = core_swap(after(ff_ours, attn_part))
    stream, normed_two, attn_square = whole(
        middle_kernel,
        "residual_norm",
        1,
        [row_f, blocks, line],
        scal,
        tokens,
        gain_b,
        after(attn_come, *d_feeds[1:]),
    )
    n_two = shard_exchange(normed_two).reshape(seq, width)

    hid = struct((seq, ff_core), bf16)
    dgu = struct((seq, 2 * ff_core), bf16)
    ff_half = ff_core // 2
    hid_a, hid_b, dgu_a, dgu_b, d_feed = whole(
        feed_kernel,
        "feed",
        6,
        [hid, hid, dgu, dgu, wide],
        scal,
        n_two,
        *d_feeds,
        w_down,
        ff_ours,
        ff_theirs,
    )

    zsum = ChipSum((chip == 1) | (chip == 2))
    down_theirs = product_low(hid_b, d_feed)
    down_come = core_swap(down_theirs)
    ff_theirs_grad = product_low(n_two, after(dgu_b, down_theirs))
    ff_come = core_swap(ff_theirs_grad)
    d_n_part = feed_back(after(dgu_a, ff_theirs_grad), dgu_b, ff_ours, ff_theirs)
    tick = d_n_part
    for i in range(2):
        at = slice(i * (ff_core // 2), (i + 1) * (ff_core // 2))
        tick = product_low(after(hid_a, tick)[:, at], d_feed, down_come[at])
        zsum.send(f"down{i}", tick)
    for i in range(2):
        at = slice(i * 2 * part, (i + 1) * 2 * part)
        tick = product(f"ff{i}", n_two, after(dgu_a, tick), ff_come, i * 2 * part, 2 * part)
        zsum.send(f"ff{i}", tick)
    d_n_come = shard_exchange(after(d_n_part, tick).reshape(SHARDS, rows, width))

    d_stream, d_attn_own, part_gain_b = whole(
        norm_two_kernel,
        "norm_two_back",
        1,
        [row_f, blocks, line],
        scal,
        stream,
        cotangent,
        gain_b,
        d_n_come,
    )
    tick = zsum.play([("cross", "down0")], d_attn_own)
    d_attn = shard_exchange(after(d_attn_own, tick)).reshape(seq, width)

    d_mixed = dot_nt(d_attn, w_out).astype(bf16)
    d_query, d_key, d_value, d_raw, d_logit = attend_backward(
        scal, queries, keyset, values, raw, logit, inv, ctx, probs, d_mixed, heads
    )
    tick = zsum.play([("give", "down0"), ("cross", "down1"), ("cross", "ff0")], d_logit)

    qk = jnp.concatenate([d_query, d_key], 1)
    vp = jnp.concatenate([d_value, d_raw], 1)
    keep = after(jnp.where(first_core, vp, qk), tick)
    p_theirs = [product_low(normed[:, i * 2 * part : (i + 1) * 2 * part], keep) for i in range(2)]
    come = [core_swap(v) for v in p_theirs]
    g_out_theirs = product_low(
        mixed, lax.dynamic_slice_in_dim(after(d_attn, *p_theirs), (1 - core) * half, half, axis=1)
    )
    g_out_come = core_swap(g_out_theirs)
    tick = zsum.play([("give", "down1"), ("cross", "ff1")], g_out_theirs)
    keep = after(jnp.where(first_core, qk, vp), tick)
    grad = [
        product_low(normed[:, i * 2 * part : (i + 1) * 2 * part], keep, come[i]) for i in range(2)
    ]
    grad = jnp.concatenate(grad, 0)
    grad_home = shard_exchange(grad.reshape(SHARDS, part, 2 * part))
    last_part, part_gain_a = whole(
        input_kernel,
        "input_back",
        4,
        [struct((SHARDS, 2 * rows, width), bf16), line],
        scal,
        tok,
        d_query,
        d_key,
        d_value,
        d_raw,
        after(d_logit, grad),
        beta_rows,
        hid_a,
        hid_b,
        w_down,
        *own_w,
        *heads_ours,
        *heads_theirs,
    )
    g_out = product_low(
        mixed,
        lax.dynamic_slice_in_dim(after(d_attn, grad), core * half, half, axis=1),
        g_out_come,
    )
    tick = zsum.play([("result", "down0")], part_gain_a)
    grad_home = after(grad_home, tick)
    zsum.send("first", jnp.concatenate([g_out, grad_home[0]], 0))
    zsum.send("second", grad_home[1:3].reshape(2 * part, 2 * part))
    tick = zsum.play([("give", "ff0")], grad_home)
    last_come = shard_exchange(after(last_part, zsum.own["first"]))
    tick = zsum.play([("give", "ff1"), ("result", "down1"), ("cross", "first"), ("result", "ff0")], tick)
    input_grad, output, feed_square = whole(
        last_kernel,
        "last",
        1,
        [struct((rows, width), bf16), struct((rows, width), bf16), line],
        scal,
        tokens,
        gain_a,
        after(last_come, tick),
        d_stream,
        stream,
    )
    tick = zsum.play([("cross", "second"), ("give", "first"), ("result", "ff1")], feed_square)

    part_beta = dot_nn(d_logit[:, 0].astype(bf16), normed)
    pack = jnp.concatenate([part_beta, part_gain_a, part_gain_b], 0)
    pack = pack.reshape(heads + 2, SHARDS, part).transpose(1, 0, 2)
    own_tok = tokens.astype(f32)
    squares = jnp.stack(
        [
            jnp.sum(live * own_tok * own_tok),
            jnp.sum(attn_square),
            jnp.sum(feed_square),
            jnp.sum(live),
        ]
    )
    squares = jnp.concatenate([squares, jnp.zeros((part - 4,), f32)])
    pack = jnp.concatenate([pack, jnp.broadcast_to(squares, (SHARDS, 1, part))], 1)
    pack = shard_exchange(pack)
    pack = jnp.concatenate(
        [
            pack[:, :heads].reshape(head_count, part),
            jnp.sum(pack[:, heads:], axis=0),
            jnp.zeros((1, part), f32),
        ],
        0,
    )
    pack = pack + core_swap(pack)
    pack_hi = pack.astype(bf16)
    pack_lo = (pack - pack_hi.astype(f32)).astype(bf16)
    pack = jnp.concatenate([pack_hi, pack_lo], 1)
    zsum.send("third", jnp.concatenate([grad_home[SHARDS - 1], pack], 0))
    downs = [zsum.out["down0"], zsum.out["down1"]]
    others = [core_swap(v) for v in downs]
    (grad_down,) = whole(
        down_grads_kernel,
        "down_grads",
        2,
        [struct((ff_part, width), f32)],
        scal,
        after(downs[0], tick),
        downs[1],
        *others,
    )
    tick = zsum.play(
        [("cross", "third"), ("give", "second"), ("result", "first"), ("give", "third")], grad_down
    )
    ff_sum = jnp.concatenate([zsum.out["ff0"], zsum.out["ff1"]], 0)
    ff_sum = shard_exchange(ff_sum.reshape(SHARDS, part, 2 * ff_core))
    ff_sum = after(ff_sum, tick)
    ff_other = [core_swap(ff_sum[:2]), core_swap(ff_sum[2:])]
    tick = zsum.play([("result", "second")], ff_sum)
    grad_gate, grad_up = ff_grads(scal, after(ff_sum, tick), *ff_other)
    tick = zsum.play([("result", "third")], grad_gate)
    last = zsum.out["third"]
    pack = last[part:, :part].astype(f32) + last[part:, part:].astype(f32)
    grad_beta = pack[:head_count].T
    grad_gain_a, grad_gain_b = pack[head_count], pack[head_count + 1]
    sq_input, sq_attn, sq_feed, live_total = (pack[head_count + 2, i] for i in range(4))
    denom = live_total * width

    ours = (zsum.out["first"], zsum.out["second"], last)
    theirs = [core_swap(v) for v in (zsum.out["first"], zsum.out["second"], last[:part])]
    grad_query, grad_key, grad_value, grad_path, grad_out = head_grads(scal, ours, theirs, part)
    return (
        output,
        input_grad,
        grad_gain_a,
        grad_query,
        grad_key,
        grad_value,
        grad_path,
        grad_beta,
        grad_out,
        grad_gain_b,
        grad_gate,
        grad_up,
        grad_down,
        jnp.sqrt(sq_input / denom),
        jnp.sqrt(sq_attn / denom),
        jnp.sqrt(sq_feed / denom),
    )


def pick(mesh):
    def layer(*args):
        head_count, ff_part = args[8].shape[1], args[13].shape[0]
        fits = mesh.shape["shard"] == SHARDS and mesh.shape["rep"] == 2 * CHIPS
        fits = fits and head_count % SHARDS == 0 and ff_part % 256 == 0
        fits = fits and args[4].shape[1] == 128 * head_count and args[0].shape[0] == 128
        return (sharded_layer if fits else gathered_layer)(*args)

    return layer


def solution(mesh):
    return jax.shard_map(
        pick(mesh),
        mesh=mesh,
        in_specs=(
            P(("rep", "shard"), None),
            P(("rep", "shard"), None),
            P("rep"),
            P("shard"),
            P("shard", None),
            P("shard", None),
            P("shard", None),
            P("shard", None),
            P("shard", None),
            P("shard", None),
            P("shard"),
            P("shard", None),
            P("shard", None),
            P("shard", None),
        ),
        out_specs=(
            P(("rep", "shard"), None),
            P(("rep", "shard"), None),
            P("shard"),
            P("shard", None),
            P("shard", None),
            P("shard", None),
            P("shard", None),
            P("shard", None),
            P("shard", None),
            P("shard"),
            P("shard", None),
            P("shard", None),
            P("shard", None),
            P(),
            P(),
            P(),
        ),
        check_vma=False,
    )
```
